128 devices in a mesh: exp: 16 (over x, z), sky: 8 (over y, core).
Axes of the slice: x: 4, y: 4, z: 4, core: 2. Of those that a mesh axis runs over, the one named last changes fastest.
Arguments:
- image: float32 [16, 4096, 4096], P('exp', 'sky'), may hold values from -21 to 21
- variance: float32 [16, 4096, 4096], P('exp', 'sky'), may hold values from 0.25 to 4
- mask: int32 [16, 256, 256], P('exp', 'sky'), may hold values 0 or 1
- foot_start: int32 [16], replicated, may hold values from 0 to 64
- pair_owner: int32 [16, 16], replicated, may hold values from 0 to 1, as said below
Outputs:
- coadd: float32 [4096, 4096], P('sky', 'exp')
- offsets: float32 [16, 9], replicated
The draws below stay inside these ranges and needn't reach their ends.
Inputs may be any that keep to these rules, and one draw needn't show every extreme that they name: pair_owner is 0 or 1, zero on the diagonal, pair_owner[i, j] and pair_owner[j, i] are never both 1, and every exposure has at least one pair.
All inputs are finite; a program needn't handle non-finite values. No bound on the sum of `mask` on one device may be relied on, other than what follows from the above.
Results may differ from the reference program's by a relative error of at most 0.0003.
Values sent between devices are 32-bit elements; how exact they have to be, the bound alone decides.
A program may use at most 256 MiB of HBM per device.

```python
import math
import jax
import jax.numpy as jnp
from jax import lax

COLS = 4096
BIN = 16
RADIUS = 10
FOOT = 3072
NEXP = 16
ROWS = 4096


def draw_image(key, part):
    scales = jnp.array([[1.0, 0.6, 0.4], [0.6, 0.4, 0.3], [0.4, 0.3, 0.2]], jnp.float32)
    coef = jax.random.truncated_normal(jax.random.fold_in(key, 11), -3.0, 3.0, (NEXP, 3, 3), jnp.float32) * scales
    noise = jax.random.truncated_normal(jax.random.fold_in(key, 13), -4.0, 4.0, (NEXP, ROWS, COLS), jnp.float32)
    ycoord = (2.0 * jnp.arange(ROWS).astype(jnp.float32) + 1.0) / ROWS - 1.0
    xcoord = (2.0 * jnp.arange(COLS).astype(jnp.float32) + 1.0) / COLS - 1.0
    ty = [jnp.ones_like(ycoord), ycoord, 2.0 * ycoord * ycoord - 1.0]
    tx = [jnp.ones_like(xcoord), xcoord, 2.0 * xcoord * xcoord - 1.0]
    back = jnp.zeros((NEXP, ROWS, COLS), jnp.float32)
    for upper in range(3):
        for lower in range(3):
            back = back + coef[:, upper, lower][:, None, None] * ty[upper][None, :, None] * tx[lower][None, None, :]
    return back + noise


def draw_pair_owner(key, part):
    rank = jax.random.permutation(jax.random.fold_in(key, 21), NEXP)
    keep = jax.random.randint(jax.random.fold_in(key, 22), (NEXP, NEXP), 0, 4)
    keep = jnp.minimum(keep, keep.T)
    rank_i = rank[:, None]
    rank_j = rank[None, :]
    nearby = jnp.abs(rank_i - rank_j) == 1
    exists = (keep != 0) | nearby
    return jnp.where(exists & (rank_i > rank_j), 1, 0).astype(jnp.int32)


def with_ends(drawn, key, least, high):
    index_at = [jax.random.randint(jax.random.fold_in(key, axis), (), 0, length) for axis, length in enumerate(drawn.shape)]
    longest = drawn.shape.index(max(drawn.shape))
    beside = index_at[:longest] + [(index_at[longest] + 1) % drawn.shape[longest]] + index_at[longest + 1:]
    return drawn.at[tuple(index_at)].set(least).at[tuple(beside)].set(high)


def block_scale(rng, extent, cuts, least, high):
    def one(position, parts):
        heights = jax.random.uniform(jax.random.fold_in(jax.random.fold_in(rng, 6), position), (parts,), jnp.float32, least / len(cuts), high / len(cuts))
        return jnp.repeat(jnp.exp(heights), extent[position] // parts).reshape((-1,) + (1,) * (len(extent) - position - 1))

    gain = one(*cuts[0])
    for cut in cuts[1:]:
        gain = gain * one(*cut)
    return gain


def setup_inputs(seed: int = 0) -> dict:
    keys = jax.random.split(jax.random.key(seed), 6)
    image = draw_image(jax.random.fold_in(keys[5], 71), 0)
    variance = jnp.clip(jnp.exp(math.log(4.0) - 2.7725887 * jax.random.uniform(keys[1], (NEXP, ROWS, COLS), jnp.float32) ** block_scale(keys[1], (NEXP, ROWS, COLS), ((0, 16), (1, 8)), -0.2, 0.2)), 0.25, 4.0)
    mask = with_ends((jax.random.randint(keys[2], (NEXP, ROWS // BIN, COLS // BIN), 0, 8) < 7).astype(jnp.int32), jax.random.fold_in(keys[2], 1), 0, 1)
    foot_start = with_ends(jax.random.randint(keys[3], (NEXP,), 0, COLS // (4 * BIN) + 1), jax.random.fold_in(keys[3], 1), 0, (COLS // (4 * BIN) + 1) - 1).astype(jnp.int32)
    pair_owner = draw_pair_owner(jax.random.fold_in(keys[5], 71), 0)
    return dict(image=image, variance=variance, mask=mask, foot_start=foot_start, pair_owner=pair_owner)


HIGH = lax.Precision.HIGHEST
LAMBDA_REG = 0.25
PRIOR = 1.0

def chebyshev(coord):
    return jnp.stack([jnp.ones_like(coord), coord, 2.0 * coord * coord - 1.0])

def centers(count, start, total):
    return (2.0 * (jnp.arange(count) + start).astype(jnp.float32) + 1.0) / total - 1.0

def footprint(count, start, width):
    cells = jnp.arange(count)
    return ((cells >= start) & (cells < start + width)).astype(jnp.float32)

def bin_basis(rows, row_first, total_rows, cols):
    by = chebyshev(centers(rows, row_first, total_rows))
    bx = chebyshev(centers(cols, 0, cols))
    return (by[:, None, :, None] * bx[None, :, None, :]).reshape(9, rows, cols)

def pair_normals(own_image, own_weight, other_image, other_weight, basis):
    weight = own_weight * other_weight / (own_weight + other_weight + 1.0)
    diff = own_image - other_image
    weighted = weight[:, None] * basis[None]
    gram = jnp.einsum('nkpq,lpq->nkl', weighted, basis, precision=HIGH)
    rhs = jnp.einsum('nkpq,npq->nk', weighted, diff, precision=HIGH)
    return (gram, rhs)

def solve_pairs(gram, rhs, owner):
    eye = jnp.eye(9, dtype=jnp.float32)
    safe = jnp.where(owner[..., None, None] > 0, gram, eye)
    factor = jnp.linalg.cholesky(safe)
    half = jax.scipy.linalg.solve_triangular(factor, rhs[..., None], lower=True)
    fit = jax.scipy.linalg.solve_triangular(factor, half, lower=True, trans=1)[..., 0]
    return fit * owner[..., None]

def global_offsets(fits, owner):
    degree = jnp.sum(owner, 1) + jnp.sum(owner, 0) + LAMBDA_REG
    system = jnp.diag(degree) - owner - owner.T
    right = jnp.sum(fits, 1) - jnp.sum(fits, 0)
    factor = jnp.linalg.cholesky(system)
    half = jax.scipy.linalg.solve_triangular(factor, right, lower=True)
    return jax.scipy.linalg.solve_triangular(factor, half, lower=True, trans=1)

def gauss_taps():
    offs = jnp.arange(-RADIUS, RADIUS + 1).astype(jnp.float32)
    taps = jnp.exp(-offs * offs / 50.0)
    return taps / jnp.sum(taps)

def smooth_rows(padded, taps, rows):
    total = taps[0] * padded[0:rows]
    for shift in range(1, 2 * RADIUS + 1):
        total = total + taps[shift] * padded[shift:shift + rows]
    return total

def smooth_cols(field, taps):
    cols = field.shape[1]
    padded = jnp.pad(field, ((0, 0), (RADIUS, RADIUS)))
    total = taps[0] * padded[:, 0:cols]
    for shift in range(1, 2 * RADIUS + 1):
        total = total + taps[shift] * padded[:, shift:shift + cols]
    return total

def expand_blocks(blocks):
    rows_b, cols_b = blocks.shape
    return jnp.broadcast_to(blocks[:, None, :, None], (rows_b, BIN, cols_b, BIN)).reshape(rows_b * BIN, cols_b * BIN)

def reference(image, variance, mask, foot_start, pair_owner):
    bins_row = ROWS // BIN
    bins_col = COLS // BIN
    owner = pair_owner.astype(jnp.float32)

    def binned(items):
        frame, spread, blocks, start = items
        bin_image = frame.reshape(bins_row, BIN, bins_col, BIN).mean(axis=(1, 3))
        inside = footprint(bins_col, start, FOOT // BIN)
        inverse = (1.0 / spread).reshape(bins_row, BIN, bins_col, BIN).sum(axis=(1, 3))
        return (bin_image, inverse * blocks.astype(jnp.float32) * inside[None, :])
    bin_images, bin_weights = lax.map(binned, (image, variance, mask, foot_start))
    basis = bin_basis(bins_row, 0, bins_row, bins_col)

    def owner_normals(items):
        own_image, own_weight = items
        return pair_normals(own_image[None], own_weight[None], bin_images, bin_weights, basis)
    gram, rhs = lax.map(owner_normals, (bin_images, bin_weights))
    fits = solve_pairs(gram, rhs, owner)
    offsets = global_offsets(fits, owner)
    ty = chebyshev(centers(ROWS, 0, ROWS))
    tx = chebyshev(centers(COLS, 0, COLS))
    taps = gauss_taps()

    def accumulate(carry, items):
        numer, denom = carry
        frame, spread, blocks, start, coeffs = items
        background = jnp.dot(jnp.dot(ty.T, coeffs.reshape(3, 3), precision=HIGH), tx, precision=HIGH)
        inside = footprint(COLS, start * BIN, FOOT)
        corrected = (frame - background) * inside[None, :]
        padded = jnp.pad(corrected, ((RADIUS, RADIUS), (0, 0)))
        smoothed = smooth_cols(smooth_rows(padded, taps, ROWS), taps)
        weight = expand_blocks(blocks.astype(jnp.float32)) * inside[None, :] / spread
        return ((numer + weight * smoothed, denom + weight), None)
    zeros = jnp.zeros((ROWS, COLS), jnp.float32)
    (numer, denom), unused = lax.scan(accumulate, (zeros, zeros), (image, variance, mask, foot_start, offsets))
    coadd = numer / (PRIOR + denom)
    return (coadd, offsets)
```

```python
import functools

import jax
import jax.numpy as jnp
import numpy as np
from jax import lax
from jax.experimental import pallas as pl
from jax.experimental.pallas import tpu as pltpu
from jax.sharding import PartitionSpec as P

F32 = jnp.float32
BF16 = jnp.bfloat16
HIGH = lax.Precision.HIGHEST
MESH = pl.DeviceIdType.MESH
BIN = 16
RADIUS = 10
NEXP = 16
ROWS = 512
COLS = 4096
SKY = 8
BROWS = 32
BCOLS = 256
FOOT_BINS = 192
HALO = 16
LAMBDA_REG = 0.25
PRIOR = 1.0


def iota(shape, dim):
    return lax.broadcasted_iota(jnp.int32, shape, dim)


def center(index, total):
    return (2.0 * index.astype(F32) + 1.0) / total - 1.0


def cheb(order, t):
    if order == 0:
        return jnp.ones_like(t)
    if order == 1:
        return t
    return 2.0 * t * t - 1.0


def split(value):
    high = value.astype(BF16)
    return high, (value - high.astype(F32)).astype(BF16)


def weigh_kernel(foot_ref, image_ref, variance_ref, mask_ref, weight_ref, bins_ref, sums, ones):
    step = pl.program_id(0)
    rows = image_ref.shape[1]
    start = foot_ref[lax.axis_index("exp")]

    @pl.when(step == 0)
    def _():
        hit = (iota((2048, 128), 0) // BIN) == iota((2048, 128), 1)
        ones[...] = jnp.where(hit, 1.0, 0.0).astype(BF16)

    nb = rows // BIN
    blocks = mask_ref[0, pl.ds(pl.multiple_of((step // 2) * 8, 8), 8), :].astype(F32)
    odd = (step % 2) == 1
    blocks = jnp.where(odd, blocks[nb:], blocks[:nb])
    cell = iota((nb, BCOLS), 1)
    blocks = jnp.where((cell >= start) & (cell < start + FOOT_BINS), blocks, 0.0)
    eight = jnp.concatenate([blocks, blocks], 0)
    lane = iota((8, 128), 1) // BIN
    wsums, isums = [], []
    for m in range(16):
        tiles = []
        for t in (2 * m, 2 * m + 1):
            half = eight[:, 128 * (t // 16) : 128 * (t // 16) + 128]
            tiles.append(jnp.take_along_axis(half, lane + 8 * (t % 16), axis=1))
        wide = jnp.concatenate(tiles, 1)[:nb]
        wide = jnp.broadcast_to(wide[:, None, :], (nb, BIN, 256)).reshape(rows, 256)
        w = wide * (1.0 / variance_ref[0, :, 256 * m : 256 * m + 256])
        weight_ref[m] = w
        wsums.append(jnp.sum(w.reshape(nb, BIN, 256), axis=1))
        isums.append(jnp.sum(image_ref[0, :, 256 * m : 256 * m + 256].reshape(nb, BIN, 256), axis=1))
    wsum = jnp.concatenate(wsums, 1)
    isum = jnp.concatenate(isums, 1) * (1.0 / (BIN * BIN))
    zero = jnp.zeros((4, COLS), F32)
    for k in range(nb // 2):
        tile = jnp.concatenate([isum[2 * k : 2 * k + 2], wsum[2 * k : 2 * k + 2], zero], 0)
        sums[pl.ds(pl.multiple_of(8 * (step * (nb // 2) + k), 8), 8), :] = tile

    @pl.when(step == pl.num_programs(0) - 1)
    def _():
        for h in range(2):
            x = sums[:, 2048 * h : 2048 * h + 2048]
            high = x.astype(BF16)
            rest = x - high.astype(F32)
            mid = rest.astype(BF16)
            low = (rest - mid.astype(F32)).astype(BF16)
            got = jnp.dot(jnp.concatenate([high, mid, low], 0), ones[...], preferred_element_type=F32)
            got = got[:128] + got[128:256] + got[256:]
            bins_ref[:, :, 128 * h : 128 * h + 128] = got.reshape(16, 8, 128)


def weigh(image, variance, mask, foot_start):
    rows = 64
    return pl.pallas_call(
        weigh_kernel,
        grid=(ROWS // rows,),
        in_specs=[
            pl.BlockSpec(memory_space=pltpu.SMEM),
            pl.BlockSpec((1, rows, COLS), lambda i: (0, i, 0)),
            pl.BlockSpec((1, rows, COLS), lambda i: (0, i, 0)),
            pl.BlockSpec((1, BROWS, BCOLS), lambda i: (0, 0, 0)),
        ],
        out_specs=[
            pl.BlockSpec((16, rows, 256), lambda i: (0, i, 0)),
            pl.BlockSpec((16, 8, BCOLS), lambda i: (0, 0, 0)),
        ],
        out_shape=[
            jax.ShapeDtypeStruct((16, ROWS, 256), F32),
            jax.ShapeDtypeStruct((16, 8, BCOLS), F32),
        ],
        scratch_shapes=[pltpu.VMEM((128, COLS), F32), pltpu.VMEM((2048, 128), BF16)],
        compiler_params=pltpu.CompilerParams(vmem_limit_bytes=40 << 20),
        cost_estimate=pl.CostEstimate(flops=10**8, bytes_accessed=25 << 20, transcendentals=2 << 20),
        name="weigh",
    )(foot_start, image, variance, mask)


def taps_matrix(offset):
    total = np.sum(np.exp(-(np.arange(-RADIUS, RADIUS + 1) ** 2) / 50.0))
    exact = np.where(np.abs(offset) <= RADIUS, np.exp(-(offset**2) / 50.0) / total, 0.0)
    high = exact.astype(BF16)
    return jnp.asarray(high), jnp.asarray((exact - high.astype(np.float64)).astype(BF16))


def smooth_kernel(foot_ref, up_ref, down_ref, prev_ref, image_ref, next_ref, ch_ref, cl_ref, rh_ref, rl_ref,
                  smooth_ref, tx_ref, ty_ref, xh, xl):
    j = pl.program_id(0)
    band = lax.axis_index("sky")
    start = foot_ref[lax.axis_index("exp")] * BIN
    tall = ROWS + 2 * HALO

    def put(first, lane0, value):
        rows, width = value.shape
        col = 256 * j - 128 + lane0 + iota((1, width), 1)
        inside = (col >= start) & (col < start + FOOT_BINS * BIN)
        high, low = split(jnp.where(inside, value, 0.0))
        xh[first : first + rows, lane0 : lane0 + width] = high
        xl[first : first + rows, lane0 : lane0 + width] = low

    lo = pl.multiple_of(jnp.maximum(256 * j - 128, 0), 128)
    mid = pl.multiple_of(256 * j, 128)
    hi = pl.multiple_of(jnp.minimum(256 * j + 256, COLS - 128), 128)
    for first, ref in ((0, up_ref), (HALO + ROWS, down_ref)):
        put(first, 0, ref[:, pl.ds(lo, 128)])
        put(first, 128, ref[:, pl.ds(mid, 256)])
        put(first, 384, ref[:, pl.ds(hi, 128)])
    put(HALO, 0, prev_ref[0])
    put(HALO, 128, image_ref[0])
    put(HALO, 384, next_ref[0])
    xcol = center(256 * j - 128 + iota((16, 512), 1), COLS)
    order = iota((16, 512), 0)
    put(tall, 0, jnp.where(order == 0, 1.0, jnp.where(order == 1, xcol, 2.0 * xcol * xcol - 1.0)))

    def row_pass(value):
        high, low = split(value)
        parts = []
        for i in range(ROWS // 128):
            zh, zl = high[128 * i : 128 * i + 160], low[128 * i : 128 * i + 160]
            parts.append(
                jnp.dot(rh_ref[...], zh, preferred_element_type=F32)
                + jnp.dot(rl_ref[...], zh, preferred_element_type=F32)
                + jnp.dot(rh_ref[...], zl, preferred_element_type=F32)
            )
        return parts

    across = (
        jnp.dot(xh[...], ch_ref[...], preferred_element_type=F32)
        + jnp.dot(xl[...], ch_ref[...], preferred_element_type=F32)
        + jnp.dot(xh[...], cl_ref[...], preferred_element_type=F32)
    )
    tx_ref[...] = across[tall : tall + 8]
    for i, part in enumerate(row_pass(across[:tall])):
        smooth_ref[0, 128 * i : 128 * i + 128, :] = part

    @pl.when(j == 0)
    def _():
        row = band * ROWS - HALO + iota((tall, 128), 0)
        y = center(row, ROWS * SKY)
        known = (row >= 0) & (row < ROWS * SKY)
        for u in range(3):
            for i, part in enumerate(row_pass(jnp.where(known, cheb(u, y), 0.0))):
                ty_ref[u, 128 * i : 128 * i + 128, :] = part


def smooth(image, up, down, foot_start):
    k, n = np.arange(512)[:, None], np.arange(256)[None, :]
    ch, cl = taps_matrix(k - n - 128)
    k, n = np.arange(160)[None, :], np.arange(128)[:, None]
    rh, rl = taps_matrix(k - n - HALO)
    last = COLS // 128 - 1
    whole = lambda shape: pl.BlockSpec(shape, lambda j: (0, 0))
    return pl.pallas_call(
        smooth_kernel,
        grid=(16,),
        in_specs=[
            pl.BlockSpec(memory_space=pltpu.SMEM),
            whole((HALO, COLS)),
            whole((HALO, COLS)),
            pl.BlockSpec((1, ROWS, 128), lambda j: (0, 0, jnp.maximum(2 * j - 1, 0))),
            pl.BlockSpec((1, ROWS, 256), lambda j: (0, 0, j)),
            pl.BlockSpec((1, ROWS, 128), lambda j: (0, 0, jnp.minimum(2 * j + 2, last))),
            whole((512, 256)),
            whole((512, 256)),
            whole((128, 160)),
            whole((128, 160)),
        ],
        out_specs=[
            pl.BlockSpec((1, ROWS, 256), lambda j: (j, 0, 0)),
            pl.BlockSpec((8, 256), lambda j: (0, j)),
            pl.BlockSpec((3, ROWS, 128), lambda j: (0, 0, 0)),
        ],
        out_shape=[
            jax.ShapeDtypeStruct((16, ROWS, 256), F32),
            jax.ShapeDtypeStruct((8, COLS), F32),
            jax.ShapeDtypeStruct((3, ROWS, 128), F32),
        ],
        scratch_shapes=[pltpu.VMEM((ROWS + 2 * HALO + 16, 512), BF16)] * 2,
        compiler_params=pltpu.CompilerParams(vmem_limit_bytes=40 << 20),
        cost_estimate=pl.CostEstimate(flops=10**10, bytes_accessed=25 << 20, transcendentals=0),
        name="smooth",
    )(foot_start, up, down, image, image, image, ch, cl, rh, rl)


def add_into(dst, terms, blocks, rows):
    per = rows // 64

    def body(i, carry):
        b, r = i // per, pl.multiple_of((i % per) * 64, 64)
        total = terms[0](b, r)
        for term in terms[1:]:
            total = total + term(b, r)
        dst(b, r, total)
        return carry

    lax.fori_loop(0, blocks * per, body, 0)


class Scatter:
    def __init__(self, part, half, x, z, sky, bufs, sems, first_sem):
        self.part, self.half = part, half
        self.me = (x, z)
        self.sky = sky
        self.f1p, self.f1m, self.rp, self.rm, self.f2p, self.f2m, self.r2p, self.r2m = bufs
        self.send_sems, self.recv_sems = sems
        self.sem = first_sem
        self.row0 = 256 * half
        self.lead = half
        self.copies = {}

    def device(self, axis, shift):
        x, z = self.me
        if axis == 0:
            x = lax.rem(x + shift + 4, 4)
        else:
            z = lax.rem(z + shift + 4, 4)
        return (4 * x + z, self.sky)

    def group(self, ref, dist, r, rows):
        g = lax.rem(self.me[self.lead] + dist, 4)
        rows = pl.ds(self.row0 + r, rows)
        return ref.at[g, :, rows, :] if self.lead == 0 else ref.at[:, g, rows, :]

    def send(self, key, src, dst, axis, shift):
        n = self.sem
        self.sem += 1
        copy = pltpu.make_async_remote_copy(
            src_ref=src, dst_ref=dst, send_sem=self.send_sems.at[n], recv_sem=self.recv_sems.at[n],
            device_id=self.device(axis, shift), device_id_type=MESH,
        )
        copy.start()
        self.copies[key] = copy

    def start1(self, ref):
        self.send("1p", self.group(ref, 2, 0, 128), self.f1p, self.lead, 1)
        self.send("1m", self.group(ref, 2, 128, 128), self.f1m, self.lead, -1)

    def start2(self, ref):
        self.send("2p", self.group(ref, 1, 128, 128), self.rp.at[:, pl.ds(128, 128), :], self.lead, 1)
        self.send("2m", self.group(ref, 3, 0, 128), self.rm.at[:, pl.ds(0, 128), :], self.lead, -1)

    def load(self, dist, shift):
        g = lax.rem(self.me[self.lead] + dist, 4)

        def get(b, r):
            rows = pl.ds(self.row0 + shift + r, 64)
            return self.part[g, b, rows, :] if self.lead == 0 else self.part[b, g, rows, :]

        return get

    def start3(self):
        for key, buf, dist, shift, to in (("p", self.f1p, 1, 0, 1), ("m", self.f1m, 3, 128, -1)):
            self.copies["1" + key].wait_recv()

            def put(b, r, v, buf=buf):
                buf[b, pl.ds(r, 64), :] = v

            add_into(put, [lambda b, r, buf=buf: buf[b, pl.ds(r, 64), :], self.load(dist, shift)], 4, 128)
            land = self.rp if to == 1 else self.rm
            self.send("3" + key, buf, land.at[:, pl.ds(shift, 128), :], self.lead, to)

    def finish1(self):
        for key in ("2p", "2m", "3p", "3m"):
            self.copies[key].wait_recv()

        def put(b, r, v):
            self.rp[b, pl.ds(r, 64), :] = v

        add_into(
            put,
            [lambda b, r: self.rp[b, pl.ds(r, 64), :], lambda b, r: self.rm[b, pl.ds(r, 64), :], self.load(0, 0)],
            4, 256,
        )
        axis = 1 - self.lead
        at = lambda dist: lax.rem(self.me[axis] + dist, 4)
        top, low = pl.ds(0, 128), pl.ds(128, 128)
        self.send("4p", self.rp.at[at(2), top, :], self.f2p, axis, 1)
        self.send("4m", self.rp.at[at(2), low, :], self.f2m, axis, -1)
        self.send("5p", self.rp.at[at(1), low, :], self.r2p.at[low, :], axis, 1)
        self.send("5m", self.rp.at[at(3), top, :], self.r2m.at[top, :], axis, -1)

    def start6(self):
        axis = 1 - self.lead
        for key, buf, dist, shift, to in (("p", self.f2p, 1, 0, 1), ("m", self.f2m, 3, 128, -1)):
            self.copies["4" + key].wait_recv()
            g = lax.rem(self.me[axis] + dist, 4)

            def put(b, r, v, buf=buf):
                buf[pl.ds(r, 64), :] = v

            add_into(
                put,
                [lambda b, r, buf=buf: buf[pl.ds(r, 64), :],
                 lambda b, r, g=g, shift=shift: self.rp[g, pl.ds(shift + r, 64), :]],
                1, 128,
            )
            land = self.r2p if to == 1 else self.r2m
            self.send("6" + key, buf, land.at[pl.ds(shift, 128), :], axis, to)

    def finish2(self):
        for key in ("5p", "5m", "6p", "6m"):
            self.copies[key].wait_recv()

    def total(self, r):
        g = self.me[1 - self.lead]
        return self.rp[g, pl.ds(r, 64), :] + self.r2p[pl.ds(r, 64), :] + self.r2m[pl.ds(r, 64), :]

    def drain(self):
        for copy in self.copies.values():
            copy.wait_send()


def invert(system):
    lane, row = iota((NEXP, 128), 1), iota((NEXP, 128), 0)
    work = jnp.concatenate([system, jnp.zeros((NEXP, 112), F32)], 1)
    work = work + jnp.where(lane == row + NEXP, 1.0, 0.0)
    for j in range(NEXP):
        pivot_row = work[j : j + 1, :] / work[j : j + 1, j : j + 1]
        factor = work[:, j : j + 1]
        work = jnp.where(row == j, pivot_row, work - factor * pivot_row)
    return work[:, NEXP : 2 * NEXP]


def moments(bins, me, band):
    image = jnp.concatenate([bins[:, 0, :], bins[:, 1, :]], 1)
    weight = jnp.concatenate([bins[:, 2, :], bins[:, 3, :]], 1)
    ws, ds = [], []
    for d in range(1, 9):
        other = pltpu.roll(weight, NEXP - d, 0)
        w = weight * other / (weight + other + 1.0)
        ws.append(w)
        ds.append(w * (image - pltpu.roll(image, NEXP - d, 0)))
    w, wd = jnp.concatenate(ws, 0), jnp.concatenate(ds, 0)

    def basis(rows, base):
        k, lane = iota((rows, 512), 0), iota((rows, 512), 1)
        y = center(BROWS * band + 2 * me + lane // 256, BCOLS)
        x = center(lane % 256, BCOLS)

        def pick(order, t):
            t2 = 2.0 * t * t - 1.0
            out = jnp.where(order == 0, 1.0, jnp.where(order == 1, t, t2))
            if base == 5:
                out = jnp.where(order == 3, 2.0 * t * t2 - t, out)
                out = jnp.where(order == 4, 2.0 * t2 * t2 - 1.0, out)
            return out

        return jnp.where(k < base * base, pick(k // base, y) * pick(k % base, x), 0.0)

    nt = (((1,), (1,)), ((), ()))
    gram = lax.dot_general(basis(32, 5), w, nt, precision=HIGH, preferred_element_type=F32)
    rhs = lax.dot_general(basis(16, 3), wd, nt, precision=HIGH, preferred_element_type=F32)
    return jnp.concatenate([gram, rhs], 0)


def solve_lanes(mom):
    m = lambda a, b: mom[5 * a + b : 5 * a + b + 1, :]
    cache = {}

    def entry(k, l):
        u, v, s, t = k // 3, k % 3, l // 3, l % 3
        key = tuple(sorted(((u + s, v + t), (abs(u - s), v + t), (u + s, abs(v - t)), (abs(u - s), abs(v - t)))))
        if key not in cache:
            cache[key] = 0.25 * ((m(*key[0]) + m(*key[1])) + (m(*key[2]) + m(*key[3])))
        return cache[key]

    a = [[entry(k, l) for l in range(k + 1)] for k in range(9)]
    b = [mom[32 + k : 33 + k, :] for k in range(9)]
    inv = [None] * 9
    for j in range(9):
        inv[j] = 1.0 / a[j][j]
        for k in range(j + 1, 9):
            f = a[k][j] * inv[j]
            for l in range(j + 1, k + 1):
                a[k][l] = a[k][l] - f * a[l][j]
            b[k] = b[k] - f * b[j]
    out = [None] * 9
    for j in reversed(range(9)):
        total = b[j]
        for k in range(j + 1, 9):
            total = total - a[k][j] * out[k]
        out[j] = total * inv[j]
    return out


def coadd_kernel(bins_ref, owner_ref, tx_ref, ty_ref, weight_hbm, smooth_hbm, coadd_ref, offsets_ref, *scratch):
    (wv, sv, bins, mom, sky_mom, exp_mom, offs, px), scratch = scratch[:8], scratch[8:]
    bufs, scratch = scratch[:32], scratch[32:]
    load_sems, send_sems, recv_sems, bin_s, bin_r, sky_s, sky_r, exp_s, exp_r = scratch
    me, band = lax.axis_index("exp"), lax.axis_index("sky")
    x, z = me // 4, lax.rem(me, 4)

    barrier = pltpu.get_barrier_semaphore()
    for k in range(1, NEXP):
        pl.semaphore_signal(barrier, inc=1, device_id=(lax.rem(me + k, NEXP), band), device_id_type=MESH)
    for k in range(1, SKY):
        pl.semaphore_signal(barrier, inc=1, device_id=(me, lax.rem(band + k, SKY)), device_id_type=MESH)
    load_w = pltpu.make_async_copy(weight_hbm, wv, load_sems.at[0])
    load_s = pltpu.make_async_copy(smooth_hbm, sv, load_sems.at[1])
    load_w.start()
    load_s.start()
    pl.semaphore_wait(barrier, NEXP + SKY - 2)

    bin_copies = []
    for k in range(1, NEXP):
        to = lax.rem(me + k, NEXP)
        copy = pltpu.make_async_remote_copy(
            src_ref=bins_ref.at[to], dst_ref=bins.at[me], send_sem=bin_s.at[k], recv_sem=bin_r.at[k],
            device_id=(to, band), device_id_type=MESH,
        )
        copy.start()
        bin_copies.append(copy)
    make = lambda part, n: [
        Scatter(part, half, x, z, band, bufs[8 * (2 * n + half) : 8 * (2 * n + half) + 8],
                (send_sems, recv_sems), 12 * (2 * n + half))
        for half in range(2)
    ]
    den, num = make(wv, 0), make(sv, 1)
    for part in den:
        part.start1(weight_hbm)
    for part in den:
        part.start2(weight_hbm)

    bins[me] = bins_ref[me]
    owner = owner_ref[...].astype(F32)
    both = owner + owner.T
    eye = iota((NEXP, NEXP), 0) == iota((NEXP, NEXP), 1)
    degree = jnp.sum(both, axis=1, keepdims=True) + LAMBDA_REG
    inverse = invert(jnp.where(eye, degree, 0.0) - both)
    lane, row = iota((NEXP, 128), 1), iota((NEXP, 128), 0)
    first = lax.rem(lane, NEXP)
    shift = lane // NEXP + 1
    second = lax.rem(first + shift, NEXP)
    at_first, at_second = row == first, row == second
    partner = jnp.dot(both, jnp.where(at_second, 1.0, 0.0), precision=HIGH, preferred_element_type=F32)
    used = jnp.sum(jnp.where(at_first, partner, 0.0), axis=0, keepdims=True)
    used = jnp.where((shift[:1] == 8) & (first[:1] >= 8), 0.0, used)
    sign = jnp.where(at_first, 1.0, 0.0) - jnp.where(at_second, 1.0, 0.0)

    for copy in bin_copies:
        copy.wait_recv()
    own = moments(bins, me, band)
    mom[...] = own
    sky_mom[band] = own
    sky_copies = []
    for k in range(1, SKY):
        copy = pltpu.make_async_remote_copy(
            src_ref=mom, dst_ref=sky_mom.at[band], send_sem=sky_s.at[k], recv_sem=sky_r.at[k],
            device_id=(me, lax.rem(band + k, SKY)), device_id_type=MESH,
        )
        copy.start()
        sky_copies.append(copy)
    for copy in sky_copies:
        copy.wait()
    total = sky_mom[0]
    for k in range(1, SKY):
        total = total + sky_mom[k]
    mom[...] = total
    exp_mom[me] = total
    exp_copies = []
    for k in range(1, NEXP):
        copy = pltpu.make_async_remote_copy(
            src_ref=mom, dst_ref=exp_mom.at[me], send_sem=exp_s.at[k], recv_sem=exp_r.at[k],
            device_id=(lax.rem(me + k, NEXP), band), device_id_type=MESH,
        )
        copy.start()
        exp_copies.append(copy)

    load_w.wait()
    for part in den:
        part.start3()

    for copy in exp_copies:
        copy.wait()
    total = exp_mom[0]
    for k in range(1, NEXP):
        total = total + exp_mom[k]
    mom[...] = total
    fits = jnp.concatenate(solve_lanes(mom) + [jnp.zeros((7, 128), F32)], 0)
    fits = jnp.where(used > 0.0, fits, 0.0)
    nt = (((1,), (1,)), ((), ()))
    right = lax.dot_general(sign, fits, nt, precision=HIGH, preferred_element_type=F32)
    answer = jnp.dot(inverse, right, precision=HIGH, preferred_element_type=F32)
    offsets_ref[...] = answer[:, :9]
    offs[:, 0:NEXP] = answer
    coef = offs[pl.ds(me, 1), :]
    for u in range(3):
        line = coef[:, 3 * u : 3 * u + 1] * tx_ref[0:1, :]
        for v in range(1, 3):
            line = line + coef[:, 3 * u + v : 3 * u + v + 1] * tx_ref[v : v + 1, :]
        for m in range(16):
            px[m, u : u + 1, :] = line[:, 256 * m : 256 * m + 256]

    load_s.wait()

    def numerator(half, dist):
        lead = (x, z)[half]
        g = lax.rem(lead + dist, 4)

        def body(i, carry):
            b, r = i // 4, pl.multiple_of(256 * half + lax.rem(i, 4) * 64, 64)
            cx, cz = (g, b) if half == 0 else (b, g)
            rows = pl.ds(r, 64)
            back = None
            for u in range(3):
                ty = ty_ref[u, rows, :]
                term = jnp.concatenate([ty, ty], 1) * px[4 * cx + cz, u : u + 1, :]
                back = term if back is None else back + term
            sv[cx, cz, rows, :] = wv[cx, cz, rows, :] * (sv[cx, cz, rows, :] - back)
            return carry

        lax.fori_loop(0, 16, body, 0)

    for half in range(2):
        numerator(half, 2)
        num[half].start1(sv)
    for half in range(2):
        numerator(half, 1)
        numerator(half, 3)
        num[half].start2(sv)
    for half in range(2):
        numerator(half, 0)
    for part in den:
        part.finish1()
    for part in num:
        part.start3()
    for part in den:
        part.start6()
    for part in num:
        part.finish1()
    for part in den:
        part.finish2()
    for part in num:
        part.start6()
    for part in num:
        part.finish2()
    for half in range(2):

        def body(i, carry):
            r = pl.multiple_of(i * 64, 64)
            coadd_ref[pl.ds(256 * half + r, 64), :] = num[half].total(r) / (PRIOR + den[half].total(r))
            return carry

        lax.fori_loop(0, 4, body, 0)
    for copy in bin_copies:
        copy.wait_send()
    for part in den + num:
        part.drain()


def fit_and_sum(bins, owner, tx, ty, weight, smoothed):
    big = lambda *shape: pltpu.VMEM(shape, F32)
    set_of = [big(4, 128, 256), big(4, 128, 256), big(4, 256, 256), big(4, 256, 256),
              big(128, 256), big(128, 256), big(256, 256), big(256, 256)]
    vmem = pl.BlockSpec(memory_space=pltpu.VMEM)
    hbm = pl.BlockSpec(memory_space=pl.ANY)
    dma = lambda n: pltpu.SemaphoreType.DMA((n,))
    return pl.pallas_call(
        coadd_kernel,
        in_specs=[vmem, vmem, vmem, vmem, hbm, hbm],
        out_specs=[vmem, vmem],
        out_shape=[jax.ShapeDtypeStruct((ROWS, 256), F32), jax.ShapeDtypeStruct((NEXP, 9), F32)],
        scratch_shapes=[
            big(4, 4, ROWS, 256), big(4, 4, ROWS, 256), big(NEXP, 8, BCOLS), big(48, 128), big(SKY, 48, 128),
            big(NEXP, 48, 128), big(NEXP, 128), big(16, 8, 256),
        ] + set_of * 4 + [dma(2), dma(48), dma(48), dma(NEXP), dma(NEXP), dma(SKY), dma(SKY), dma(NEXP), dma(NEXP)],
        compiler_params=pltpu.CompilerParams(
            collective_id=0, has_side_effects=True, vmem_limit_bytes=48 << 20
        ),
        cost_estimate=pl.CostEstimate(flops=10**8, bytes_accessed=64 << 20, transcendentals=0),
        name="fit_and_sum",
    )(bins, owner, tx, ty, weight.reshape(4, 4, ROWS, 256), smoothed.reshape(4, 4, ROWS, 256))


def per_device(image, variance, mask, foot_start, pair_owner):
    up_pairs = [(i, i + 1) for i in range(SKY - 1)]
    up = lax.ppermute(image[0, ROWS - HALO :, :], "sky", up_pairs)
    down = lax.ppermute(image[0, :HALO, :], "sky", [(j, i) for i, j in up_pairs])
    weight, bins = weigh(image, variance, mask, foot_start)
    smoothed, tx, ty = smooth(image, up, down, foot_start)
    return tuple(fit_and_sum(bins, pair_owner, tx, ty, weight, smoothed))


def solution(mesh):
    placed = (P("exp", "sky", None), P("exp", "sky", None), P("exp", "sky", None), P(), P())
    return jax.shard_map(
        per_device, mesh=mesh, in_specs=placed, out_specs=(P("sky", "exp"), P()), check_vma=False
    )
```

```python
import functools

import jax
import jax.numpy as jnp
import numpy as np
from jax import lax
from jax.experimental import pallas as pl
from jax.experimental.pallas import tpu as pltpu
from jax.sharding import PartitionSpec as P

F32 = jnp.float32
BF16 = jnp.bfloat16
HIGH = lax.Precision.HIGHEST
MESH = pl.DeviceIdType.MESH
BIN = 16
RADIUS = 10
NEXP = 16
ROWS = 512
COLS = 4096
SKY = 8
BROWS = 32
BCOLS = 256
FOOT_BINS = 192
HALO = 16
LAMBDA_REG = 0.25
PRIOR = 1.0


def iota(shape, dim):
    return lax.broadcasted_iota(jnp.int32, shape, dim)


def center(index, total):
    return (2.0 * index.astype(F32) + 1.0) / total - 1.0


def cheb(order, t):
    if order == 0:
        return jnp.ones_like(t)
    if order == 1:
        return t
    return 2.0 * t * t - 1.0


def split(value):
    high = value.astype(BF16)
    return high, (value - high.astype(F32)).astype(BF16)


def taps_matrix(offset):
    total = np.sum(np.exp(-(np.arange(-RADIUS, RADIUS + 1) ** 2) / 50.0))
    exact = np.where(np.abs(offset) <= RADIUS, np.exp(-(offset**2) / 50.0) / total, 0.0)
    high = exact.astype(BF16)
    return jnp.asarray(high), jnp.asarray((exact - high.astype(np.float64)).astype(BF16))


def add_into(dst, terms, blocks, rows):
    per = rows // 64

    def body(i, carry):
        b, r = i // per, pl.multiple_of((i % per) * 64, 64)
        total = terms[0](b, r)
        for term in terms[1:]:
            total = total + term(b, r)
        dst(b, r, total)
        return carry

    lax.fori_loop(0, blocks * per, body, 0)


class Scatter:
    def __init__(self, part, lead, row0, rows, place, bufs, sems, first_sem):
        self.part, self.lead, self.row0, self.half = part, lead, row0, rows // 2
        self.me, self.sky = place
        self.f1p, self.f1m, self.rp, self.rm, self.f2p, self.f2m, self.r2p, self.r2m = bufs
        self.send_sems, self.recv_sems = sems
        self.sem = first_sem
        self.copies = {}

    def device(self, axis, shift):
        x, z = self.me
        if axis == 0:
            x = lax.rem(x + shift + 4, 4)
        else:
            z = lax.rem(z + shift + 4, 4)
        return (4 * x + z, self.sky)

    def group(self, dist, r):
        g = lax.rem(self.me[self.lead] + dist, 4)
        rows = pl.ds(self.row0 + r, self.half)
        return self.part.at[g, :, rows, :] if self.lead == 0 else self.part.at[:, g, rows, :]

    def send(self, key, src, dst, axis, shift):
        n = self.sem
        self.sem += 1
        copy = pltpu.make_async_remote_copy(
            src_ref=src, dst_ref=dst, send_sem=self.send_sems.at[n], recv_sem=self.recv_sems.at[n],
            device_id=self.device(axis, shift), device_id_type=MESH,
        )
        copy.start()
        self.copies[key] = copy

    def start1(self):
        self.send("1p", self.group(2, 0), self.f1p, self.lead, 1)
        self.send("1m", self.group(2, self.half), self.f1m, self.lead, -1)

    def start2p(self):
        self.send("2p", self.group(1, self.half), self.rp.at[:, pl.ds(self.half, self.half), :], self.lead, 1)

    def start2m(self):
        self.send("2m", self.group(3, 0), self.rm.at[:, pl.ds(0, self.half), :], self.lead, -1)

    def load(self, dist, shift):
        g = lax.rem(self.me[self.lead] + dist, 4)

        def get(b, r):
            rows = pl.ds(self.row0 + shift + r, 64)
            return self.part[g, b, rows, :] if self.lead == 0 else self.part[b, g, rows, :]

        return get

    def start3(self):
        for key, buf, dist, shift, to in (("p", self.f1p, 1, 0, 1), ("m", self.f1m, 3, self.half, -1)):
            self.copies["1" + key].wait_recv()

            def put(b, r, v, buf=buf):
                buf[b, pl.ds(r, 64), :] = v

            add_into(put, [lambda b, r, buf=buf: buf[b, pl.ds(r, 64), :], self.load(dist, shift)], 4, self.half)
            land = self.rp if to == 1 else self.rm
            self.send("3" + key, buf, land.at[:, pl.ds(shift, self.half), :], self.lead, to)

    def finish1(self):
        for key in ("2p", "2m", "3p", "3m"):
            self.copies[key].wait_recv()

        def put(b, r, v):
            self.rp[b, pl.ds(r, 64), :] = v

        add_into(
            put,
            [lambda b, r: self.rp[b, pl.ds(r, 64), :], lambda b, r: self.rm[b, pl.ds(r, 64), :], self.load(0, 0)],
            4, 2 * self.half,
        )
        axis = 1 - self.lead
        at = lambda dist: lax.rem(self.me[axis] + dist, 4)
        top, low = pl.ds(0, self.half), pl.ds(self.half, self.half)
        self.send("4p", self.rp.at[at(2), top, :], self.f2p, axis, 1)
        self.send("4m", self.rp.at[at(2), low, :], self.f2m, axis, -1)
        self.send("5p", self.rp.at[at(1), low, :], self.r2p.at[low, :], axis, 1)
        self.send("5m", self.rp.at[at(3), top, :], self.r2m.at[top, :], axis, -1)

    def start6(self):
        axis = 1 - self.lead
        for key, buf, dist, shift, to in (("p", self.f2p, 1, 0, 1), ("m", self.f2m, 3, self.half, -1)):
            self.copies["4" + key].wait_recv()
            g = lax.rem(self.me[axis] + dist, 4)

            def put(b, r, v, buf=buf):
                buf[pl.ds(r, 64), :] = v

            add_into(
                put,
                [lambda b, r, buf=buf: buf[pl.ds(r, 64), :],
                 lambda b, r, g=g, shift=shift: self.rp[g, pl.ds(shift + r, 64), :]],
                1, self.half,
            )
            land = self.r2p if to == 1 else self.r2m
            self.send("6" + key, buf, land.at[pl.ds(shift, self.half), :], axis, to)

    def finish2(self):
        for key in ("5p", "5m", "6p", "6m"):
            self.copies[key].wait_recv()

    def total(self, r):
        g = self.me[1 - self.lead]
        return self.rp[g, pl.ds(r, 64), :] + self.r2p[pl.ds(r, 64), :] + self.r2m[pl.ds(r, 64), :]

    def drain(self):
        for copy in self.copies.values():
            copy.wait_send()


def invert(system):
    lane, row = iota((NEXP, 128), 1), iota((NEXP, 128), 0)
    work = jnp.concatenate([system, jnp.zeros((NEXP, 112), F32)], 1)
    work = work + jnp.where(lane == row + NEXP, 1.0, 0.0)
    for j in range(NEXP):
        pivot_row = work[j : j + 1, :] / work[j : j + 1, j : j + 1]
        factor = work[:, j : j + 1]
        work = jnp.where(row == j, pivot_row, work - factor * pivot_row)
    return work[:, NEXP : 2 * NEXP]


def moments(bins, me, band):
    image = jnp.concatenate([bins[:, 0, :], bins[:, 1, :]], 1)
    weight = jnp.concatenate([bins[:, 2, :], bins[:, 3, :]], 1)
    ws, ds = [], []
    for d in range(1, 9):
        other = pltpu.roll(weight, NEXP - d, 0)
        w = weight * other / (weight + other + 1.0)
        ws.append(w)
        ds.append(w * (image - pltpu.roll(image, NEXP - d, 0)))
    w, wd = jnp.concatenate(ws, 0), jnp.concatenate(ds, 0)

    def basis(rows, base):
        k, lane = iota((rows, 512), 0), iota((rows, 512), 1)
        y = center(BROWS * band + 2 * me + lane // 256, BCOLS)
        x = center(lane % 256, BCOLS)

        def pick(order, t):
            t2 = 2.0 * t * t - 1.0
            out = jnp.where(order == 0, 1.0, jnp.where(order == 1, t, t2))
            if base == 5:
                out = jnp.where(order == 3, 2.0 * t * t2 - t, out)
                out = jnp.where(order == 4, 2.0 * t2 * t2 - 1.0, out)
            return out

        return jnp.where(k < base * base, pick(k // base, y) * pick(k % base, x), 0.0)

    nt = (((1,), (1,)), ((), ()))
    gram = lax.dot_general(basis(32, 5), w, nt, precision=HIGH, preferred_element_type=F32)
    rhs = lax.dot_general(basis(16, 3), wd, nt, precision=HIGH, preferred_element_type=F32)
    return jnp.concatenate([gram, rhs], 0)


def solve_lanes(mom):
    m = lambda a, b: mom[5 * a + b : 5 * a + b + 1, :]
    cache = {}

    def entry(k, l):
        u, v, s, t = k // 3, k % 3, l // 3, l % 3
        key = tuple(sorted(((u + s, v + t), (abs(u - s), v + t), (u + s, abs(v - t)), (abs(u - s), abs(v - t)))))
        if key not in cache:
            cache[key] = 0.25 * ((m(*key[0]) + m(*key[1])) + (m(*key[2]) + m(*key[3])))
        return cache[key]

    a = [[entry(k, l) for l in range(k + 1)] for k in range(9)]
    b = [mom[32 + k : 33 + k, :] for k in range(9)]
    inv = [None] * 9
    for j in range(9):
        inv[j] = 1.0 / a[j][j]
        for k in range(j + 1, 9):
            f = a[k][j] * inv[j]
            for l in range(j + 1, k + 1):
                a[k][l] = a[k][l] - f * a[l][j]
            b[k] = b[k] - f * b[j]
    out = [None] * 9
    for j in reversed(range(9)):
        total = b[j]
        for k in range(j + 1, 9):
            total = total - a[k][j] * out[k]
        out[j] = total * inv[j]
    return out


SETS = (
    (4, lambda i: (2, i)),
    (3, lambda i: (lax.rem(i + 3, 4), 2)),
    (3, lambda i: (1, lax.rem(i + 3, 4))),
    (3, lambda i: (3, lax.rem(i + 3, 4))),
    (3, lambda i: (0, lax.rem(i + 3, 4))),
)
NUM_SCRATCH = 19


def coadd_kernel(image_hbm, variance_hbm, mask_hbm, foot_hbm, owner_hbm, ch_hbm, cl_hbm, rh_hbm, rl_hbm,
                 coadd_ref, offsets_ref, *scratch):
    (img, wv, sv, mask_ref, foot_ref, owner_ref, ch_ref, cl_ref, rh_ref, rl_ref, up_ref, down_ref, xh, xl, tx_ref,
     ty_ref, blocks, sums, bins_own), scratch = scratch[:NUM_SCRATCH], scratch[NUM_SCRATCH:]
    (bins, mom, sky_mom, exp_mom, offs, coefs), scratch = scratch[:6], scratch[6:]
    bufs, scratch = scratch[:48], scratch[48:]
    (small_sems, var_sems, img_sems, halo_s, halo_r, send_sems, recv_sems,
     bin_s, bin_r, sky_s, sky_r, exp_s, exp_r) = scratch
    me, band = lax.axis_index("exp"), lax.axis_index("sky")
    x, z = me // 4, lax.rem(me, 4)
    tall = ROWS + 2 * HALO

    barrier = pltpu.get_barrier_semaphore()
    for k in range(1, NEXP):
        pl.semaphore_signal(barrier, inc=1, device_id=(lax.rem(me + k, NEXP), band), device_id_type=MESH)
    for k in range(1, SKY):
        pl.semaphore_signal(barrier, inc=1, device_id=(me, lax.rem(band + k, SKY)), device_id_type=MESH)

    def place(rel):
        return lax.rem(x + rel[0], 4), lax.rem(z + rel[1], 4)

    def load_var(n, rel):
        cx, cz = place(rel)
        cols = pl.ds(pl.multiple_of(256 * (4 * cx + cz), 256), 256)
        return pltpu.make_async_copy(variance_hbm.at[0, :, cols], wv.at[cx, cz], var_sems.at[n])

    def load_img(n, rel):
        cx, cz = place(rel)
        cols = pl.ds(pl.multiple_of(256 * (4 * cx + cz), 256), 256)
        return pltpu.make_async_copy(image_hbm.at[0, :, cols], img.at[4 * cx + cz], img_sems.at[n])

    def each(fn, sets=range(5)):
        for s in sets:
            base = sum(SETS[t][0] for t in range(s))

            def body(i, carry, base=base, s=s):
                fn(base + i, SETS[s][1](i))
                return carry

            lax.fori_loop(0, SETS[s][0], body, 0)

    small = [
        pltpu.make_async_copy(src, dst, small_sems.at[n])
        for n, (src, dst) in enumerate((
            (mask_hbm.at[0], mask_ref), (foot_hbm, foot_ref), (owner_hbm, owner_ref),
            (ch_hbm, ch_ref), (cl_hbm, cl_ref), (rh_hbm, rh_ref), (rl_hbm, rl_ref),
        ))
    ]
    for copy in small[:2]:
        copy.start()
    each(lambda n, rel: load_var(n, rel).start())
    each(lambda n, rel: load_img(n, rel).start())
    for copy in small[2:]:
        copy.start()

    for copy in small[:2]:
        copy.wait()
    start = foot_ref[me]
    cell = iota((BROWS, BCOLS), 1)
    inside = (cell >= start) & (cell < start + FOOT_BINS)
    blocks[...] = jnp.where(inside, mask_ref[...].astype(F32), 0.0).astype(BF16)

    def onehot(m):
        hit = iota((256, 256), 0) == 16 * m + iota((256, 256), 1) // BIN
        return jnp.where(hit, 1.0, 0.0).astype(BF16)

    def weights(n, rel):
        load_var(n, rel).wait()
        cx, cz = place(rel)
        wide = jnp.dot(blocks[...], onehot(4 * cx + cz), preferred_element_type=F32)
        for r in range(4):
            rows = slice(128 * r, 128 * r + 128)
            keep = jnp.broadcast_to(wide[8 * r : 8 * r + 8][:, None, :], (8, BIN, 256)).reshape(128, 256)
            w = keep * (1.0 / wv[cx, cz, rows, :])
            wv[cx, cz, rows, :] = w
            sums[4 * cx + cz, 8 * r : 8 * r + 8, :] = jnp.sum(w.reshape(8, BIN, 256), axis=1)

    where = ((x, z), band)
    take = lambda n: bufs[8 * n : 8 * n + 8]
    sems = (send_sems, recv_sems)
    den = [Scatter(wv, h, 256 * h, 256, where, take(h), sems, 12 * h) for h in range(2)]
    num = [Scatter(sv, h, 256 * h + 128 * q, 128, where, take(2 + 2 * q + h), sems, 12 * (2 + 2 * q + h))
           for q in range(2) for h in range(2)]

    each(weights, [0])
    pl.semaphore_wait(barrier, NEXP + SKY - 2)
    den[0].start1()
    halos = []
    for n, (rows, dst, to) in enumerate(((ROWS - HALO, up_ref, band + 1), (0, down_ref, band + SKY - 1))):
        copy = pltpu.make_async_remote_copy(
            src_ref=image_hbm.at[0, pl.ds(rows, HALO), :], dst_ref=dst, send_sem=halo_s.at[n], recv_sem=halo_r.at[n],
            device_id=(me, lax.rem(to, SKY)), device_id_type=MESH,
        )
        copy.start()
        halos.append(copy)
    each(weights, [1])
    den[1].start1()
    each(weights, [2])
    den[0].start2p()
    each(weights, [3])
    den[0].start2m()
    each(weights, [4])
    den[1].start2p()
    den[1].start2m()

    def image_sums(n, rel):
        load_img(n, rel).wait()
        cx, cz = place(rel)
        m = 4 * cx + cz
        parts = []
        for r in range(4):
            parts.append(jnp.sum(img[m, 128 * r : 128 * r + 128, :].reshape(8, BIN, 256), axis=1))
        both = jnp.concatenate([jnp.concatenate(parts, 0) * (1.0 / (BIN * BIN)), sums[m]], 0)
        high = both.astype(BF16)
        rest = both - high.astype(F32)
        mid = rest.astype(BF16)
        low = (rest - mid.astype(F32)).astype(BF16)
        got = lax.dot_general(
            jnp.concatenate([high, mid, low], 0), onehot(m), (((1,), (1,)), ((), ())), preferred_element_type=F32
        )
        binned[...] = binned[...] + (got[:64] + got[64:128] + got[128:])

    binned = bins_own.at[NEXP]
    binned[...] = jnp.zeros((64, BCOLS), F32)
    each(image_sums)
    for m in range(NEXP):
        tile = [binned[2 * m : 2 * m + 2, :], binned[32 + 2 * m : 34 + 2 * m, :], jnp.zeros((4, BCOLS), F32)]
        bins_own[m, 0:8, :] = jnp.concatenate(tile, 0)
    bin_copies = []
    for k in range(1, NEXP):
        to = lax.rem(me + k, NEXP)
        copy = pltpu.make_async_remote_copy(
            src_ref=bins_own.at[to, pl.ds(0, 8), :], dst_ref=bins.at[me], send_sem=bin_s.at[k], recv_sem=bin_r.at[k],
            device_id=(to, band), device_id_type=MESH,
        )
        copy.start()
        bin_copies.append(copy)
    bins[me] = bins_own[me, 0:8, :]

    for copy in small[2:]:
        copy.wait()
    for copy in halos:
        copy.wait_recv()

    def put(j, first, lane0, value):
        rows, width = value.shape
        col = 256 * j - 128 + lane0 + iota((1, width), 1)
        keep = (col >= BIN * start) & (col < BIN * (start + FOOT_BINS))
        high, low = split(jnp.where(keep, value, 0.0))
        xh[first : first + rows, lane0 : lane0 + width] = high
        xl[first : first + rows, lane0 : lane0 + width] = low

    def row_pass(value, out):
        high, low = split(value)
        for i in range(ROWS // 128):
            zh, zl = high[128 * i : 128 * i + 160], low[128 * i : 128 * i + 160]
            out(
                128 * i,
                jnp.dot(rh_ref[...], zh, preferred_element_type=F32)
                + jnp.dot(rl_ref[...], zh, preferred_element_type=F32)
                + jnp.dot(rh_ref[...], zl, preferred_element_type=F32),
            )

    def smooth(n, rel):
        cx, cz = place(rel)
        j = 4 * cx + cz
        before, after = jnp.maximum(j - 1, 0), jnp.minimum(j + 1, 15)
        lo = pl.multiple_of(jnp.maximum(256 * j - 128, 0), 128)
        mid = pl.multiple_of(256 * j, 128)
        hi = pl.multiple_of(jnp.minimum(256 * j + 256, COLS - 128), 128)
        for first, ref, known in ((0, up_ref, band > 0), (HALO + ROWS, down_ref, band < SKY - 1)):
            put(j, first, 0, jnp.where(known, ref[:, pl.ds(lo, 128)], 0.0))
            put(j, first, 128, jnp.where(known, ref[:, pl.ds(mid, 256)], 0.0))
            put(j, first, 384, jnp.where(known, ref[:, pl.ds(hi, 128)], 0.0))
        put(j, HALO, 0, img[before, :, 128:256])
        put(j, HALO, 128, img[j])
        put(j, HALO, 384, img[after, :, 0:128])
        xcol = center(256 * j - 128 + iota((16, 512), 1), COLS)
        order = iota((16, 512), 0)
        put(j, tall, 0, jnp.where(order == 0, 1.0, jnp.where(order == 1, xcol, 2.0 * xcol * xcol - 1.0)))
        across = (
            jnp.dot(xh[...], ch_ref[...], preferred_element_type=F32)
            + jnp.dot(xl[...], ch_ref[...], preferred_element_type=F32)
            + jnp.dot(xh[...], cl_ref[...], preferred_element_type=F32)
        )
        tx_ref[j] = across[tall : tall + 8]

        def out(r, part):
            sv[cx, cz, r : r + 128, :] = part

        row_pass(across[:tall], out)

    each(smooth, [0])

    owner = owner_ref[...].astype(F32)
    both = owner + owner.T
    eye = iota((NEXP, NEXP), 0) == iota((NEXP, NEXP), 1)
    degree = jnp.sum(both, axis=1, keepdims=True) + LAMBDA_REG
    inverse = invert(jnp.where(eye, degree, 0.0) - both)
    lane, row = iota((NEXP, 128), 1), iota((NEXP, 128), 0)
    first = lax.rem(lane, NEXP)
    shift = lane // NEXP + 1
    second = lax.rem(first + shift, NEXP)
    at_first, at_second = row == first, row == second
    partner = jnp.dot(both, jnp.where(at_second, 1.0, 0.0), precision=HIGH, preferred_element_type=F32)
    used = jnp.sum(jnp.where(at_first, partner, 0.0), axis=0, keepdims=True)
    used = jnp.where((shift[:1] == 8) & (first[:1] >= 8), 0.0, used)
    sign = jnp.where(at_first, 1.0, 0.0) - jnp.where(at_second, 1.0, 0.0)

    for copy in bin_copies:
        copy.wait_recv()
    own = moments(bins, me, band)
    mom[0] = own
    sky_mom[band] = own
    sky_copies = []
    for k in range(1, SKY):
        copy = pltpu.make_async_remote_copy(
            src_ref=mom.at[0], dst_ref=sky_mom.at[band], send_sem=sky_s.at[k], recv_sem=sky_r.at[k],
            device_id=(me, lax.rem(band + k, SKY)), device_id_type=MESH,
        )
        copy.start()
        sky_copies.append(copy)
    ty_row = band * ROWS - HALO + iota((tall, 128), 0)
    y = center(ty_row, ROWS * SKY)
    known = (ty_row >= 0) & (ty_row < ROWS * SKY)
    for u in range(3):

        def out(r, part, u=u):
            ty_ref[u, r : r + 128, :] = part

        row_pass(jnp.where(known, cheb(u, y), 0.0), out)
    for copy in sky_copies:
        copy.wait_recv()
    total = sky_mom[0]
    for k in range(1, SKY):
        total = total + sky_mom[k]
    mom[1] = total
    exp_mom[me] = total
    exp_copies = []
    for k in range(1, NEXP):
        copy = pltpu.make_async_remote_copy(
            src_ref=mom.at[1], dst_ref=exp_mom.at[me], send_sem=exp_s.at[k], recv_sem=exp_r.at[k],
            device_id=(lax.rem(me + k, NEXP), band), device_id_type=MESH,
        )
        copy.start()
        exp_copies.append(copy)
    for part in den:
        part.start3()
    each(smooth, [1])
    for copy in exp_copies:
        copy.wait_recv()
    total = exp_mom[0]
    for k in range(1, NEXP):
        total = total + exp_mom[k]
    fits = jnp.concatenate(solve_lanes(total) + [jnp.zeros((7, 128), F32)], 0)
    fits = jnp.where(used > 0.0, fits, 0.0)
    nt = (((1,), (1,)), ((), ()))
    right = lax.dot_general(sign, fits, nt, precision=HIGH, preferred_element_type=F32)
    answer = jnp.dot(inverse, right, precision=HIGH, preferred_element_type=F32)
    offsets_ref[...] = answer[:, :9]
    offs[:, 0:NEXP] = answer
    coef = offs[pl.ds(me, 1), :]
    for k in range(9):
        coefs[k : k + 1, :] = jnp.broadcast_to(coef[:, k : k + 1], (1, 256))

    def numerator(half, dist):
        g = lax.rem((x, z)[half] + dist, 4)

        def chunk(b, carry):
            cx, cz = (g, b) if half == 0 else (b, g)
            tx = tx_ref[4 * cx + cz]
            lines = []
            for u in range(3):
                line = coefs[3 * u : 3 * u + 1, :] * tx[0:1]
                for v in range(1, 3):
                    line = line + coefs[3 * u + v : 3 * u + v + 1, :] * tx[v : v + 1]
                lines.append(line)
            for i in range(4):
                rows = slice(256 * half + 64 * i, 256 * half + 64 * i + 64)
                back = None
                for u in range(3):
                    ty = ty_ref[u, rows, :]
                    term = jnp.concatenate([ty, ty], 1) * lines[u]
                    back = term if back is None else back + term
                sv[cx, cz, rows, :] = wv[cx, cz, rows, :] * (sv[cx, cz, rows, :] - back)
            return carry

        lax.fori_loop(0, 4, chunk, 0)

    numerator(0, 2)
    num[0].start1()
    numerator(1, 2)
    num[1].start1()
    each(smooth, [2])
    numerator(0, 1)
    num[0].start2p()
    each(smooth, [3])
    numerator(0, 3)
    num[0].start2m()
    each(smooth, [4])
    numerator(1, 1)
    num[1].start2p()
    numerator(1, 3)
    num[1].start2m()
    for part in num[2:]:
        part.start1()
        part.start2p()
        part.start2m()
    for half in range(2):
        numerator(half, 0)
    for part in den:
        part.finish1()
    for part in num[:2]:
        part.start3()
    for part in den:
        part.start6()
    for part in num[2:]:
        part.start3()
    for part in num[:2]:
        part.finish1()
    for part in den:
        part.finish2()
    for part in num[:2]:
        part.start6()
    for part in num[2:]:
        part.finish1()
    for part in num[2:]:
        part.start6()

    def finish(n):
        part = num[n]
        part.finish2()
        h, q = n % 2, n // 2

        def body(i, carry):
            r = pl.multiple_of(i * 64, 64)
            value = part.total(r) / (PRIOR + den[h].total(128 * q + r))
            coadd_ref[pl.ds(256 * h + 128 * q + r, 64), :] = value
            return carry

        lax.fori_loop(0, 2, body, 0)

    for n in range(4):
        finish(n)
    for copy in halos + bin_copies + sky_copies + exp_copies:
        copy.wait_send()
    for part in den + num:
        part.drain()


def per_device(image, variance, mask, foot_start, pair_owner):
    k, n = np.arange(512)[:, None], np.arange(256)[None, :]
    ch, cl = taps_matrix(k - n - 128)
    k, n = np.arange(160)[None, :], np.arange(128)[:, None]
    rh, rl = taps_matrix(k - n - HALO)
    big = lambda *shape: pltpu.VMEM(shape, F32)
    half = lambda *shape: pltpu.VMEM(shape, BF16)
    pieces = lambda r: [big(4, r // 2, 256), big(4, r // 2, 256), big(4, r, 256), big(4, r, 256),
                        big(r // 2, 256), big(r // 2, 256), big(r, 256), big(r, 256)]
    dma = lambda n: pltpu.SemaphoreType.DMA((n,))
    vmem = pl.BlockSpec(memory_space=pltpu.VMEM)
    tall = ROWS + 2 * HALO
    held = [
        big(16, ROWS, 256), big(4, 4, ROWS, 256), big(4, 4, ROWS, 256),
        pltpu.VMEM((BROWS, BCOLS), jnp.int32), pltpu.SMEM((NEXP,), jnp.int32), pltpu.VMEM((NEXP, NEXP), jnp.int32),
        half(512, 256), half(512, 256), half(128, 160), half(128, 160), big(HALO, COLS), big(HALO, COLS),
        half(tall + 16, 512), half(tall + 16, 512), big(16, 8, 256), big(3, ROWS, 128), half(BROWS, BCOLS),
        big(16, BROWS, 256), big(NEXP + 1, 64, BCOLS),
    ]
    fit = [big(NEXP, 8, BCOLS), big(2, 48, 128), big(SKY, 48, 128), big(NEXP, 48, 128), big(NEXP, 128), big(16, 256)]
    sems = [dma(7), dma(16), dma(16), dma(2), dma(2), dma(72), dma(72), dma(NEXP), dma(NEXP), dma(SKY), dma(SKY),
            dma(NEXP), dma(NEXP)]
    return tuple(pl.pallas_call(
        coadd_kernel,
        in_specs=[pl.BlockSpec(memory_space=pl.ANY)] * 9,
        out_specs=[vmem, vmem],
        out_shape=[jax.ShapeDtypeStruct((ROWS, 256), F32), jax.ShapeDtypeStruct((NEXP, 9), F32)],
        scratch_shapes=held + fit + pieces(256) * 2 + pieces(128) * 4 + sems,
        compiler_params=pltpu.CompilerParams(collective_id=0, has_side_effects=True, vmem_limit_bytes=56 << 20),
        name="coadd",
    )(image, variance, mask, foot_start, pair_owner, ch, cl, rh, rl))


def solution(mesh):
    placed = (P("exp", "sky", None), P("exp", "sky", None), P("exp", "sky", None), P(), P())
    return jax.shard_map(
        per_device, mesh=mesh, in_specs=placed, out_specs=(P("sky", "exp"), P()), check_vma=False
    )
```

```python
import functools

import jax
import jax.numpy as jnp
import numpy as np
from jax import lax
from jax.experimental import pallas as pl
from jax.experimental.pallas import tpu as pltpu
from jax.sharding import PartitionSpec as P

F32 = jnp.float32
BF16 = jnp.bfloat16
HIGH = lax.Precision.HIGHEST
MESH = pl.DeviceIdType.MESH
BIN = 16
RADIUS = 10
NEXP = 16
ROWS = 512
COLS = 4096
SKY = 8
BROWS = 32
BCOLS = 256
FOOT_BINS = 192
HALO = 16
LAMBDA_REG = 0.25
PRIOR = 1.0


def iota(shape, dim):
    return lax.broadcasted_iota(jnp.int32, shape, dim)


def center(index, total):
    return (2.0 * index.astype(F32) + 1.0) / total - 1.0


def cheb(order, t):
    if order == 0:
        return jnp.ones_like(t)
    if order == 1:
        return t
    return 2.0 * t * t - 1.0


def split(value):
    high = value.astype(BF16)
    return high, (value - high.astype(F32)).astype(BF16)


def taps_matrix(offset):
    total = np.sum(np.exp(-(np.arange(-RADIUS, RADIUS + 1) ** 2) / 50.0))
    exact = np.where(np.abs(offset) <= RADIUS, np.exp(-(offset**2) / 50.0) / total, 0.0)
    high = exact.astype(BF16)
    return jnp.asarray(high), jnp.asarray((exact - high.astype(np.float64)).astype(BF16))


def add_into(dst, terms, blocks, rows):
    per = rows // 64

    def body(i, carry):
        b, r = i // per, pl.multiple_of((i % per) * 64, 64)
        total = terms[0](b, r)
        for term in terms[1:]:
            total = total + term(b, r)
        dst(b, r, total)
        return carry

    lax.fori_loop(0, blocks * per, body, 0)


class Scatter:
    def __init__(self, part, lead, row0, rows, place, bufs, sems, first_sem):
        self.part, self.lead, self.row0, self.half = part, lead, row0, rows // 2
        self.me, self.sky = place
        self.f1p, self.f1m, self.rp, self.rm, self.f2p, self.f2m, self.r2p, self.r2m = bufs
        self.send_sems, self.recv_sems = sems
        self.sem = first_sem
        self.copies = {}
        self.first = {"p": [], "m": []}

    def device(self, axis, shift):
        x, z = self.me
        if axis == 0:
            x = lax.rem(x + shift + 4, 4)
        else:
            z = lax.rem(z + shift + 4, 4)
        return (4 * x + z, self.sky)

    def group(self, dist, r):
        g = lax.rem(self.me[self.lead] + dist, 4)
        rows = pl.ds(self.row0 + r, self.half)
        return self.part.at[g, :, rows, :] if self.lead == 0 else self.part.at[:, g, rows, :]

    def send(self, key, src, dst, axis, shift):
        n = self.sem
        self.sem += 1
        copy = pltpu.make_async_remote_copy(
            src_ref=src, dst_ref=dst, send_sem=self.send_sems.at[n], recv_sem=self.recv_sems.at[n],
            device_id=self.device(axis, shift), device_id_type=MESH,
        )
        copy.start()
        self.copies[key] = copy
        return copy

    def start1(self):
        self.first["p"].append(self.send("1p", self.group(2, 0), self.f1p, self.lead, 1))
        self.first["m"].append(self.send("1m", self.group(2, self.half), self.f1m, self.lead, -1))

    def start1_chunk(self, dist):
        b = lax.rem(self.me[1 - self.lead] + dist, 4)
        key = str(dist)
        self.first["p"].append(self.send("1p" + key, self.group(2, 0).at[b], self.f1p.at[b], self.lead, 1))
        self.first["m"].append(self.send("1m" + key, self.group(2, self.half).at[b], self.f1m.at[b], self.lead, -1))

    def start2p(self):
        self.send("2p", self.group(1, self.half), self.rp.at[:, pl.ds(self.half, self.half), :], self.lead, 1)

    def start2m(self):
        self.send("2m", self.group(3, 0), self.rm.at[:, pl.ds(0, self.half), :], self.lead, -1)

    def load(self, dist, shift):
        g = lax.rem(self.me[self.lead] + dist, 4)

        def get(b, r):
            rows = pl.ds(self.row0 + shift + r, 64)
            return self.part[g, b, rows, :] if self.lead == 0 else self.part[b, g, rows, :]

        return get

    def start3(self):
        for key, buf, dist, shift, to in (("p", self.f1p, 1, 0, 1), ("m", self.f1m, 3, self.half, -1)):
            for copy in self.first[key]:
                copy.wait_recv()

            def put(b, r, v, buf=buf):
                buf[b, pl.ds(r, 64), :] = v

            add_into(put, [lambda b, r, buf=buf: buf[b, pl.ds(r, 64), :], self.load(dist, shift)], 4, self.half)
            land = self.rp if to == 1 else self.rm
            self.send("3" + key, buf, land.at[:, pl.ds(shift, self.half), :], self.lead, to)

    def finish1(self):
        for key in ("2p", "2m", "3p", "3m"):
            self.copies[key].wait_recv()

        def put(b, r, v):
            self.rp[b, pl.ds(r, 64), :] = v

        add_into(
            put,
            [lambda b, r: self.rp[b, pl.ds(r, 64), :], lambda b, r: self.rm[b, pl.ds(r, 64), :], self.load(0, 0)],
            4, 2 * self.half,
        )
        axis = 1 - self.lead
        at = lambda dist: lax.rem(self.me[axis] + dist, 4)
        top, low = pl.ds(0, self.half), pl.ds(self.half, self.half)
        self.send("4p", self.rp.at[at(2), top, :], self.f2p, axis, 1)
        self.send("4m", self.rp.at[at(2), low, :], self.f2m, axis, -1)
        self.send("5p", self.rp.at[at(1), low, :], self.r2p.at[low, :], axis, 1)
        self.send("5m", self.rp.at[at(3), top, :], self.r2m.at[top, :], axis, -1)

    def start6(self):
        axis = 1 - self.lead
        for key, buf, dist, shift, to in (("p", self.f2p, 1, 0, 1), ("m", self.f2m, 3, self.half, -1)):
            self.copies["4" + key].wait_recv()
            g = lax.rem(self.me[axis] + dist, 4)

            def put(b, r, v, buf=buf):
                buf[pl.ds(r, 64), :] = v

            add_into(
                put,
                [lambda b, r, buf=buf: buf[pl.ds(r, 64), :],
                 lambda b, r, g=g, shift=shift: self.rp[g, pl.ds(shift + r, 64), :]],
                1, self.half,
            )
            land = self.r2p if to == 1 else self.r2m
            self.send("6" + key, buf, land.at[pl.ds(shift, self.half), :], axis, to)

    def finish2(self):
        for key in ("5p", "5m", "6p", "6m"):
            self.copies[key].wait_recv()

    def total(self, r):
        g = self.me[1 - self.lead]
        return self.rp[g, pl.ds(r, 64), :] + self.r2p[pl.ds(r, 64), :] + self.r2m[pl.ds(r, 64), :]

    def drain(self):
        for copy in self.copies.values():
            copy.wait_send()


def invert(system):
    lane, row = iota((NEXP, 128), 1), iota((NEXP, 128), 0)
    work = jnp.concatenate([system, jnp.zeros((NEXP, 112), F32)], 1)
    work = work + jnp.where(lane == row + NEXP, 1.0, 0.0)
    for j in range(NEXP):
        pivot_row = work[j : j + 1, :] / work[j : j + 1, j : j + 1]
        factor = work[:, j : j + 1]
        work = jnp.where(row == j, pivot_row, work - factor * pivot_row)
    return work[:, NEXP : 2 * NEXP]


def moments(bins, me, band):
    image = jnp.concatenate([bins[:, 0, :], bins[:, 4, :], bins[:, 1, :], bins[:, 5, :]], 1)
    weight = jnp.concatenate([bins[:, 2, :], bins[:, 6, :], bins[:, 3, :], bins[:, 7, :]], 1)
    ws, ds = [], []
    for d in range(1, 9):
        other = pltpu.roll(weight, NEXP - d, 0)
        w = weight * other / (weight + other + 1.0)
        ws.append(w)
        ds.append(w * (image - pltpu.roll(image, NEXP - d, 0)))
    w, wd = jnp.concatenate(ws, 0), jnp.concatenate(ds, 0)

    def basis(rows, base):
        k, lane = iota((rows, 512), 0), iota((rows, 512), 1)
        y = center(BROWS * band + 2 * me + lane // 256, BCOLS)
        x = center(lane % 256, BCOLS)

        def pick(order, t):
            t2 = 2.0 * t * t - 1.0
            out = jnp.where(order == 0, 1.0, jnp.where(order == 1, t, t2))
            if base == 5:
                out = jnp.where(order == 3, 2.0 * t * t2 - t, out)
                out = jnp.where(order == 4, 2.0 * t2 * t2 - 1.0, out)
            return out

        return jnp.where(k < base * base, pick(k // base, y) * pick(k % base, x), 0.0)

    nt = (((1,), (1,)), ((), ()))
    gram = lax.dot_general(basis(32, 5), w, nt, precision=HIGH, preferred_element_type=F32)
    rhs = lax.dot_general(basis(16, 3), wd, nt, precision=HIGH, preferred_element_type=F32)
    return jnp.concatenate([gram[:25], rhs[:9], jnp.zeros((6, 128), F32)], 0)


def solve_lanes(mom):
    m = lambda a, b: mom[5 * a + b : 5 * a + b + 1, :]
    cache = {}

    def entry(k, l):
        u, v, s, t = k // 3, k % 3, l // 3, l % 3
        key = tuple(sorted(((u + s, v + t), (abs(u - s), v + t), (u + s, abs(v - t)), (abs(u - s), abs(v - t)))))
        if key not in cache:
            cache[key] = 0.25 * ((m(*key[0]) + m(*key[1])) + (m(*key[2]) + m(*key[3])))
        return cache[key]

    a = [[entry(k, l) for l in range(k + 1)] for k in range(9)]
    b = [mom[25 + k : 26 + k, :] for k in range(9)]
    inv = [None] * 9
    for j in range(9):
        inv[j] = 1.0 / a[j][j]
        for k in range(j + 1, 9):
            f = a[k][j] * inv[j]
            for l in range(j + 1, k + 1):
                a[k][l] = a[k][l] - f * a[l][j]
            b[k] = b[k] - f * b[j]
    out = [None] * 9
    for j in reversed(range(9)):
        total = b[j]
        for k in range(j + 1, 9):
            total = total - a[k][j] * out[k]
        out[j] = total * inv[j]
    return out


def early(n):
    other = lax.rem((n - 1) // 2 + 3, 4) - 2
    odd = lax.rem(n - 1, 2)
    return 2 + odd * other, 2 + (1 - odd) * other


def late(n):
    return lax.rem((n - 7) // 3 + 3, 4), lax.rem(lax.rem(n - 7, 3) + 3, 4)


NUM_SCRATCH = 20


def coadd_kernel(image_hbm, variance_hbm, mask_hbm, foot_hbm, owner_hbm, ch_hbm, cl_hbm, rh_hbm, rl_hbm,
                 coadd_ref, offsets_ref, *scratch):
    (img, wv, sv, mask_ref, foot_ref, owner_ref, ch_ref, cl_ref, rh_ref, rl_ref, up_ref, down_ref, xh, xl, tx_ref,
     ty_ref, blocks, sums, binned, bins_own), scratch = scratch[:NUM_SCRATCH], scratch[NUM_SCRATCH:]
    (bins, mom, sky_mom, exp_mom, offs, coefs), scratch = scratch[:6], scratch[6:]
    bufs, scratch = scratch[:48], scratch[48:]
    (small_sems, var_sems, img_sems, halo_s, halo_r, send_sems, recv_sems,
     bin_s, bin_r, sky_s, sky_r, exp_s, exp_r) = scratch
    me, band = lax.axis_index("exp"), lax.axis_index("sky")
    x, z = me // 4, lax.rem(me, 4)
    tall = ROWS + 2 * HALO

    barrier = pltpu.get_barrier_semaphore()
    for k in range(1, NEXP):
        pl.semaphore_signal(barrier, inc=1, device_id=(lax.rem(me + k, NEXP), band), device_id_type=MESH)
    for k in range(1, SKY):
        pl.semaphore_signal(barrier, inc=1, device_id=(me, lax.rem(band + k, SKY)), device_id_type=MESH)

    def place(rel):
        return lax.rem(x + rel[0], 4), lax.rem(z + rel[1], 4)

    def load_var(n, rel):
        cx, cz = place(rel)
        cols = pl.ds(pl.multiple_of(256 * (4 * cx + cz), 256), 256)
        return pltpu.make_async_copy(variance_hbm.at[0, :, cols], wv.at[cx, cz], var_sems.at[n])

    def load_img(n, rel):
        cx, cz = place(rel)
        cols = pl.ds(pl.multiple_of(256 * (4 * cx + cz), 256), 256)
        return pltpu.make_async_copy(image_hbm.at[0, :, cols], img.at[4 * cx + cz], img_sems.at[n])

    def each(fn, lo=0, hi=16):
        if lo == 0:
            fn(0, (2, 2))
        for first, last, rel in ((1, 7, early), (7, 16, late)):
            first, last = max(lo, first), min(hi, last)
            if first < last:

                def body(n, carry, rel=rel):
                    fn(n, rel(n))
                    return carry

                lax.fori_loop(first, last, body, 0)

    small = [
        pltpu.make_async_copy(src, dst, small_sems.at[n])
        for n, (src, dst) in enumerate((
            (mask_hbm.at[0], mask_ref), (foot_hbm, foot_ref), (owner_hbm, owner_ref),
            (ch_hbm, ch_ref), (cl_hbm, cl_ref), (rh_hbm, rh_ref), (rl_hbm, rl_ref),
        ))
    ]
    for copy in small[:2]:
        copy.start()
    each(lambda n, rel: load_var(n, rel).start())
    each(lambda n, rel: load_img(n, rel).start())
    for copy in small[2:]:
        copy.start()

    for copy in small[:2]:
        copy.wait()
    start = foot_ref[me]
    cell = iota((BROWS, BCOLS), 1)
    inside = (cell >= start) & (cell < start + FOOT_BINS)
    blocks[...] = jnp.where(inside, mask_ref[...].astype(F32), 0.0).astype(BF16)

    def onehot(m):
        hit = iota((256, 256), 0) == 16 * m + iota((256, 256), 1) // BIN
        return jnp.where(hit, 1.0, 0.0).astype(BF16)

    def weights(n, rel):
        load_var(n, rel).wait()
        cx, cz = place(rel)
        wide = jnp.dot(blocks[...], onehot(4 * cx + cz), preferred_element_type=F32)
        for r in range(4):
            rows = slice(128 * r, 128 * r + 128)
            keep = jnp.broadcast_to(wide[8 * r : 8 * r + 8][:, None, :], (8, BIN, 256)).reshape(128, 256)
            w = keep * (1.0 / wv[cx, cz, rows, :])
            wv[cx, cz, rows, :] = w
            sums[4 * cx + cz, 8 * r : 8 * r + 8, :] = jnp.sum(w.reshape(8, BIN, 256), axis=1)

    where = ((x, z), band)
    take = lambda n: bufs[8 * n : 8 * n + 8]
    sems = (send_sems, recv_sems)
    den = [Scatter(wv, h, 256 * h, 256, where, take(h), sems, 18 * h) for h in range(2)]
    num = [Scatter(sv, h, 256 * h + 128 * q, 128, where, take(2 + 2 * q + h), sems, 36 + 12 * (2 * q + h))
           for q in range(2) for h in range(2)]

    weights(0, (2, 2))
    pl.semaphore_wait(barrier, NEXP + SKY - 2)
    for part in den:
        part.start1_chunk(2)
    halos = []
    for n, (rows, dst, to) in enumerate(((ROWS - HALO, up_ref, band + 1), (0, down_ref, band + SKY - 1))):
        copy = pltpu.make_async_remote_copy(
            src_ref=image_hbm.at[0, pl.ds(rows, HALO), :], dst_ref=dst, send_sem=halo_s.at[n], recv_sem=halo_r.at[n],
            device_id=(me, lax.rem(to, SKY)), device_id_type=MESH,
        )
        copy.start()
        halos.append(copy)
    for t in range(3):
        dist = (3 + t) % 4
        weights(1 + 2 * t, (2, dist))
        den[0].start1_chunk(dist)
        weights(2 + 2 * t, (dist, 2))
        den[1].start1_chunk(dist)
    each(weights, 7, 16)

    def image_sums(n, rel):
        load_img(n, rel).wait()
        cx, cz = place(rel)
        m = 4 * cx + cz
        parts = []
        for r in range(4):
            parts.append(jnp.sum(img[m, 128 * r : 128 * r + 128, :].reshape(8, BIN, 256), axis=1))
        both = jnp.concatenate([jnp.concatenate(parts, 0) * (1.0 / (BIN * BIN)), sums[m]], 0)
        high = both.astype(BF16)
        rest = both - high.astype(F32)
        mid = rest.astype(BF16)
        low = (rest - mid.astype(F32)).astype(BF16)
        got = lax.dot_general(
            jnp.concatenate([high, mid, low], 0), onehot(m), (((1,), (1,)), ((), ())), preferred_element_type=F32
        )
        binned[...] = binned[...] + (got[:64] + got[64:128] + got[128:])

    binned[...] = jnp.zeros((64, BCOLS), F32)
    each(image_sums)
    for m in range(NEXP):
        tile = jnp.concatenate([binned[2 * m : 2 * m + 2, :], binned[32 + 2 * m : 34 + 2 * m, :]], 0)
        bins_own[m] = jnp.concatenate([tile[:, :128], tile[:, 128:]], 0)
    bin_copies = []
    for k in range(1, NEXP):
        to = lax.rem(me + k, NEXP)
        copy = pltpu.make_async_remote_copy(
            src_ref=bins_own.at[to], dst_ref=bins.at[me], send_sem=bin_s.at[k], recv_sem=bin_r.at[k],
            device_id=(to, band), device_id_type=MESH,
        )
        copy.start()
        bin_copies.append(copy)
    bins[me] = bins_own[me]
    for part in den:
        part.start2p()
        part.start2m()

    for copy in small[2:]:
        copy.wait()
    for copy in halos:
        copy.wait_recv()

    def put(j, first, lane0, value):
        rows, width = value.shape
        col = 256 * j - 128 + lane0 + iota((1, width), 1)
        keep = (col >= BIN * start) & (col < BIN * (start + FOOT_BINS))
        high, low = split(jnp.where(keep, value, 0.0))
        xh[first : first + rows, lane0 : lane0 + width] = high
        xl[first : first + rows, lane0 : lane0 + width] = low

    def row_pass(value, out):
        high, low = split(value)
        for i in range(ROWS // 128):
            zh, zl = high[128 * i : 128 * i + 160], low[128 * i : 128 * i + 160]
            out(
                128 * i,
                jnp.dot(rh_ref[...], zh, preferred_element_type=F32)
                + jnp.dot(rl_ref[...], zh, preferred_element_type=F32)
                + jnp.dot(rh_ref[...], zl, preferred_element_type=F32),
            )

    def smooth(n, rel):
        cx, cz = place(rel)
        j = 4 * cx + cz
        before, after = jnp.maximum(j - 1, 0), jnp.minimum(j + 1, 15)
        lo = pl.multiple_of(jnp.maximum(256 * j - 128, 0), 128)
        mid = pl.multiple_of(256 * j, 128)
        hi = pl.multiple_of(jnp.minimum(256 * j + 256, COLS - 128), 128)
        for first, ref, known in ((0, up_ref, band > 0), (HALO + ROWS, down_ref, band < SKY - 1)):
            put(j, first, 0, jnp.where(known, ref[:, pl.ds(lo, 128)], 0.0))
            put(j, first, 128, jnp.where(known, ref[:, pl.ds(mid, 256)], 0.0))
            put(j, first, 384, jnp.where(known, ref[:, pl.ds(hi, 128)], 0.0))
        put(j, HALO, 0, img[before, :, 128:256])
        put(j, HALO, 128, img[j])
        put(j, HALO, 384, img[after, :, 0:128])
        xcol = center(256 * j - 128 + iota((16, 512), 1), COLS)
        order = iota((16, 512), 0)
        put(j, tall, 0, jnp.where(order == 0, 1.0, jnp.where(order == 1, xcol, 2.0 * xcol * xcol - 1.0)))
        across = (
            jnp.dot(xh[...], ch_ref[...], preferred_element_type=F32)
            + jnp.dot(xl[...], ch_ref[...], preferred_element_type=F32)
            + jnp.dot(xh[...], cl_ref[...], preferred_element_type=F32)
        )
        tx_ref[j] = across[tall : tall + 8]

        def out(r, part):
            sv[cx, cz, r : r + 128, :] = part

        row_pass(across[:tall], out)

    owner = owner_ref[...].astype(F32)
    both = owner + owner.T
    eye = iota((NEXP, NEXP), 0) == iota((NEXP, NEXP), 1)
    degree = jnp.sum(both, axis=1, keepdims=True) + LAMBDA_REG
    inverse = invert(jnp.where(eye, degree, 0.0) - both)
    lane, row = iota((NEXP, 128), 1), iota((NEXP, 128), 0)
    first = lax.rem(lane, NEXP)
    shift = lane // NEXP + 1
    second = lax.rem(first + shift, NEXP)
    at_first, at_second = row == first, row == second
    partner = jnp.dot(both, jnp.where(at_second, 1.0, 0.0), precision=HIGH, preferred_element_type=F32)
    used = jnp.sum(jnp.where(at_first, partner, 0.0), axis=0, keepdims=True)
    used = jnp.where((shift[:1] == 8) & (first[:1] >= 8), 0.0, used)
    sign = jnp.where(at_first, 1.0, 0.0) - jnp.where(at_second, 1.0, 0.0)

    each(smooth, 0, 2)
    for copy in bin_copies:
        copy.wait_recv()
    own = moments(bins, me, band)
    mom[0] = own
    sky_mom[band] = own
    sky_copies = []
    for k in range(1, SKY):
        copy = pltpu.make_async_remote_copy(
            src_ref=mom.at[0], dst_ref=sky_mom.at[band], send_sem=sky_s.at[k], recv_sem=sky_r.at[k],
            device_id=(me, lax.rem(band + k, SKY)), device_id_type=MESH,
        )
        copy.start()
        sky_copies.append(copy)
    ty_row = band * ROWS - HALO + iota((tall, 128), 0)
    y = center(ty_row, ROWS * SKY)
    known = (ty_row >= 0) & (ty_row < ROWS * SKY)
    for u in range(3):

        def out(r, part, u=u):
            ty_ref[u, r : r + 128, :] = part

        row_pass(jnp.where(known, cheb(u, y), 0.0), out)
    each(smooth, 2, 4)
    for copy in sky_copies:
        copy.wait_recv()
    total = sky_mom[0]
    for k in range(1, SKY):
        total = total + sky_mom[k]
    mom[1] = total
    exp_mom[me] = total
    exp_copies = []
    for k in range(1, NEXP):
        copy = pltpu.make_async_remote_copy(
            src_ref=mom.at[1], dst_ref=exp_mom.at[me], send_sem=exp_s.at[k], recv_sem=exp_r.at[k],
            device_id=(lax.rem(me + k, NEXP), band), device_id_type=MESH,
        )
        copy.start()
        exp_copies.append(copy)
    for part in den:
        part.start3()
    each(smooth, 4, 8)
    for copy in exp_copies:
        copy.wait_recv()
    total = exp_mom[0]
    for k in range(1, NEXP):
        total = total + exp_mom[k]
    fits = jnp.concatenate(solve_lanes(total) + [jnp.zeros((7, 128), F32)], 0)
    fits = jnp.where(used > 0.0, fits, 0.0)
    nt = (((1,), (1,)), ((), ()))
    right = lax.dot_general(sign, fits, nt, precision=HIGH, preferred_element_type=F32)
    answer = jnp.dot(inverse, right, precision=HIGH, preferred_element_type=F32)
    offsets_ref[...] = answer[:, :9]
    offs[:, 0:NEXP] = answer
    coef = offs[pl.ds(me, 1), :]
    for k in range(9):
        coefs[k : k + 1, :] = jnp.broadcast_to(coef[:, k : k + 1], (1, 256))

    def numerator(half, dist):
        g = lax.rem((x, z)[half] + dist, 4)

        def chunk(b, carry):
            cx, cz = (g, b) if half == 0 else (b, g)
            tx = tx_ref[4 * cx + cz]
            lines = []
            for u in range(3):
                line = coefs[3 * u : 3 * u + 1, :] * tx[0:1]
                for v in range(1, 3):
                    line = line + coefs[3 * u + v : 3 * u + v + 1, :] * tx[v : v + 1]
                lines.append(line)
            for i in range(4):
                rows = slice(256 * half + 64 * i, 256 * half + 64 * i + 64)
                back = None
                for u in range(3):
                    ty = ty_ref[u, rows, :]
                    term = jnp.concatenate([ty, ty], 1) * lines[u]
                    back = term if back is None else back + term
                sv[cx, cz, rows, :] = wv[cx, cz, rows, :] * (sv[cx, cz, rows, :] - back)
            return carry

        lax.fori_loop(0, 4, chunk, 0)

    for half in range(2):
        numerator(half, 2)
        num[half].start1()
    for part in num[2:]:
        part.start1()
    each(smooth, 8, 16)
    for half in range(2):
        numerator(half, 1)
        num[half].start2p()
        numerator(half, 3)
        num[half].start2m()
    for part in num[2:]:
        part.start2p()
        part.start2m()
    for part in den:
        part.finish1()
    for part in num[:2]:
        part.start3()
    for half in range(2):
        numerator(half, 0)
    for part in num[2:]:
        part.start3()
    for part in den:
        part.start6()
    for part in num[:2]:
        part.finish1()
    for part in den:
        part.finish2()
    for part in num[:2]:
        part.start6()
    for part in num[2:]:
        part.finish1()
    for part in num[2:]:
        part.start6()

    def finish(n):
        part = num[n]
        part.finish2()
        h, q = n % 2, n // 2

        def body(i, carry):
            r = pl.multiple_of(i * 64, 64)
            value = part.total(r) / (PRIOR + den[h].total(128 * q + r))
            coadd_ref[pl.ds(256 * h + 128 * q + r, 64), :] = value
            return carry

        lax.fori_loop(0, 2, body, 0)

    for n in range(4):
        finish(n)
    for copy in halos + bin_copies + sky_copies + exp_copies:
        copy.wait_send()
    for part in den + num:
        part.drain()


def per_device(image, variance, mask, foot_start, pair_owner):
    k, n = np.arange(512)[:, None], np.arange(256)[None, :]
    ch, cl = taps_matrix(k - n - 128)
    k, n = np.arange(160)[None, :], np.arange(128)[:, None]
    rh, rl = taps_matrix(k - n - HALO)
    big = lambda *shape: pltpu.VMEM(shape, F32)
    half = lambda *shape: pltpu.VMEM(shape, BF16)
    pieces = lambda r: [big(4, r // 2, 256), big(4, r // 2, 256), big(4, r, 256), big(4, r, 256),
                        big(r // 2, 256), big(r // 2, 256), big(r, 256), big(r, 256)]
    dma = lambda n: pltpu.SemaphoreType.DMA((n,))
    vmem = pl.BlockSpec(memory_space=pltpu.VMEM)
    tall = ROWS + 2 * HALO
    held = [
        big(16, ROWS, 256), big(4, 4, ROWS, 256), big(4, 4, ROWS, 256),
        pltpu.VMEM((BROWS, BCOLS), jnp.int32), pltpu.SMEM((NEXP,), jnp.int32), pltpu.VMEM((NEXP, NEXP), jnp.int32),
        half(512, 256), half(512, 256), half(128, 160), half(128, 160), big(HALO, COLS), big(HALO, COLS),
        half(tall + 16, 512), half(tall + 16, 512), big(16, 8, 256), big(3, ROWS, 128), half(BROWS, BCOLS),
        big(16, BROWS, 256), big(64, BCOLS), big(NEXP, 8, 128),
    ]
    fit = [big(NEXP, 8, 128), big(2, 40, 128), big(SKY, 40, 128), big(NEXP, 40, 128), big(NEXP, 128), big(16, 256)]
    sems = [dma(7), dma(16), dma(16), dma(2), dma(2), dma(84), dma(84), dma(NEXP), dma(NEXP), dma(SKY), dma(SKY),
            dma(NEXP), dma(NEXP)]
    return tuple(pl.pallas_call(
        coadd_kernel,
        in_specs=[pl.BlockSpec(memory_space=pltpu.HBM)] * 9,
        out_specs=[vmem, vmem],
        out_shape=[jax.ShapeDtypeStruct((ROWS, 256), F32), jax.ShapeDtypeStruct((NEXP, 9), F32)],
        scratch_shapes=held + fit + pieces(256) * 2 + pieces(128) * 4 + sems,
        compiler_params=pltpu.CompilerParams(collective_id=0, has_side_effects=True, vmem_limit_bytes=48 << 20),
        name="coadd",
    )(*(pltpu.with_memory_space_constraint(a, pltpu.HBM)
        for a in (image, variance, mask, foot_start, pair_owner, ch, cl, rh, rl))))


def solution(mesh):
    placed = (P("exp", "sky", None), P("exp", "sky", None), P("exp", "sky", None), P(), P())
    return jax.shard_map(
        per_device, mesh=mesh, in_specs=placed, out_specs=(P("sky", "exp"), P()), check_vma=False
    )
```

```python
import functools

import jax
import jax.numpy as jnp
import numpy as np
from jax import lax
from jax.experimental import pallas as pl
from jax.experimental.pallas import tpu as pltpu
from jax.sharding import PartitionSpec as P

F32 = jnp.float32
BF16 = jnp.bfloat16
HIGH = lax.Precision.HIGHEST
MESH = pl.DeviceIdType.MESH
BIN = 16
RADIUS = 10
NEXP = 16
ROWS = 512
COLS = 4096
SKY = 8
BROWS = 32
BCOLS = 256
FOOT_BINS = 192
HALO = 16
LAMBDA_REG = 0.25
DEN_ROWS = (240, 272)
NUM_ROWS = (224, 288)
PRIOR = 1.0


def iota(shape, dim):
    return lax.broadcasted_iota(jnp.int32, shape, dim)


def center(index, total):
    return (2.0 * index.astype(F32) + 1.0) / total - 1.0


def cheb(order, t):
    if order == 0:
        return jnp.ones_like(t)
    if order == 1:
        return t
    return 2.0 * t * t - 1.0


def split(value):
    high = value.astype(BF16)
    return high, (value - high.astype(F32)).astype(BF16)


def taps_matrix(offset):
    total = np.sum(np.exp(-(np.arange(-RADIUS, RADIUS + 1) ** 2) / 50.0))
    exact = np.where(np.abs(offset) <= RADIUS, np.exp(-(offset**2) / 50.0) / total, 0.0)
    high = exact.astype(BF16)
    return jnp.asarray(high), jnp.asarray((exact - high.astype(np.float64)).astype(BF16))


class Scatter:
    def __init__(self, part, lead, row0, rows, place, foot, bufs, sems, packed):
        self.part, self.lead, self.row0, self.half = part, lead, row0, rows // 2
        self.me, self.sky, self.foot = place[0], place[1], foot
        (self.f1p, self.f1m, self.rp, self.rm, self.f2p, self.f2m, self.r2p, self.r2m), rest = bufs[:8], bufs[8:]
        self.packs, self.lands = rest or (None, None)
        self.send_sems, self.recv_sems, self.counter = sems
        self.packed = packed
        self.copies = {}
        self.first = {"p": [], "m": []}
        self.second = []

    def device(self, axis, shift):
        x, z = self.me
        if axis == 0:
            x = lax.rem(x + shift + 4, 4)
        else:
            z = lax.rem(z + shift + 4, 4)
        return (4 * x + z, self.sky)

    def to(self, dist):
        return lax.rem(self.me[self.lead] + dist, 4)

    def group(self, dist, r, chunks=(0, 4)):
        rows = pl.ds(self.row0 + r, self.half)
        some = pl.ds(*chunks)
        g = self.to(dist)
        return self.part.at[g, some, rows, :] if self.lead == 0 else self.part.at[some, g, rows, :]

    def own(self, b, dist, r):
        rows = pl.ds(self.row0 + r, self.half)
        g = self.to(dist)
        return self.part[g, b, rows, :] if self.lead == 0 else self.part[b, g, rows, :]

    def send(self, key, src, dst, axis, shift):
        n = self.counter[0]
        self.counter[0] += 1
        copy = pltpu.make_async_remote_copy(
            src_ref=src, dst_ref=dst, send_sem=self.send_sems.at[n], recv_sem=self.recv_sems.at[n],
            device_id=self.device(axis, shift), device_id_type=MESH,
        )
        copy.start()
        self.copies[key] = copy
        return copy

    def send_group(self, key, packed, slot, dist, r, land, to):
        if not packed:
            return [self.send(key, self.group(dist, r), land, self.lead, to)]
        raw = self.send(key, self.group(dist, r, (1, 2)), land.at[pl.ds(1, 2)], self.lead, to)
        self.packs[slot] = self.own(0, dist, r) + self.own(3, dist, r)
        return [raw, self.send(key + "s", self.packs.at[slot], self.lands.at[slot], self.lead, to)]

    def apart(self, slot, b):
        sender = self.foot[self.device(1, -1 if slot in (0, 2) else 1)[0]]
        g = self.to({0: 1, 1: 3, 2: 0, 3: 0}[slot])
        low = 256 * g + iota((1, 256), 1) >= BIN * sender
        return jnp.where(low if b == 0 else jnp.logical_not(low), self.lands[slot], 0.0)

    def start1(self):
        h = self.half
        self.first["p"] += self.send_group("1p", self.packed[0], 0, 2, 0, self.f1p, 1)
        self.first["m"] += self.send_group("1m", self.packed[0], 1, 2, h, self.f1m, -1)

    def start1_chunk(self, dist):
        b = lax.rem(self.me[1 - self.lead] + dist, 4)
        key = str(dist)
        self.first["p"].append(self.send("1p" + key, self.group(2, 0).at[b], self.f1p.at[b], self.lead, 1))
        self.first["m"].append(self.send("1m" + key, self.group(2, self.half).at[b], self.f1m.at[b], self.lead, -1))

    def start2(self):
        h = self.half
        self.second += self.send_group("2p", self.packed[1], 2, 1, h, self.rp.at[:, pl.ds(h, h), :], 1)
        self.second += self.send_group("2m", self.packed[1], 3, 3, 0, self.rm.at[:, pl.ds(0, h), :], -1)

    def start3(self):
        h = self.half
        for key, buf, dist, shift, land, slot, to in (
            ("p", self.f1p, 1, 0, self.rp, 0, 1), ("m", self.f1m, 3, h, self.rm, 1, -1)
        ):
            for copy in self.first[key]:
                copy.wait_recv()

            def body(b, carry, buf=buf, dist=dist, shift=shift):
                buf[b] = buf[b] + self.own(b, dist, shift)
                return carry

            if self.packed[0]:
                for b in (0, 3):
                    buf[b] = self.apart(slot, b) + self.own(b, dist, shift)
                lax.fori_loop(1, 3, body, 0)
            else:
                lax.fori_loop(0, 4, body, 0)
            self.send("3" + key, buf, land.at[:, pl.ds(shift, h), :], self.lead, to)

    def finish1(self):
        h = self.half
        top, low = pl.ds(0, h), pl.ds(h, h)
        for copy in self.second + [self.copies["3p"], self.copies["3m"]]:
            copy.wait_recv()

        def body(b, carry):
            for shift in (0, h):
                rows = pl.ds(shift, h)
                self.rp[b, rows, :] = self.rp[b, rows, :] + self.rm[b, rows, :] + self.own(b, 0, shift)
            return carry

        if self.packed[1]:
            for b in (0, 3):
                self.rp[b, top, :] = self.rp[b, top, :] + self.apart(3, b) + self.own(b, 0, 0)
                self.rp[b, low, :] = self.apart(2, b) + self.rm[b, low, :] + self.own(b, 0, h)
            lax.fori_loop(1, 3, body, 0)
        else:
            lax.fori_loop(0, 4, body, 0)
        axis = 1 - self.lead
        at = lambda dist: lax.rem(self.me[axis] + dist, 4)
        self.send("4p", self.rp.at[at(2), top, :], self.f2p, axis, 1)
        self.send("4m", self.rp.at[at(2), low, :], self.f2m, axis, -1)
        self.send("5p", self.rp.at[at(1), low, :], self.r2p.at[low, :], axis, 1)
        self.send("5m", self.rp.at[at(3), top, :], self.r2m.at[top, :], axis, -1)

    def start6(self):
        axis = 1 - self.lead
        for key, buf, dist, shift, land, to in (
            ("p", self.f2p, 1, 0, self.r2p, 1), ("m", self.f2m, 3, self.half, self.r2m, -1)
        ):
            self.copies["4" + key].wait_recv()
            g = lax.rem(self.me[axis] + dist, 4)
            rows = pl.ds(shift, self.half)
            buf[...] = buf[...] + self.rp[g, rows, :]
            self.send("6" + key, buf, land.at[rows, :], axis, to)

    def finish2(self):
        for key in ("5p", "5m", "6p", "6m"):
            self.copies[key].wait_recv()
        g = self.me[1 - self.lead]
        return self.rp[g] + self.r2p[...] + self.r2m[...]

    def drain(self):
        for copy in self.copies.values():
            copy.wait_send()


def invert(system):
    lane, row = iota((NEXP, 128), 1), iota((NEXP, 128), 0)
    work = jnp.concatenate([system, jnp.zeros((NEXP, 112), F32)], 1)
    work = work + jnp.where(lane == row + NEXP, 1.0, 0.0)
    for j in range(NEXP):
        pivot_row = work[j : j + 1, :] / work[j : j + 1, j : j + 1]
        factor = work[:, j : j + 1]
        work = jnp.where(row == j, pivot_row, work - factor * pivot_row)
    return work[:, NEXP : 2 * NEXP]


def moments(bins, me, band):
    image = jnp.concatenate([bins[:, 0, :], bins[:, 4, :], bins[:, 1, :], bins[:, 5, :]], 1)
    weight = jnp.concatenate([bins[:, 2, :], bins[:, 6, :], bins[:, 3, :], bins[:, 7, :]], 1)
    ws, ds = [], []
    for d in range(1, 9):
        other = pltpu.roll(weight, NEXP - d, 0)
        w = weight * other / (weight + other + 1.0)
        ws.append(w)
        ds.append(w * (image - pltpu.roll(image, NEXP - d, 0)))
    w, wd = jnp.concatenate(ws, 0), jnp.concatenate(ds, 0)

    def basis(rows, base):
        k, lane = iota((rows, 512), 0), iota((rows, 512), 1)
        y = center(BROWS * band + 2 * me + lane // 256, BCOLS)
        x = center(lane % 256, BCOLS)

        def pick(order, t):
            t2 = 2.0 * t * t - 1.0
            out = jnp.where(order == 0, 1.0, jnp.where(order == 1, t, t2))
            if base == 5:
                out = jnp.where(order == 3, 2.0 * t * t2 - t, out)
                out = jnp.where(order == 4, 2.0 * t2 * t2 - 1.0, out)
            return out

        return jnp.where(k < base * base, pick(k // base, y) * pick(k % base, x), 0.0)

    nt = (((1,), (1,)), ((), ()))
    gram = lax.dot_general(basis(32, 5), w, nt, precision=HIGH, preferred_element_type=F32)
    rhs = lax.dot_general(basis(16, 3), wd, nt, precision=HIGH, preferred_element_type=F32)
    return jnp.concatenate([gram[:25], rhs[:9], jnp.zeros((6, 128), F32)], 0)


def solve_lanes(mom):
    m = lambda a, b: mom[5 * a + b : 5 * a + b + 1, :]
    cache = {}

    def entry(k, l):
        u, v, s, t = k // 3, k % 3, l // 3, l % 3
        key = tuple(sorted(((u + s, v + t), (abs(u - s), v + t), (u + s, abs(v - t)), (abs(u - s), abs(v - t)))))
        if key not in cache:
            cache[key] = 0.25 * ((m(*key[0]) + m(*key[1])) + (m(*key[2]) + m(*key[3])))
        return cache[key]

    a = [[entry(k, l) for l in range(k + 1)] for k in range(9)]
    b = [mom[25 + k : 26 + k, :] for k in range(9)]
    inv = [None] * 9
    for j in range(9):
        inv[j] = 1.0 / a[j][j]
        for k in range(j + 1, 9):
            f = a[k][j] * inv[j]
            for l in range(j + 1, k + 1):
                a[k][l] = a[k][l] - f * a[l][j]
            b[k] = b[k] - f * b[j]
    out = [None] * 9
    for j in reversed(range(9)):
        total = b[j]
        for k in range(j + 1, 9):
            total = total - a[k][j] * out[k]
        out[j] = total * inv[j]
    return out


def early(n):
    other = lax.rem((n - 1) // 2 + 3, 4) - 2
    odd = lax.rem(n - 1, 2)
    return 2 + odd * other, 2 + (1 - odd) * other


def late(n):
    return lax.rem((n - 7) // 3 + 3, 4), lax.rem(lax.rem(n - 7, 3) + 3, 4)


NUM_SCRATCH = 20


def coadd_kernel(image_hbm, variance_hbm, mask_hbm, foot_hbm, owner_hbm, ch_hbm, cl_hbm, rh_hbm, rl_hbm,
                 coadd_ref, offsets_ref, *scratch):
    (img, wv, sv, mask_ref, foot_ref, owner_ref, ch_ref, cl_ref, rh_ref, rl_ref, up_ref, down_ref, xh, xl, tx_ref,
     ty_ref, blocks, sums, binned, bins_own), scratch = scratch[:NUM_SCRATCH], scratch[NUM_SCRATCH:]
    (bins, mom, sky_mom, exp_mom, offs, coefs, total_den), scratch = scratch[:7], scratch[7:]
    bufs, scratch = scratch[:54], scratch[54:]
    (small_sems, var_sems, img_sems, halo_s, halo_r, send_sems, recv_sems,
     bin_s, bin_r, sky_s, sky_r, exp_s, exp_r) = scratch
    me, band = lax.axis_index("exp"), lax.axis_index("sky")
    x, z = me // 4, lax.rem(me, 4)
    tall = ROWS + 2 * HALO

    barrier = pltpu.get_barrier_semaphore()
    for k in range(1, NEXP):
        pl.semaphore_signal(barrier, inc=1, device_id=(lax.rem(me + k, NEXP), band), device_id_type=MESH)
    for k in range(1, SKY):
        pl.semaphore_signal(barrier, inc=1, device_id=(me, lax.rem(band + k, SKY)), device_id_type=MESH)

    def place(rel):
        return lax.rem(x + rel[0], 4), lax.rem(z + rel[1], 4)

    def load_var(n, rel):
        cx, cz = place(rel)
        cols = pl.ds(pl.multiple_of(256 * (4 * cx + cz), 256), 256)
        return pltpu.make_async_copy(variance_hbm.at[0, :, cols], wv.at[cx, cz], var_sems.at[n])

    def load_img(n, rel):
        cx, cz = place(rel)
        cols = pl.ds(pl.multiple_of(256 * (4 * cx + cz), 256), 256)
        return pltpu.make_async_copy(image_hbm.at[0, :, cols], img.at[4 * cx + cz], img_sems.at[n])

    def each(fn, lo=0, hi=16):
        if lo == 0:
            fn(0, (2, 2))
        for first, last, rel in ((1, 7, early), (7, 16, late)):
            first, last = max(lo, first), min(hi, last)
            if first < last:

                def body(n, carry, rel=rel):
                    fn(n, rel(n))
                    return carry

                lax.fori_loop(first, last, body, 0)

    small = [
        pltpu.make_async_copy(src, dst, small_sems.at[n])
        for n, (src, dst) in enumerate((
            (mask_hbm.at[0], mask_ref), (foot_hbm, foot_ref), (owner_hbm, owner_ref),
            (ch_hbm, ch_ref), (cl_hbm, cl_ref), (rh_hbm, rh_ref), (rl_hbm, rl_ref),
        ))
    ]
    for copy in small[:2]:
        copy.start()
    each(lambda n, rel: load_var(n, rel).start())
    each(lambda n, rel: load_img(n, rel).start())
    for copy in small[2:]:
        copy.start()

    for copy in small[:2]:
        copy.wait()
    start = foot_ref[me]
    cell = iota((BROWS, BCOLS), 1)
    inside = (cell >= start) & (cell < start + FOOT_BINS)
    blocks[...] = jnp.where(inside, mask_ref[...].astype(F32), 0.0).astype(BF16)

    def onehot(m):
        hit = iota((256, 256), 0) == 16 * m + iota((256, 256), 1) // BIN
        return jnp.where(hit, 1.0, 0.0).astype(BF16)

    def weights(n, rel):
        load_var(n, rel).wait()
        cx, cz = place(rel)
        wide = jnp.dot(blocks[...], onehot(4 * cx + cz), preferred_element_type=F32)
        for r in range(4):
            rows = slice(128 * r, 128 * r + 128)
            keep = jnp.broadcast_to(wide[8 * r : 8 * r + 8][:, None, :], (8, BIN, 256)).reshape(128, 256)
            w = keep * (1.0 / wv[cx, cz, rows, :])
            wv[cx, cz, rows, :] = w
            sums[4 * cx + cz, 8 * r : 8 * r + 8, :] = jnp.sum(w.reshape(8, BIN, 256), axis=1)

    where = ((x, z), band)
    take = lambda n: bufs[18 * (n // 2) : 18 * (n // 2) + 8] if n % 2 == 0 else bufs[18 * (n // 2) + 8 : 18 * (n // 2) + 18]
    sems = (send_sems, recv_sems, [0])
    den = [Scatter(wv, h, DEN_ROWS[0] * h, DEN_ROWS[h], where, foot_ref, take(h), sems, (False, h == 1)) for h in range(2)]
    num = [
        Scatter(sv, h, NUM_ROWS[0] * h + NUM_ROWS[h] // 2 * q, NUM_ROWS[h] // 2, where, foot_ref, take(2 + 2 * q + h),
                sems, (h == 1, h == 1))
        for q in range(2) for h in range(2)
    ]

    weights(0, (2, 2))
    pl.semaphore_wait(barrier, NEXP + SKY - 2)
    for part in den:
        part.start1_chunk(2)
    halos = []
    for n, (rows, dst, to) in enumerate(((ROWS - HALO, up_ref, band + 1), (0, down_ref, band + SKY - 1))):
        copy = pltpu.make_async_remote_copy(
            src_ref=image_hbm.at[0, pl.ds(rows, HALO), :], dst_ref=dst, send_sem=halo_s.at[n], recv_sem=halo_r.at[n],
            device_id=(me, lax.rem(to, SKY)), device_id_type=MESH,
        )
        copy.start()
        halos.append(copy)
    for t in range(3):
        dist = (3 + t) % 4
        weights(1 + 2 * t, (2, dist))
        den[0].start1_chunk(dist)
        weights(2 + 2 * t, (dist, 2))
        den[1].start1_chunk(dist)
    each(weights, 7, 16)

    def image_sums(n, rel):
        load_img(n, rel).wait()
        cx, cz = place(rel)
        m = 4 * cx + cz
        parts = []
        for r in range(4):
            parts.append(jnp.sum(img[m, 128 * r : 128 * r + 128, :].reshape(8, BIN, 256), axis=1))
        both = jnp.concatenate([jnp.concatenate(parts, 0) * (1.0 / (BIN * BIN)), sums[m]], 0)
        high = both.astype(BF16)
        rest = both - high.astype(F32)
        mid = rest.astype(BF16)
        low = (rest - mid.astype(F32)).astype(BF16)
        got = lax.dot_general(
            jnp.concatenate([high, mid, low], 0), onehot(m), (((1,), (1,)), ((), ())), preferred_element_type=F32
        )
        binned[...] = binned[...] + (got[:64] + got[64:128] + got[128:])

    binned[...] = jnp.zeros((64, BCOLS), F32)
    each(image_sums)
    for m in range(NEXP):
        tile = jnp.concatenate([binned[2 * m : 2 * m + 2, :], binned[32 + 2 * m : 34 + 2 * m, :]], 0)
        bins_own[m] = jnp.concatenate([tile[:, :128], tile[:, 128:]], 0)
    bin_copies = []
    for k in range(1, NEXP):
        to = lax.rem(me + k, NEXP)
        copy = pltpu.make_async_remote_copy(
            src_ref=bins_own.at[to], dst_ref=bins.at[me], send_sem=bin_s.at[k], recv_sem=bin_r.at[k],
            device_id=(to, band), device_id_type=MESH,
        )
        copy.start()
        bin_copies.append(copy)
    bins[me] = bins_own[me]
    for part in den:
        part.start2()

    for copy in small[2:]:
        copy.wait()
    for copy in halos:
        copy.wait_recv()

    def put(j, first, lane0, value):
        rows, width = value.shape
        col = 256 * j - 128 + lane0 + iota((1, width), 1)
        keep = (col >= BIN * start) & (col < BIN * (start + FOOT_BINS))
        high, low = split(jnp.where(keep, value, 0.0))
        xh[first : first + rows, lane0 : lane0 + width] = high
        xl[first : first + rows, lane0 : lane0 + width] = low

    def row_pass(value, out):
        high, low = split(value)
        for i in range(ROWS // 128):
            zh, zl = high[128 * i : 128 * i + 160], low[128 * i : 128 * i + 160]
            out(
                128 * i,
                jnp.dot(rh_ref[...], zh, preferred_element_type=F32)
                + jnp.dot(rl_ref[...], zh, preferred_element_type=F32)
                + jnp.dot(rh_ref[...], zl, preferred_element_type=F32),
            )

    def smooth(n, rel):
        cx, cz = place(rel)
        j = 4 * cx + cz
        before, after = jnp.maximum(j - 1, 0), jnp.minimum(j + 1, 15)
        lo = pl.multiple_of(jnp.maximum(256 * j - 128, 0), 128)
        mid = pl.multiple_of(256 * j, 128)
        hi = pl.multiple_of(jnp.minimum(256 * j + 256, COLS - 128), 128)
        for first, ref, known in ((0, up_ref, band > 0), (HALO + ROWS, down_ref, band < SKY - 1)):
            put(j, first, 0, jnp.where(known, ref[:, pl.ds(lo, 128)], 0.0))
            put(j, first, 128, jnp.where(known, ref[:, pl.ds(mid, 256)], 0.0))
            put(j, first, 384, jnp.where(known, ref[:, pl.ds(hi, 128)], 0.0))
        put(j, HALO, 0, img[before, :, 128:256])
        put(j, HALO, 128, img[j])
        put(j, HALO, 384, img[after, :, 0:128])
        xcol = center(256 * j - 128 + iota((16, 512), 1), COLS)
        order = iota((16, 512), 0)
        put(j, tall, 0, jnp.where(order == 0, 1.0, jnp.where(order == 1, xcol, 2.0 * xcol * xcol - 1.0)))
        across = (
            jnp.dot(xh[...], ch_ref[...], preferred_element_type=F32)
            + jnp.dot(xl[...], ch_ref[...], preferred_element_type=F32)
            + jnp.dot(xh[...], cl_ref[...], preferred_element_type=F32)
        )
        tx_ref[j] = across[tall : tall + 8]

        def out(r, part):
            sv[cx, cz, r : r + 128, :] = part

        row_pass(across[:tall], out)

    owner = owner_ref[...].astype(F32)
    both = owner + owner.T
    eye = iota((NEXP, NEXP), 0) == iota((NEXP, NEXP), 1)
    degree = jnp.sum(both, axis=1, keepdims=True) + LAMBDA_REG
    inverse = invert(jnp.where(eye, degree, 0.0) - both)
    lane, row = iota((NEXP, 128), 1), iota((NEXP, 128), 0)
    first = lax.rem(lane, NEXP)
    shift = lane // NEXP + 1
    second = lax.rem(first + shift, NEXP)
    at_first, at_second = row == first, row == second
    partner = jnp.dot(both, jnp.where(at_second, 1.0, 0.0), precision=HIGH, preferred_element_type=F32)
    used = jnp.sum(jnp.where(at_first, partner, 0.0), axis=0, keepdims=True)
    used = jnp.where((shift[:1] == 8) & (first[:1] >= 8), 0.0, used)
    sign = jnp.where(at_first, 1.0, 0.0) - jnp.where(at_second, 1.0, 0.0)

    each(smooth, 0, 2)
    for copy in bin_copies:
        copy.wait_recv()
    own = moments(bins, me, band)
    mom[0] = own
    sky_mom[band] = own
    sky_copies = []
    for k in range(1, SKY):
        copy = pltpu.make_async_remote_copy(
            src_ref=mom.at[0], dst_ref=sky_mom.at[band], send_sem=sky_s.at[k], recv_sem=sky_r.at[k],
            device_id=(me, lax.rem(band + k, SKY)), device_id_type=MESH,
        )
        copy.start()
        sky_copies.append(copy)
    ty_row = band * ROWS - HALO + iota((tall, 128), 0)
    y = center(ty_row, ROWS * SKY)
    known = (ty_row >= 0) & (ty_row < ROWS * SKY)
    for u in range(3):

        def out(r, part, u=u):
            ty_ref[u, r : r + 128, :] = part

        row_pass(jnp.where(known, cheb(u, y), 0.0), out)
    each(smooth, 2, 4)
    for copy in sky_copies:
        copy.wait_recv()
    total = sky_mom[0]
    for k in range(1, SKY):
        total = total + sky_mom[k]
    mom[1] = total
    exp_mom[me] = total
    exp_copies = []
    for k in range(1, NEXP):
        copy = pltpu.make_async_remote_copy(
            src_ref=mom.at[1], dst_ref=exp_mom.at[me], send_sem=exp_s.at[k], recv_sem=exp_r.at[k],
            device_id=(lax.rem(me + k, NEXP), band), device_id_type=MESH,
        )
        copy.start()
        exp_copies.append(copy)
    for part in den:
        part.start3()
    each(smooth, 4, 8)
    for copy in exp_copies:
        copy.wait_recv()
    total = exp_mom[0]
    for k in range(1, NEXP):
        total = total + exp_mom[k]
    fits = jnp.concatenate(solve_lanes(total) + [jnp.zeros((7, 128), F32)], 0)
    fits = jnp.where(used > 0.0, fits, 0.0)
    nt = (((1,), (1,)), ((), ()))
    right = lax.dot_general(sign, fits, nt, precision=HIGH, preferred_element_type=F32)
    answer = jnp.dot(inverse, right, precision=HIGH, preferred_element_type=F32)
    offsets_ref[...] = answer[:, :9]
    offs[:, 0:NEXP] = answer
    coef = offs[pl.ds(me, 1), :]
    for k in range(9):
        coefs[k : k + 1, :] = jnp.broadcast_to(coef[:, k : k + 1], (1, 256))

    def numerator(half, dist):
        g = lax.rem((x, z)[half] + dist, 4)

        def chunk(b, carry):
            cx, cz = (g, b) if half == 0 else (b, g)
            tx = tx_ref[4 * cx + cz]
            lines = []
            for u in range(3):
                line = coefs[3 * u : 3 * u + 1, :] * tx[0:1]
                for v in range(1, 3):
                    line = line + coefs[3 * u + v : 3 * u + v + 1, :] * tx[v : v + 1]
                lines.append(line)
            step = NUM_ROWS[half] // 4
            for i in range(4):
                rows = slice(NUM_ROWS[0] * half + step * i, NUM_ROWS[0] * half + step * i + step)
                back = None
                for u in range(3):
                    ty = ty_ref[u, rows, :]
                    term = jnp.concatenate([ty, ty], 1) * lines[u]
                    back = term if back is None else back + term
                sv[cx, cz, rows, :] = wv[cx, cz, rows, :] * (sv[cx, cz, rows, :] - back)
            return carry

        lax.fori_loop(0, 4, chunk, 0)

    for half in range(2):
        numerator(half, 2)
        num[half].start1()
    for part in num[2:]:
        part.start1()
    each(smooth, 8, 16)
    for half in range(2):
        numerator(half, 1)
        numerator(half, 3)
        num[half].start2()
    for part in num[2:]:
        part.start2()
    for part in den:
        part.finish1()
    for part in num[:2]:
        part.start3()
    for half in range(2):
        numerator(half, 0)
    for part in num[2:]:
        part.start3()
    for part in den:
        part.start6()
    for part in num[:2]:
        part.finish1()
    for h in range(2):
        total_den[DEN_ROWS[0] * h : DEN_ROWS[0] * h + DEN_ROWS[h], :] = PRIOR + den[h].finish2()
    for part in num[:2]:
        part.start6()
    for part in num[2:]:
        part.finish1()
    for part in num[2:]:
        part.start6()

    for part in num:
        rows = slice(part.row0, part.row0 + 2 * part.half)
        coadd_ref[rows, :] = part.finish2() / total_den[rows, :]
    for copy in halos + bin_copies + sky_copies + exp_copies:
        copy.wait_send()
    for part in den + num:
        part.drain()


def per_device(image, variance, mask, foot_start, pair_owner):
    k, n = np.arange(512)[:, None], np.arange(256)[None, :]
    ch, cl = taps_matrix(k - n - 128)
    k, n = np.arange(160)[None, :], np.arange(128)[:, None]
    rh, rl = taps_matrix(k - n - HALO)
    big = lambda *shape: pltpu.VMEM(shape, F32)
    half = lambda *shape: pltpu.VMEM(shape, BF16)
    piece = lambda r: [big(4, r // 2, 256), big(4, r // 2, 256), big(4, r, 256), big(4, r, 256),
                       big(r // 2, 256), big(r // 2, 256), big(r, 256), big(r, 256)]
    pieces = lambda a, b: piece(a) + piece(b) + [big(4, b // 2, 256), big(4, b // 2, 256)]
    dma = lambda n: pltpu.SemaphoreType.DMA((n,))
    vmem = pl.BlockSpec(memory_space=pltpu.VMEM)
    tall = ROWS + 2 * HALO
    held = [
        big(16, ROWS, 256), big(4, 4, ROWS, 256), big(4, 4, ROWS, 256),
        pltpu.VMEM((BROWS, BCOLS), jnp.int32), pltpu.SMEM((NEXP,), jnp.int32), pltpu.VMEM((NEXP, NEXP), jnp.int32),
        half(512, 256), half(512, 256), half(128, 160), half(128, 160), big(HALO, COLS), big(HALO, COLS),
        half(tall + 16, 512), half(tall + 16, 512), big(16, 8, 256), big(3, ROWS, 128), half(BROWS, BCOLS),
        big(16, BROWS, 256), big(64, BCOLS), big(NEXP, 8, 128),
    ]
    fit = [big(NEXP, 8, 128), big(2, 40, 128), big(SKY, 40, 128), big(NEXP, 40, 128), big(NEXP, 128), big(16, 256),
           big(ROWS, 256)]
    sems = [dma(7), dma(16), dma(16), dma(2), dma(2), dma(96), dma(96), dma(NEXP), dma(NEXP), dma(SKY), dma(SKY),
            dma(NEXP), dma(NEXP)]
    return tuple(pl.pallas_call(
        coadd_kernel,
        in_specs=[pl.BlockSpec(memory_space=pltpu.HBM)] * 9,
        out_specs=[vmem, vmem],
        out_shape=[jax.ShapeDtypeStruct((ROWS, 256), F32), jax.ShapeDtypeStruct((NEXP, 9), F32)],
        scratch_shapes=held + fit + pieces(*DEN_ROWS) + pieces(NUM_ROWS[0] // 2, NUM_ROWS[1] // 2) * 2 + sems,
        compiler_params=pltpu.CompilerParams(collective_id=0, has_side_effects=True, vmem_limit_bytes=52 << 20),
        name="coadd",
    )(*(pltpu.with_memory_space_constraint(a, pltpu.HBM)
        for a in (image, variance, mask, foot_start, pair_owner, ch, cl, rh, rl))))


def solution(mesh):
    placed = (P("exp", "sky", None), P("exp", "sky", None), P("exp", "sky", None), P(), P())
    return jax.shard_map(
        per_device, mesh=mesh, in_specs=placed, out_specs=(P("sky", "exp"), P()), check_vma=False
    )
```

```python
import functools

import jax
import jax.numpy as jnp
import numpy as np
from jax import lax
from jax.experimental import pallas as pl
from jax.experimental.pallas import tpu as pltpu
from jax.sharding import PartitionSpec as P

F32 = jnp.float32
BF16 = jnp.bfloat16
HIGH = lax.Precision.HIGHEST
MESH = pl.DeviceIdType.MESH
BIN = 16
RADIUS = 10
NEXP = 16
ROWS = 512
COLS = 4096
SKY = 8
BROWS = 32
BCOLS = 256
FOOT_BINS = 192
HALO = 16
LAMBDA_REG = 0.25
DEN_ROWS = (240, 272)
NUM_ROWS = (224, 288)
PRIOR = 1.0


def iota(shape, dim):
    return lax.broadcasted_iota(jnp.int32, shape, dim)


def center(index, total):
    return (2.0 * index.astype(F32) + 1.0) / total - 1.0


def cheb(order, t):
    if order == 0:
        return jnp.ones_like(t)
    if order == 1:
        return t
    return 2.0 * t * t - 1.0


def split(value):
    high = value.astype(BF16)
    return high, (value - high.astype(F32)).astype(BF16)


def taps_matrix(offset):
    total = np.sum(np.exp(-(np.arange(-RADIUS, RADIUS + 1) ** 2) / 50.0))
    exact = np.where(np.abs(offset) <= RADIUS, np.exp(-(offset**2) / 50.0) / total, 0.0)
    high = exact.astype(BF16)
    return jnp.asarray(high), jnp.asarray((exact - high.astype(np.float64)).astype(BF16))


class Scatter:
    def __init__(self, part, lead, row0, rows, place, foot, bufs, sems, packed):
        self.part, self.lead, self.row0, self.half = part, lead, row0, rows // 2
        self.me, self.sky, self.foot = place[0], place[1], foot
        (self.f1p, self.f1m, self.rp, self.rm, self.f2p, self.f2m, self.r2p, self.r2m), rest = bufs[:8], bufs[8:]
        self.packs, self.lands = rest or (None, None)
        self.send_sems, self.recv_sems, self.counter = sems
        self.packed = packed
        self.copies = {}
        self.first = {"p": [], "m": []}
        self.second = []
        self.third = []

    def device(self, axis, shift):
        x, z = self.me
        if axis == 0:
            x = lax.rem(x + shift + 4, 4)
        else:
            z = lax.rem(z + shift + 4, 4)
        return (4 * x + z, self.sky)

    def to(self, dist):
        return lax.rem(self.me[self.lead] + dist, 4)

    def group(self, dist, r, chunks=(0, 4)):
        rows = pl.ds(self.row0 + r, self.half)
        some = pl.ds(*chunks)
        g = self.to(dist)
        return self.part.at[g, some, rows, :] if self.lead == 0 else self.part.at[some, g, rows, :]

    def own(self, b, dist, r):
        rows = pl.ds(self.row0 + r, self.half)
        g = self.to(dist)
        return self.part[g, b, rows, :] if self.lead == 0 else self.part[b, g, rows, :]

    def send(self, key, src, dst, axis, shift):
        n = self.counter[0]
        self.counter[0] += 1
        copy = pltpu.make_async_remote_copy(
            src_ref=src, dst_ref=dst, send_sem=self.send_sems.at[n], recv_sem=self.recv_sems.at[n],
            device_id=self.device(axis, shift), device_id_type=MESH,
        )
        copy.start()
        self.copies[key] = copy
        return copy

    def send_group(self, key, packed, slot, dist, r, land, to):
        if not packed:
            return [self.send(key, self.group(dist, r), land, self.lead, to)]
        raw = self.send(key, self.group(dist, r, (1, 2)), land.at[pl.ds(1, 2)], self.lead, to)
        self.packs[slot] = self.own(0, dist, r) + self.own(3, dist, r)
        return [raw, self.send(key + "s", self.packs.at[slot], self.lands.at[slot], self.lead, to)]

    def apart(self, slot, b):
        sender = self.foot[self.device(1, -1 if slot in (0, 2) else 1)[0]]
        g = self.to({0: 1, 1: 3, 2: 0, 3: 0}[slot])
        low = 256 * g + iota((1, 256), 1) >= BIN * sender
        return jnp.where(low if b == 0 else jnp.logical_not(low), self.lands[slot], 0.0)

    def start1(self):
        h = self.half
        self.first["p"] += self.send_group("1p", self.packed[0], 0, 2, 0, self.f1p, 1)
        self.first["m"] += self.send_group("1m", self.packed[0], 1, 2, h, self.f1m, -1)

    def start1_chunk(self, dist):
        b = lax.rem(self.me[1 - self.lead] + dist, 4)
        key = str(dist)
        self.first["p"].append(self.send("1p" + key, self.group(2, 0).at[b], self.f1p.at[b], self.lead, 1))
        self.first["m"].append(self.send("1m" + key, self.group(2, self.half).at[b], self.f1m.at[b], self.lead, -1))

    def start2(self):
        h = self.half
        self.second += self.send_group("2p", self.packed[1], 2, 1, h, self.rp.at[:, pl.ds(h, h), :], 1)
        self.second += self.send_group("2m", self.packed[1], 3, 3, 0, self.rm.at[:, pl.ds(0, h), :], -1)

    def start3(self, lo=0, hi=4):
        h = self.half
        for key, buf, dist, shift, land, slot, to in (
            ("p", self.f1p, 1, 0, self.rp, 0, 1), ("m", self.f1m, 3, h, self.rm, 1, -1)
        ):
            if lo == 0:
                for copy in self.first[key]:
                    copy.wait_recv()

            def body(b, carry, buf=buf, dist=dist, shift=shift):
                buf[b] = buf[b] + self.own(b, dist, shift)
                return carry

            if self.packed[0]:
                for b in (0, 3):
                    if lo <= b < hi:
                        buf[b] = self.apart(slot, b) + self.own(b, dist, shift)
                lax.fori_loop(max(lo, 1), min(hi, 3), body, 0)
            else:
                lax.fori_loop(lo, hi, body, 0)
            some = pl.ds(lo, hi - lo)
            self.third.append(
                self.send("3" + key + str(lo), buf.at[some], land.at[some, pl.ds(shift, h), :], self.lead, to)
            )

    def finish1(self):
        h = self.half
        top, low = pl.ds(0, h), pl.ds(h, h)
        for copy in self.second + self.third:
            copy.wait_recv()

        def body(b, carry):
            for shift in (0, h):
                rows = pl.ds(shift, h)
                self.rp[b, rows, :] = self.rp[b, rows, :] + self.rm[b, rows, :] + self.own(b, 0, shift)
            return carry

        if self.packed[1]:
            for b in (0, 3):
                self.rp[b, top, :] = self.rp[b, top, :] + self.apart(3, b) + self.own(b, 0, 0)
                self.rp[b, low, :] = self.apart(2, b) + self.rm[b, low, :] + self.own(b, 0, h)
            lax.fori_loop(1, 3, body, 0)
        else:
            lax.fori_loop(0, 4, body, 0)
        axis = 1 - self.lead
        at = lambda dist: lax.rem(self.me[axis] + dist, 4)
        self.send("4p", self.rp.at[at(2), top, :], self.f2p, axis, 1)
        self.send("4m", self.rp.at[at(2), low, :], self.f2m, axis, -1)
        self.send("5p", self.rp.at[at(1), low, :], self.r2p.at[low, :], axis, 1)
        self.send("5m", self.rp.at[at(3), top, :], self.r2m.at[top, :], axis, -1)

    def start6(self):
        axis = 1 - self.lead
        for key, buf, dist, shift, land, to in (
            ("p", self.f2p, 1, 0, self.r2p, 1), ("m", self.f2m, 3, self.half, self.r2m, -1)
        ):
            self.copies["4" + key].wait_recv()
            g = lax.rem(self.me[axis] + dist, 4)
            rows = pl.ds(shift, self.half)
            buf[...] = buf[...] + self.rp[g, rows, :]
            self.send("6" + key, buf, land.at[rows, :], axis, to)

    def finish2(self):
        for key in ("5p", "5m", "6p", "6m"):
            self.copies[key].wait_recv()
        g = self.me[1 - self.lead]
        return self.rp[g] + self.r2p[...] + self.r2m[...]

    def drain(self):
        for copy in self.copies.values():
            copy.wait_send()


def invert(system):
    lane, row = iota((NEXP, 128), 1), iota((NEXP, 128), 0)
    work = jnp.concatenate([system, jnp.zeros((NEXP, 112), F32)], 1)
    work = work + jnp.where(lane == row + NEXP, 1.0, 0.0)
    for j in range(NEXP):
        pivot_row = work[j : j + 1, :] / work[j : j + 1, j : j + 1]
        factor = work[:, j : j + 1]
        work = jnp.where(row == j, pivot_row, work - factor * pivot_row)
    return work[:, NEXP : 2 * NEXP]


def moments(bins, me, band):
    image = jnp.concatenate([bins[:, 0, :], bins[:, 4, :], bins[:, 1, :], bins[:, 5, :]], 1)
    weight = jnp.concatenate([bins[:, 2, :], bins[:, 6, :], bins[:, 3, :], bins[:, 7, :]], 1)
    ws, ds = [], []
    for d in range(1, 9):
        other = pltpu.roll(weight, NEXP - d, 0)
        w = weight * other / (weight + other + 1.0)
        ws.append(w)
        ds.append(w * (image - pltpu.roll(image, NEXP - d, 0)))
    w, wd = jnp.concatenate(ws, 0), jnp.concatenate(ds, 0)

    def basis(rows, base):
        k, lane = iota((rows, 512), 0), iota((rows, 512), 1)
        y = center(BROWS * band + 2 * me + lane // 256, BCOLS)
        x = center(lane % 256, BCOLS)

        def pick(order, t):
            t2 = 2.0 * t * t - 1.0
            out = jnp.where(order == 0, 1.0, jnp.where(order == 1, t, t2))
            if base == 5:
                out = jnp.where(order == 3, 2.0 * t * t2 - t, out)
                out = jnp.where(order == 4, 2.0 * t2 * t2 - 1.0, out)
            return out

        return jnp.where(k < base * base, pick(k // base, y) * pick(k % base, x), 0.0)

    nt = (((1,), (1,)), ((), ()))
    gram = lax.dot_general(basis(32, 5), w, nt, precision=HIGH, preferred_element_type=F32)
    rhs = lax.dot_general(basis(16, 3), wd, nt, precision=HIGH, preferred_element_type=F32)
    return jnp.concatenate([gram[:25], rhs[:9], jnp.zeros((6, 128), F32)], 0)


def solve_lanes(mom):
    m = lambda a, b: mom[5 * a + b : 5 * a + b + 1, :]
    cache = {}

    def entry(k, l):
        u, v, s, t = k // 3, k % 3, l // 3, l % 3
        key = tuple(sorted(((u + s, v + t), (abs(u - s), v + t), (u + s, abs(v - t)), (abs(u - s), abs(v - t)))))
        if key not in cache:
            cache[key] = 0.25 * ((m(*key[0]) + m(*key[1])) + (m(*key[2]) + m(*key[3])))
        return cache[key]

    a = [[entry(k, l) for l in range(k + 1)] for k in range(9)]
    b = [mom[25 + k : 26 + k, :] for k in range(9)]
    inv = [None] * 9
    for j in range(9):
        inv[j] = 1.0 / a[j][j]
        for k in range(j + 1, 9):
            f = a[k][j] * inv[j]
            for l in range(j + 1, k + 1):
                a[k][l] = a[k][l] - f * a[l][j]
            b[k] = b[k] - f * b[j]
    out = [None] * 9
    for j in reversed(range(9)):
        total = b[j]
        for k in range(j + 1, 9):
            total = total - a[k][j] * out[k]
        out[j] = total * inv[j]
    return out


def early(n):
    other = lax.rem((n - 1) // 2 + 3, 4) - 2
    odd = lax.rem(n - 1, 2)
    return 2 + odd * other, 2 + (1 - odd) * other


def late(n):
    return lax.rem((n - 7) // 3 + 3, 4), lax.rem(lax.rem(n - 7, 3) + 3, 4)


NUM_SCRATCH = 20


def coadd_kernel(image_hbm, variance_hbm, mask_hbm, foot_hbm, owner_hbm, ch_hbm, cl_hbm, rh_hbm, rl_hbm,
                 coadd_ref, offsets_ref, *scratch):
    (img, wv, sv, mask_ref, foot_ref, owner_ref, ch_ref, cl_ref, rh_ref, rl_ref, up_ref, down_ref, xh, xl, tx_ref,
     ty_ref, blocks, sums, binned, bins_own), scratch = scratch[:NUM_SCRATCH], scratch[NUM_SCRATCH:]
    (bins, mom, sky_mom, axis_mom, offs, coefs, total_den), scratch = scratch[:7], scratch[7:]
    bufs, scratch = scratch[:54], scratch[54:]
    (small_sems, var_sems, img_sems, halo_s, halo_r, send_sems, recv_sems,
     bin_s, bin_r, sky_s, sky_r, axis_s, axis_r) = scratch
    me, band = lax.axis_index("exp"), lax.axis_index("sky")
    x, z = me // 4, lax.rem(me, 4)
    tall = ROWS + 2 * HALO

    barrier = pltpu.get_barrier_semaphore()
    for k in range(1, NEXP):
        pl.semaphore_signal(barrier, inc=1, device_id=(lax.rem(me + k, NEXP), band), device_id_type=MESH)
    for k in range(1, SKY):
        pl.semaphore_signal(barrier, inc=1, device_id=(me, lax.rem(band + k, SKY)), device_id_type=MESH)

    def place(rel):
        return lax.rem(x + rel[0], 4), lax.rem(z + rel[1], 4)

    def load_var(n, rel):
        cx, cz = place(rel)
        cols = pl.ds(pl.multiple_of(256 * (4 * cx + cz), 256), 256)
        return pltpu.make_async_copy(variance_hbm.at[0, :, cols], wv.at[cx, cz], var_sems.at[n])

    def load_img(n, rel):
        cx, cz = place(rel)
        cols = pl.ds(pl.multiple_of(256 * (4 * cx + cz), 256), 256)
        return pltpu.make_async_copy(image_hbm.at[0, :, cols], img.at[4 * cx + cz], img_sems.at[n])

    def each(fn, lo=0, hi=16):
        if lo == 0:
            fn(0, (2, 2))
        for first, last, rel in ((1, 7, early), (7, 16, late)):
            first, last = max(lo, first), min(hi, last)
            if first < last:

                def body(n, carry, rel=rel):
                    fn(n, rel(n))
                    return carry

                lax.fori_loop(first, last, body, 0)

    small = [
        pltpu.make_async_copy(src, dst, small_sems.at[n])
        for n, (src, dst) in enumerate((
            (mask_hbm.at[0], mask_ref), (foot_hbm, foot_ref), (owner_hbm, owner_ref),
            (ch_hbm, ch_ref), (cl_hbm, cl_ref), (rh_hbm, rh_ref), (rl_hbm, rl_ref),
        ))
    ]
    for copy in small[:2]:
        copy.start()
    each(lambda n, rel: load_var(n, rel).start())
    each(lambda n, rel: load_img(n, rel).start())
    for copy in small[2:]:
        copy.start()

    for copy in small[:2]:
        copy.wait()
    start = foot_ref[me]
    cell = iota((BROWS, BCOLS), 1)
    inside = (cell >= start) & (cell < start + FOOT_BINS)
    blocks[...] = jnp.where(inside, mask_ref[...].astype(F32), 0.0).astype(BF16)

    def onehot(m):
        hit = iota((256, 256), 0) == 16 * m + iota((256, 256), 1) // BIN
        return jnp.where(hit, 1.0, 0.0).astype(BF16)

    def weights(n, rel):
        load_var(n, rel).wait()
        cx, cz = place(rel)
        wide = jnp.dot(blocks[...], onehot(4 * cx + cz), preferred_element_type=F32)
        for r in range(4):
            rows = slice(128 * r, 128 * r + 128)
            keep = jnp.broadcast_to(wide[8 * r : 8 * r + 8][:, None, :], (8, BIN, 256)).reshape(128, 256)
            w = keep * (1.0 / wv[cx, cz, rows, :])
            wv[cx, cz, rows, :] = w
            sums[4 * cx + cz, 8 * r : 8 * r + 8, :] = jnp.sum(w.reshape(8, BIN, 256), axis=1)

    where = ((x, z), band)
    take = lambda n: bufs[18 * (n // 2) : 18 * (n // 2) + 8] if n % 2 == 0 else bufs[18 * (n // 2) + 8 : 18 * (n // 2) + 18]
    sems = (send_sems, recv_sems, [0])
    den = [Scatter(wv, h, DEN_ROWS[0] * h, DEN_ROWS[h], where, foot_ref, take(h), sems, (False, h == 1)) for h in range(2)]
    num = [
        Scatter(sv, h, NUM_ROWS[0] * h + NUM_ROWS[h] // 2 * q, NUM_ROWS[h] // 2, where, foot_ref, take(2 + 2 * q + h),
                sems, (h == 1, h == 1))
        for q in range(2) for h in range(2)
    ]

    weights(0, (2, 2))
    pl.semaphore_wait(barrier, NEXP + SKY - 2)
    for part in den:
        part.start1_chunk(2)
    halos = []
    for n, (rows, dst, to) in enumerate(((ROWS - HALO, up_ref, band + 1), (0, down_ref, band + SKY - 1))):
        copy = pltpu.make_async_remote_copy(
            src_ref=image_hbm.at[0, pl.ds(rows, HALO), :], dst_ref=dst, send_sem=halo_s.at[n], recv_sem=halo_r.at[n],
            device_id=(me, lax.rem(to, SKY)), device_id_type=MESH,
        )
        copy.start()
        halos.append(copy)
    for t in range(3):
        dist = (3 + t) % 4
        weights(1 + 2 * t, (2, dist))
        den[0].start1_chunk(dist)
        weights(2 + 2 * t, (dist, 2))
        den[1].start1_chunk(dist)
    each(weights, 7, 16)

    def image_sums(n, rel):
        load_img(n, rel).wait()
        cx, cz = place(rel)
        m = 4 * cx + cz
        parts = []
        for r in range(4):
            parts.append(jnp.sum(img[m, 128 * r : 128 * r + 128, :].reshape(8, BIN, 256), axis=1))
        both = jnp.concatenate([jnp.concatenate(parts, 0) * (1.0 / (BIN * BIN)), sums[m]], 0)
        high = both.astype(BF16)
        rest = both - high.astype(F32)
        mid = rest.astype(BF16)
        low = (rest - mid.astype(F32)).astype(BF16)
        got = lax.dot_general(
            jnp.concatenate([high, mid, low], 0), onehot(m), (((1,), (1,)), ((), ())), preferred_element_type=F32
        )
        binned[...] = binned[...] + (got[:64] + got[64:128] + got[128:])

    binned[...] = jnp.zeros((64, BCOLS), F32)
    each(image_sums)
    for m in range(NEXP):
        tile = jnp.concatenate([binned[2 * m : 2 * m + 2, :], binned[32 + 2 * m : 34 + 2 * m, :]], 0)
        bins_own[m] = jnp.concatenate([tile[:, :128], tile[:, 128:]], 0)
    bin_copies = []
    for k in range(1, NEXP):
        to = lax.rem(me + k, NEXP)
        copy = pltpu.make_async_remote_copy(
            src_ref=bins_own.at[to], dst_ref=bins.at[me], send_sem=bin_s.at[k], recv_sem=bin_r.at[k],
            device_id=(to, band), device_id_type=MESH,
        )
        copy.start()
        bin_copies.append(copy)
    bins[me] = bins_own[me]
    for part in den:
        part.start2()

    for copy in small[2:]:
        copy.wait()
    for copy in halos:
        copy.wait_recv()

    def put(j, first, lane0, value):
        rows, width = value.shape
        col = 256 * j - 128 + lane0 + iota((1, width), 1)
        keep = (col >= BIN * start) & (col < BIN * (start + FOOT_BINS))
        high, low = split(jnp.where(keep, value, 0.0))
        xh[first : first + rows, lane0 : lane0 + width] = high
        xl[first : first + rows, lane0 : lane0 + width] = low

    def row_pass(value, out):
        high, low = split(value)
        for i in range(ROWS // 128):
            zh, zl = high[128 * i : 128 * i + 160], low[128 * i : 128 * i + 160]
            out(
                128 * i,
                jnp.dot(rh_ref[...], zh, preferred_element_type=F32)
                + jnp.dot(rl_ref[...], zh, preferred_element_type=F32)
                + jnp.dot(rh_ref[...], zl, preferred_element_type=F32),
            )

    def smooth(n, rel):
        cx, cz = place(rel)
        j = 4 * cx + cz
        before, after = jnp.maximum(j - 1, 0), jnp.minimum(j + 1, 15)
        lo = pl.multiple_of(jnp.maximum(256 * j - 128, 0), 128)
        mid = pl.multiple_of(256 * j, 128)
        hi = pl.multiple_of(jnp.minimum(256 * j + 256, COLS - 128), 128)
        for first, ref, known in ((0, up_ref, band > 0), (HALO + ROWS, down_ref, band < SKY - 1)):
            put(j, first, 0, jnp.where(known, ref[:, pl.ds(lo, 128)], 0.0))
            put(j, first, 128, jnp.where(known, ref[:, pl.ds(mid, 256)], 0.0))
            put(j, first, 384, jnp.where(known, ref[:, pl.ds(hi, 128)], 0.0))
        put(j, HALO, 0, img[before, :, 128:256])
        put(j, HALO, 128, img[j])
        put(j, HALO, 384, img[after, :, 0:128])
        xcol = center(256 * j - 128 + iota((16, 512), 1), COLS)
        order = iota((16, 512), 0)
        put(j, tall, 0, jnp.where(order == 0, 1.0, jnp.where(order == 1, xcol, 2.0 * xcol * xcol - 1.0)))
        across = (
            jnp.dot(xh[...], ch_ref[...], preferred_element_type=F32)
            + jnp.dot(xl[...], ch_ref[...], preferred_element_type=F32)
            + jnp.dot(xh[...], cl_ref[...], preferred_element_type=F32)
        )
        tx_ref[j] = across[tall : tall + 8]

        def out(r, part):
            sv[cx, cz, r : r + 128, :] = part

        row_pass(across[:tall], out)

    owner = owner_ref[...].astype(F32)
    both = owner + owner.T
    eye = iota((NEXP, NEXP), 0) == iota((NEXP, NEXP), 1)
    degree = jnp.sum(both, axis=1, keepdims=True) + LAMBDA_REG
    inverse = invert(jnp.where(eye, degree, 0.0) - both)
    lane, row = iota((NEXP, 128), 1), iota((NEXP, 128), 0)
    first = lax.rem(lane, NEXP)
    shift = lane // NEXP + 1
    second = lax.rem(first + shift, NEXP)
    at_first, at_second = row == first, row == second
    partner = jnp.dot(both, jnp.where(at_second, 1.0, 0.0), precision=HIGH, preferred_element_type=F32)
    used = jnp.sum(jnp.where(at_first, partner, 0.0), axis=0, keepdims=True)
    used = jnp.where((shift[:1] == 8) & (first[:1] >= 8), 0.0, used)
    sign = jnp.where(at_first, 1.0, 0.0) - jnp.where(at_second, 1.0, 0.0)

    each(smooth, 0, 2)
    for copy in bin_copies:
        copy.wait_recv()
    own = moments(bins, me, band)
    mom[0] = own
    sky_mom[band] = own
    sky_copies = []
    for k in range(1, SKY):
        copy = pltpu.make_async_remote_copy(
            src_ref=mom.at[0], dst_ref=sky_mom.at[band], send_sem=sky_s.at[k], recv_sem=sky_r.at[k],
            device_id=(me, lax.rem(band + k, SKY)), device_id_type=MESH,
        )
        copy.start()
        sky_copies.append(copy)
    ty_row = band * ROWS - HALO + iota((tall, 128), 0)
    y = center(ty_row, ROWS * SKY)
    known = (ty_row >= 0) & (ty_row < ROWS * SKY)
    for u in range(3):

        def out(r, part, u=u):
            ty_ref[u, r : r + 128, :] = part

        row_pass(jnp.where(known, cheb(u, y), 0.0), out)
    each(smooth, 2, 4)
    for copy in sky_copies:
        copy.wait_recv()
    total = sky_mom[0]
    for k in range(1, SKY):
        total = total + sky_mom[k]
    def exchange(n, total, at, device):
        mom[1 + n] = total
        axis_mom[n, at] = total
        copies = []
        for k in range(1, 4):
            copy = pltpu.make_async_remote_copy(
                src_ref=mom.at[1 + n], dst_ref=axis_mom.at[n, at], send_sem=axis_s.at[n, k], recv_sem=axis_r.at[n, k],
                device_id=(device(k), band), device_id_type=MESH,
            )
            copy.start()
            copies.append(copy)
        return copies

    def gathered(n, copies):
        for copy in copies:
            copy.wait_recv()
        return (axis_mom[n, 0] + axis_mom[n, 1]) + (axis_mom[n, 2] + axis_mom[n, 3])

    x_copies = exchange(0, total, x, lambda k: 4 * lax.rem(x + k, 4) + z)
    den[0].start3()
    den[1].start3(0, 2)
    each(smooth, 4, 5)
    z_copies = exchange(1, gathered(0, x_copies), z, lambda k: 4 * x + lax.rem(z + k, 4))
    den[1].start3(2, 4)
    each(smooth, 5, 8)
    total = gathered(1, z_copies)
    fits = jnp.concatenate(solve_lanes(total) + [jnp.zeros((7, 128), F32)], 0)
    fits = jnp.where(used > 0.0, fits, 0.0)
    nt = (((1,), (1,)), ((), ()))
    right = lax.dot_general(sign, fits, nt, precision=HIGH, preferred_element_type=F32)
    answer = jnp.dot(inverse, right, precision=HIGH, preferred_element_type=F32)
    offsets_ref[...] = answer[:, :9]
    offs[:, 0:NEXP] = answer
    coef = offs[pl.ds(me, 1), :]
    for k in range(9):
        coefs[k : k + 1, :] = jnp.broadcast_to(coef[:, k : k + 1], (1, 256))

    def numerator(half, dist):
        g = lax.rem((x, z)[half] + dist, 4)

        def chunk(b, carry):
            cx, cz = (g, b) if half == 0 else (b, g)
            tx = tx_ref[4 * cx + cz]
            lines = []
            for u in range(3):
                line = coefs[3 * u : 3 * u + 1, :] * tx[0:1]
                for v in range(1, 3):
                    line = line + coefs[3 * u + v : 3 * u + v + 1, :] * tx[v : v + 1]
                lines.append(line)
            step = NUM_ROWS[half] // 4
            for i in range(4):
                rows = slice(NUM_ROWS[0] * half + step * i, NUM_ROWS[0] * half + step * i + step)
                back = None
                for u in range(3):
                    ty = ty_ref[u, rows, :]
                    term = jnp.concatenate([ty, ty], 1) * lines[u]
                    back = term if back is None else back + term
                sv[cx, cz, rows, :] = wv[cx, cz, rows, :] * (sv[cx, cz, rows, :] - back)
            return carry

        lax.fori_loop(0, 4, chunk, 0)

    for half in range(2):
        numerator(half, 2)
        num[half].start1()
    for part in num[2:]:
        part.start1()
    each(smooth, 8, 16)
    for half in range(2):
        numerator(half, 1)
        numerator(half, 3)
        num[half].start2()
    for part in num[2:]:
        part.start2()
    for part in den:
        part.finish1()
    for part in num[:2]:
        part.start3()
    for half in range(2):
        numerator(half, 0)
    for part in num[2:]:
        part.start3()
    for part in den:
        part.start6()
    for part in num[:2]:
        part.finish1()
    for h in range(2):
        total_den[DEN_ROWS[0] * h : DEN_ROWS[0] * h + DEN_ROWS[h], :] = PRIOR + den[h].finish2()
    for part in num[:2]:
        part.start6()
    for part in num[2:]:
        part.finish1()
    for part in num[2:]:
        part.start6()

    for part in num:
        rows = slice(part.row0, part.row0 + 2 * part.half)
        coadd_ref[rows, :] = part.finish2() / total_den[rows, :]
    for copy in halos + bin_copies + sky_copies + x_copies + z_copies:
        copy.wait_send()
    for part in den + num:
        part.drain()


def per_device(image, variance, mask, foot_start, pair_owner):
    k, n = np.arange(512)[:, None], np.arange(256)[None, :]
    ch, cl = taps_matrix(k - n - 128)
    k, n = np.arange(160)[None, :], np.arange(128)[:, None]
    rh, rl = taps_matrix(k - n - HALO)
    big = lambda *shape: pltpu.VMEM(shape, F32)
    half = lambda *shape: pltpu.VMEM(shape, BF16)
    piece = lambda r: [big(4, r // 2, 256), big(4, r // 2, 256), big(4, r, 256), big(4, r, 256),
                       big(r // 2, 256), big(r // 2, 256), big(r, 256), big(r, 256)]
    pieces = lambda a, b: piece(a) + piece(b) + [big(4, b // 2, 256), big(4, b // 2, 256)]
    dma = lambda n: pltpu.SemaphoreType.DMA((n,))
    vmem = pl.BlockSpec(memory_space=pltpu.VMEM)
    tall = ROWS + 2 * HALO
    held = [
        big(16, ROWS, 256), big(4, 4, ROWS, 256), big(4, 4, ROWS, 256),
        pltpu.VMEM((BROWS, BCOLS), jnp.int32), pltpu.SMEM((NEXP,), jnp.int32), pltpu.VMEM((NEXP, NEXP), jnp.int32),
        half(512, 256), half(512, 256), half(128, 160), half(128, 160), big(HALO, COLS), big(HALO, COLS),
        half(tall + 16, 512), half(tall + 16, 512), big(16, 8, 256), big(3, ROWS, 128), half(BROWS, BCOLS),
        big(16, BROWS, 256), big(64, BCOLS), big(NEXP, 8, 128),
    ]
    fit = [big(NEXP, 8, 128), big(3, 40, 128), big(SKY, 40, 128), big(2, 4, 40, 128), big(NEXP, 128), big(16, 256),
           big(ROWS, 256)]
    sems = [dma(7), dma(16), dma(16), dma(2), dma(2), dma(104), dma(104), dma(NEXP), dma(NEXP), dma(SKY), dma(SKY),
            pltpu.SemaphoreType.DMA((2, 4)), pltpu.SemaphoreType.DMA((2, 4))]
    return tuple(pl.pallas_call(
        coadd_kernel,
        in_specs=[pl.BlockSpec(memory_space=pltpu.HBM)] * 9,
        out_specs=[vmem, vmem],
        out_shape=[jax.ShapeDtypeStruct((ROWS, 256), F32), jax.ShapeDtypeStruct((NEXP, 9), F32)],
        scratch_shapes=held + fit + pieces(*DEN_ROWS) + pieces(NUM_ROWS[0] // 2, NUM_ROWS[1] // 2) * 2 + sems,
        compiler_params=pltpu.CompilerParams(collective_id=0, has_side_effects=True, vmem_limit_bytes=52 << 20),
        name="coadd",
    )(*(pltpu.with_memory_space_constraint(a, pltpu.HBM)
        for a in (image, variance, mask, foot_start, pair_owner, ch, cl, rh, rl))))


def solution(mesh):
    placed = (P("exp", "sky", None), P("exp", "sky", None), P("exp", "sky", None), P(), P())
    return jax.shard_map(
        per_device, mesh=mesh, in_specs=placed, out_specs=(P("sky", "exp"), P()), check_vma=False
    )
```

```python
import functools

import jax
import jax.numpy as jnp
import numpy as np
from jax import lax
from jax.experimental import pallas as pl
from jax.experimental.pallas import tpu as pltpu
from jax.sharding import PartitionSpec as P

F32 = jnp.float32
BF16 = jnp.bfloat16
HIGH = lax.Precision.HIGHEST
MESH = pl.DeviceIdType.MESH
BIN = 16
RADIUS = 10
NEXP = 16
ROWS = 512
COLS = 4096
SKY = 8
BROWS = 32
BCOLS = 256
FOOT_BINS = 192
HALO = 16
LAMBDA_REG = 0.25
DEN_ROWS = (224, 288)
NUM_ROWS = (224, 288)
NUM_PIECES = ((160, 208), (64, 80))
PRIOR = 1.0


def iota(shape, dim):
    return lax.broadcasted_iota(jnp.int32, shape, dim)


def center(index, total):
    return (2.0 * index.astype(F32) + 1.0) / total - 1.0


def cheb(order, t):
    if order == 0:
        return jnp.ones_like(t)
    if order == 1:
        return t
    return 2.0 * t * t - 1.0


def split(value):
    high = value.astype(BF16)
    return high, (value - high.astype(F32)).astype(BF16)


def taps_matrix(offset):
    total = np.sum(np.exp(-(np.arange(-RADIUS, RADIUS + 1) ** 2) / 50.0))
    exact = np.where(np.abs(offset) <= RADIUS, np.exp(-(offset**2) / 50.0) / total, 0.0)
    high = exact.astype(BF16)
    return jnp.asarray(high), jnp.asarray((exact - high.astype(np.float64)).astype(BF16))


class Scatter:
    def __init__(self, part, lead, row0, rows, place, foot, bufs, sems, packed):
        self.part, self.lead, self.row0, self.half = part, lead, row0, rows // 2
        self.me, self.sky, self.foot = place[0], place[1], foot
        (self.f1p, self.f1m, self.rp, self.rm, self.f2p, self.f2m, self.r2p, self.r2m), rest = bufs[:8], bufs[8:]
        self.packs, self.lands = rest or (None, None)
        self.send_sems, self.recv_sems, self.counter = sems
        self.packed = packed
        self.copies = {}
        self.first = {"p": [], "m": []}
        self.second = []
        self.third = []

    def device(self, axis, shift):
        x, z = self.me
        if axis == 0:
            x = lax.rem(x + shift + 4, 4)
        else:
            z = lax.rem(z + shift + 4, 4)
        return (4 * x + z, self.sky)

    def to(self, dist):
        return lax.rem(self.me[self.lead] + dist, 4)

    def group(self, dist, r, chunks=(0, 4)):
        rows = pl.ds(self.row0 + r, self.half)
        some = pl.ds(*chunks)
        g = self.to(dist)
        return self.part.at[g, some, rows, :] if self.lead == 0 else self.part.at[some, g, rows, :]

    def own(self, b, dist, r):
        rows = pl.ds(self.row0 + r, self.half)
        g = self.to(dist)
        return self.part[g, b, rows, :] if self.lead == 0 else self.part[b, g, rows, :]

    def remote(self, src, dst, axis, shift):
        n = self.counter[0]
        self.counter[0] += 1
        return pltpu.make_async_remote_copy(
            src_ref=src, dst_ref=dst, send_sem=self.send_sems.at[n], recv_sem=self.recv_sems.at[n],
            device_id=self.device(axis, shift), device_id_type=MESH,
        )

    def keep(self, key, copies, copy):
        self.copies[key] = copy
        copies.append(copy)

    def send(self, key, src, dst, axis, shift):
        copy = self.remote(src, dst, axis, shift)
        copy.start()
        self.copies[key] = copy
        return copy

    def send_group(self, key, packed, slot, dist, r, land, to):
        if not packed:
            return [self.send(key, self.group(dist, r), land, self.lead, to)]
        raw = self.send(key, self.group(dist, r, (1, 2)), land.at[pl.ds(1, 2)], self.lead, to)
        self.packs[slot] = self.own(0, dist, r) + self.own(3, dist, r)
        return [raw, self.send(key + "s", self.packs.at[slot], self.lands.at[slot], self.lead, to)]

    def apart(self, slot, b):
        sender = self.foot[self.device(1, -1 if slot in (0, 2) else 1)[0]]
        g = self.to({0: 1, 1: 3, 2: 0, 3: 0}[slot])
        low = 256 * g + iota((1, 256), 1) >= BIN * sender
        return jnp.where(low if b == 0 else jnp.logical_not(low), self.lands[slot], 0.0)

    def start1(self):
        h = self.half
        self.first["p"] += self.send_group("1p", self.packed[0], 0, 2, 0, self.f1p, 1)
        self.first["m"] += self.send_group("1m", self.packed[0], 1, 2, h, self.f1m, -1)

    def start1_chunk(self, dist):
        b = lax.rem(self.me[1 - self.lead] + dist, 4)
        for key, r, buf, to in (("p", 0, self.f1p, 1), ("m", self.half, self.f1m, -1)):
            if not self.packed[0]:
                copy = self.remote(self.group(2, r).at[b], buf.at[b], self.lead, to)
                copy.start()
                self.keep("1" + key + str(dist), self.first[key], copy)
                continue
            for c in (1, 2):
                name = "1" + key + str(c)
                if name not in self.copies:
                    self.keep(name, self.first[key], self.remote(self.group(2, r).at[c], buf.at[c], self.lead, to))

                @pl.when(b == c)
                def _(name=name):
                    self.copies[name].start()

    def start1_sum(self):
        for key, slot, r, to in (("p", 0, 0, 1), ("m", 1, self.half, -1)):
            self.packs[slot] = self.own(0, 2, r) + self.own(3, 2, r)
            copy = self.remote(self.packs.at[slot], self.lands.at[slot], self.lead, to)
            copy.start()
            self.keep("1s" + key, self.first[key], copy)

    def start2(self):
        h = self.half
        self.second += self.send_group("2p", self.packed[1], 2, 1, h, self.rp.at[:, pl.ds(h, h), :], 1)
        self.second += self.send_group("2m", self.packed[1], 3, 3, 0, self.rm.at[:, pl.ds(0, h), :], -1)

    def start3(self, lo=0, hi=4):
        h = self.half
        for key, buf, dist, shift, land, slot, to in (
            ("p", self.f1p, 1, 0, self.rp, 0, 1), ("m", self.f1m, 3, h, self.rm, 1, -1)
        ):
            if lo == 0:
                for copy in self.first[key]:
                    copy.wait_recv()

            def body(b, carry, buf=buf, dist=dist, shift=shift):
                buf[b] = buf[b] + self.own(b, dist, shift)
                return carry

            if self.packed[0]:
                for b in (0, 3):
                    if lo <= b < hi:
                        buf[b] = self.apart(slot, b) + self.own(b, dist, shift)
                lax.fori_loop(max(lo, 1), min(hi, 3), body, 0)
            else:
                lax.fori_loop(lo, hi, body, 0)
            some = pl.ds(lo, hi - lo)
            self.third.append(
                self.send("3" + key + str(lo), buf.at[some], land.at[some, pl.ds(shift, h), :], self.lead, to)
            )

    def finish1(self):
        h = self.half
        top, low = pl.ds(0, h), pl.ds(h, h)
        for copy in self.second + self.third:
            copy.wait_recv()

        def body(b, carry):
            for shift in (0, h):
                rows = pl.ds(shift, h)
                self.rp[b, rows, :] = self.rp[b, rows, :] + self.rm[b, rows, :] + self.own(b, 0, shift)
            return carry

        if self.packed[1]:
            for b in (0, 3):
                self.rp[b, top, :] = self.rp[b, top, :] + self.apart(3, b) + self.own(b, 0, 0)
                self.rp[b, low, :] = self.apart(2, b) + self.rm[b, low, :] + self.own(b, 0, h)
            lax.fori_loop(1, 3, body, 0)
        else:
            lax.fori_loop(0, 4, body, 0)
        axis = 1 - self.lead
        at = lambda dist: lax.rem(self.me[axis] + dist, 4)
        self.send("4p", self.rp.at[at(2), top, :], self.f2p, axis, 1)
        self.send("4m", self.rp.at[at(2), low, :], self.f2m, axis, -1)
        self.send("5p", self.rp.at[at(1), low, :], self.r2p.at[low, :], axis, 1)
        self.send("5m", self.rp.at[at(3), top, :], self.r2m.at[top, :], axis, -1)

    def start6(self):
        axis = 1 - self.lead
        for key, buf, dist, shift, land, to in (
            ("p", self.f2p, 1, 0, self.r2p, 1), ("m", self.f2m, 3, self.half, self.r2m, -1)
        ):
            self.copies["4" + key].wait_recv()
            g = lax.rem(self.me[axis] + dist, 4)
            rows = pl.ds(shift, self.half)
            buf[...] = buf[...] + self.rp[g, rows, :]
            self.send("6" + key, buf, land.at[rows, :], axis, to)

    def finish2(self):
        for key in ("5p", "5m", "6p", "6m"):
            self.copies[key].wait_recv()
        g = self.me[1 - self.lead]
        return self.rp[g] + self.r2p[...] + self.r2m[...]

    def drain(self):
        for copy in self.copies.values():
            copy.wait_send()


def invert(system):
    lane, row = iota((NEXP, 128), 1), iota((NEXP, 128), 0)
    work = jnp.concatenate([system, jnp.zeros((NEXP, 112), F32)], 1)
    work = work + jnp.where(lane == row + NEXP, 1.0, 0.0)
    for j in range(NEXP):
        pivot_row = work[j : j + 1, :] / work[j : j + 1, j : j + 1]
        factor = work[:, j : j + 1]
        work = jnp.where(row == j, pivot_row, work - factor * pivot_row)
    return work[:, NEXP : 2 * NEXP]


def moments(bins, me, band):
    image = jnp.concatenate([bins[:, 0, :], bins[:, 4, :], bins[:, 1, :], bins[:, 5, :]], 1)
    weight = jnp.concatenate([bins[:, 2, :], bins[:, 6, :], bins[:, 3, :], bins[:, 7, :]], 1)
    ws, ds = [], []
    for d in range(1, 9):
        other = pltpu.roll(weight, NEXP - d, 0)
        w = weight * other / (weight + other + 1.0)
        ws.append(w)
        ds.append(w * (image - pltpu.roll(image, NEXP - d, 0)))
    w, wd = jnp.concatenate(ws, 0), jnp.concatenate(ds, 0)

    def basis(rows, base):
        k, lane = iota((rows, 512), 0), iota((rows, 512), 1)
        y = center(BROWS * band + 2 * me + lane // 256, BCOLS)
        x = center(lane % 256, BCOLS)

        def pick(order, t):
            t2 = 2.0 * t * t - 1.0
            out = jnp.where(order == 0, 1.0, jnp.where(order == 1, t, t2))
            if base == 5:
                out = jnp.where(order == 3, 2.0 * t * t2 - t, out)
                out = jnp.where(order == 4, 2.0 * t2 * t2 - 1.0, out)
            return out

        return jnp.where(k < base * base, pick(k // base, y) * pick(k % base, x), 0.0)

    nt = (((1,), (1,)), ((), ()))
    gram = lax.dot_general(basis(32, 5), w, nt, precision=HIGH, preferred_element_type=F32)
    rhs = lax.dot_general(basis(16, 3), wd, nt, precision=HIGH, preferred_element_type=F32)
    return jnp.concatenate([gram[:25], rhs[:9], jnp.zeros((6, 128), F32)], 0)


def solve_lanes(mom):
    m = lambda a, b: mom[5 * a + b : 5 * a + b + 1, :]
    cache = {}

    def entry(k, l):
        u, v, s, t = k // 3, k % 3, l // 3, l % 3
        key = tuple(sorted(((u + s, v + t), (abs(u - s), v + t), (u + s, abs(v - t)), (abs(u - s), abs(v - t)))))
        if key not in cache:
            cache[key] = 0.25 * ((m(*key[0]) + m(*key[1])) + (m(*key[2]) + m(*key[3])))
        return cache[key]

    a = [[entry(k, l) for l in range(k + 1)] for k in range(9)]
    b = [mom[25 + k : 26 + k, :] for k in range(9)]
    inv = [None] * 9
    for j in range(9):
        inv[j] = 1.0 / a[j][j]
        for k in range(j + 1, 9):
            f = a[k][j] * inv[j]
            for l in range(j + 1, k + 1):
                a[k][l] = a[k][l] - f * a[l][j]
            b[k] = b[k] - f * b[j]
    out = [None] * 9
    for j in reversed(range(9)):
        total = b[j]
        for k in range(j + 1, 9):
            total = total - a[k][j] * out[k]
        out[j] = total * inv[j]
    return out


def early(n):
    t = (n - 1) // 2
    other = t + t // 2 - 2
    odd = lax.rem(n - 1, 2)
    return 2 + odd * other, 2 + (1 - odd) * other


def late(n):
    return lax.rem((n - 7) // 3 + 3, 4), lax.rem(lax.rem(n - 7, 3) + 3, 4)


NUM_SCRATCH = 20


def coadd_kernel(image_hbm, variance_hbm, mask_hbm, foot_hbm, owner_hbm, ch_hbm, cl_hbm, rh_hbm, rl_hbm,
                 coadd_ref, offsets_ref, *scratch):
    (img, wv, sv, mask_ref, foot_ref, owner_ref, ch_ref, cl_ref, rh_ref, rl_ref, up_ref, down_ref, xh, xl, tx_ref,
     ty_ref, blocks, sums, binned, bins_own), scratch = scratch[:NUM_SCRATCH], scratch[NUM_SCRATCH:]
    (bins, mom, sky_mom, axis_mom, offs, coefs, total_den), scratch = scratch[:7], scratch[7:]
    bufs, scratch = scratch[:54], scratch[54:]
    (small_sems, var_sems, img_sems, halo_s, halo_r, send_sems, recv_sems,
     bin_s, bin_r, sky_s, sky_r, axis_s, axis_r) = scratch
    me, band = lax.axis_index("exp"), lax.axis_index("sky")
    x, z = me // 4, lax.rem(me, 4)
    tall = ROWS + 2 * HALO

    barrier = pltpu.get_barrier_semaphore()
    for k in range(1, NEXP):
        pl.semaphore_signal(barrier, inc=1, device_id=(lax.rem(me + k, NEXP), band), device_id_type=MESH)
    for k in range(1, SKY):
        pl.semaphore_signal(barrier, inc=1, device_id=(me, lax.rem(band + k, SKY)), device_id_type=MESH)

    def place(rel):
        return lax.rem(x + rel[0], 4), lax.rem(z + rel[1], 4)

    def load_var(n, rel):
        cx, cz = place(rel)
        cols = pl.ds(pl.multiple_of(256 * (4 * cx + cz), 256), 256)
        return pltpu.make_async_copy(variance_hbm.at[0, :, cols], wv.at[cx, cz], var_sems.at[n])

    def load_img(n, rel):
        cx, cz = place(rel)
        cols = pl.ds(pl.multiple_of(256 * (4 * cx + cz), 256), 256)
        return pltpu.make_async_copy(image_hbm.at[0, :, cols], img.at[4 * cx + cz], img_sems.at[n])

    def each(fn, lo=0, hi=16):
        if lo == 0:
            fn(0, (2, 2))
        for first, last, rel in ((1, 7, early), (7, 16, late)):
            first, last = max(lo, first), min(hi, last)
            if first < last:

                def body(n, carry, rel=rel):
                    fn(n, rel(n))
                    return carry

                lax.fori_loop(first, last, body, 0)

    small = [
        pltpu.make_async_copy(src, dst, small_sems.at[n])
        for n, (src, dst) in enumerate((
            (mask_hbm.at[0], mask_ref), (foot_hbm, foot_ref), (owner_hbm, owner_ref),
            (ch_hbm, ch_ref), (cl_hbm, cl_ref), (rh_hbm, rh_ref), (rl_hbm, rl_ref),
        ))
    ]
    for copy in small[:2]:
        copy.start()
    each(lambda n, rel: load_var(n, rel).start())
    each(lambda n, rel: load_img(n, rel).start())
    for copy in small[2:]:
        copy.start()

    for copy in small[:2]:
        copy.wait()
    start = foot_ref[me]
    cell = iota((BROWS, BCOLS), 1)
    inside = (cell >= start) & (cell < start + FOOT_BINS)
    blocks[...] = jnp.where(inside, mask_ref[...].astype(F32), 0.0).astype(BF16)

    def onehot(m):
        hit = iota((256, 256), 0) == 16 * m + iota((256, 256), 1) // BIN
        return jnp.where(hit, 1.0, 0.0).astype(BF16)

    def weights(n, rel):
        load_var(n, rel).wait()
        cx, cz = place(rel)
        wide = jnp.dot(blocks[...], onehot(4 * cx + cz), preferred_element_type=F32)
        for r in range(4):
            rows = slice(128 * r, 128 * r + 128)
            keep = jnp.broadcast_to(wide[8 * r : 8 * r + 8][:, None, :], (8, BIN, 256)).reshape(128, 256)
            w = keep * (1.0 / wv[cx, cz, rows, :])
            wv[cx, cz, rows, :] = w
            sums[4 * cx + cz, 8 * r : 8 * r + 8, :] = jnp.sum(w.reshape(8, BIN, 256), axis=1)

    where = ((x, z), band)
    take = lambda n: bufs[18 * (n // 2) : 18 * (n // 2) + 8] if n % 2 == 0 else bufs[18 * (n // 2) + 8 : 18 * (n // 2) + 18]
    sems = (send_sems, recv_sems, [0])
    den = [Scatter(wv, h, DEN_ROWS[0] * h, DEN_ROWS[h], where, foot_ref, take(h), sems, (h == 1, h == 1)) for h in range(2)]
    num = [
        Scatter(sv, h, NUM_ROWS[0] * h + NUM_PIECES[0][h] * q, NUM_PIECES[q][h], where, foot_ref, take(2 + 2 * q + h),
                sems, (h == 1, h == 1))
        for q in range(2) for h in range(2)
    ]

    weights(0, (2, 2))
    pl.semaphore_wait(barrier, NEXP + SKY - 2)
    for part in den:
        part.start1_chunk(2)
    halos = []
    for n, (rows, dst, to) in enumerate(((ROWS - HALO, up_ref, band + 1), (0, down_ref, band + SKY - 1))):
        copy = pltpu.make_async_remote_copy(
            src_ref=image_hbm.at[0, pl.ds(rows, HALO), :], dst_ref=dst, send_sem=halo_s.at[n], recv_sem=halo_r.at[n],
            device_id=(me, lax.rem(to, SKY)), device_id_type=MESH,
        )
        copy.start()
        halos.append(copy)
    for t in range(3):
        dist = (0, 1, 3)[t]
        weights(1 + 2 * t, (2, dist))
        den[0].start1_chunk(dist)
        weights(2 + 2 * t, (dist, 2))
        den[1].start1_chunk(dist)
    den[1].start1_sum()
    each(weights, 7, 16)

    def image_sums(n, rel):
        load_img(n, rel).wait()
        cx, cz = place(rel)
        m = 4 * cx + cz
        parts = []
        for r in range(4):
            parts.append(jnp.sum(img[m, 128 * r : 128 * r + 128, :].reshape(8, BIN, 256), axis=1))
        both = jnp.concatenate([jnp.concatenate(parts, 0) * (1.0 / (BIN * BIN)), sums[m]], 0)
        high = both.astype(BF16)
        rest = both - high.astype(F32)
        mid = rest.astype(BF16)
        low = (rest - mid.astype(F32)).astype(BF16)
        got = lax.dot_general(
            jnp.concatenate([high, mid, low], 0), onehot(m), (((1,), (1,)), ((), ())), preferred_element_type=F32
        )
        binned[...] = binned[...] + (got[:64] + got[64:128] + got[128:])

    binned[...] = jnp.zeros((64, BCOLS), F32)
    each(image_sums)
    for m in range(NEXP):
        tile = jnp.concatenate([binned[2 * m : 2 * m + 2, :], binned[32 + 2 * m : 34 + 2 * m, :]], 0)
        bins_own[m] = jnp.concatenate([tile[:, :128], tile[:, 128:]], 0)
    bin_copies = []
    for k in range(1, NEXP):
        to = lax.rem(me + k, NEXP)
        copy = pltpu.make_async_remote_copy(
            src_ref=bins_own.at[to], dst_ref=bins.at[me], send_sem=bin_s.at[k], recv_sem=bin_r.at[k],
            device_id=(to, band), device_id_type=MESH,
        )
        copy.start()
        bin_copies.append(copy)
    bins[me] = bins_own[me]
    for part in den:
        part.start2()

    for copy in small[2:]:
        copy.wait()
    for copy in halos:
        copy.wait_recv()

    def put(j, first, lane0, value):
        rows, width = value.shape
        col = 256 * j - 128 + lane0 + iota((1, width), 1)
        keep = (col >= BIN * start) & (col < BIN * (start + FOOT_BINS))
        high, low = split(jnp.where(keep, value, 0.0))
        xh[first : first + rows, lane0 : lane0 + width] = high
        xl[first : first + rows, lane0 : lane0 + width] = low

    def row_pass(value, out):
        high, low = split(value)
        for i in range(ROWS // 128):
            zh, zl = high[128 * i : 128 * i + 160], low[128 * i : 128 * i + 160]
            out(
                128 * i,
                jnp.dot(rh_ref[...], zh, preferred_element_type=F32)
                + jnp.dot(rl_ref[...], zh, preferred_element_type=F32)
                + jnp.dot(rh_ref[...], zl, preferred_element_type=F32),
            )

    def smooth(n, rel):
        cx, cz = place(rel)
        j = 4 * cx + cz
        before, after = jnp.maximum(j - 1, 0), jnp.minimum(j + 1, 15)
        lo = pl.multiple_of(jnp.maximum(256 * j - 128, 0), 128)
        mid = pl.multiple_of(256 * j, 128)
        hi = pl.multiple_of(jnp.minimum(256 * j + 256, COLS - 128), 128)
        for first, ref, known in ((0, up_ref, band > 0), (HALO + ROWS, down_ref, band < SKY - 1)):
            put(j, first, 0, jnp.where(known, ref[:, pl.ds(lo, 128)], 0.0))
            put(j, first, 128, jnp.where(known, ref[:, pl.ds(mid, 256)], 0.0))
            put(j, first, 384, jnp.where(known, ref[:, pl.ds(hi, 128)], 0.0))
        put(j, HALO, 0, img[before, :, 128:256])
        put(j, HALO, 128, img[j])
        put(j, HALO, 384, img[after, :, 0:128])
        xcol = center(256 * j - 128 + iota((16, 512), 1), COLS)
        order = iota((16, 512), 0)
        put(j, tall, 0, jnp.where(order == 0, 1.0, jnp.where(order == 1, xcol, 2.0 * xcol * xcol - 1.0)))
        across = (
            jnp.dot(xh[...], ch_ref[...], preferred_element_type=F32)
            + jnp.dot(xl[...], ch_ref[...], preferred_element_type=F32)
            + jnp.dot(xh[...], cl_ref[...], preferred_element_type=F32)
        )
        tx_ref[j] = across[tall : tall + 8]

        def out(r, part):
            sv[cx, cz, r : r + 128, :] = part

        row_pass(across[:tall], out)

    owner = owner_ref[...].astype(F32)
    both = owner + owner.T
    eye = iota((NEXP, NEXP), 0) == iota((NEXP, NEXP), 1)
    degree = jnp.sum(both, axis=1, keepdims=True) + LAMBDA_REG
    inverse = invert(jnp.where(eye, degree, 0.0) - both)
    lane, row = iota((NEXP, 128), 1), iota((NEXP, 128), 0)
    first = lax.rem(lane, NEXP)
    shift = lane // NEXP + 1
    second = lax.rem(first + shift, NEXP)
    at_first, at_second = row == first, row == second
    partner = jnp.dot(both, jnp.where(at_second, 1.0, 0.0), precision=HIGH, preferred_element_type=F32)
    used = jnp.sum(jnp.where(at_first, partner, 0.0), axis=0, keepdims=True)
    used = jnp.where((shift[:1] == 8) & (first[:1] >= 8), 0.0, used)
    sign = jnp.where(at_first, 1.0, 0.0) - jnp.where(at_second, 1.0, 0.0)

    each(smooth, 0, 2)
    for copy in bin_copies:
        copy.wait_recv()
    own = moments(bins, me, band)
    mom[0] = own
    sky_mom[band] = own
    sky_copies = []
    for k in range(1, SKY):
        copy = pltpu.make_async_remote_copy(
            src_ref=mom.at[0], dst_ref=sky_mom.at[band], send_sem=sky_s.at[k], recv_sem=sky_r.at[k],
            device_id=(me, lax.rem(band + k, SKY)), device_id_type=MESH,
        )
        copy.start()
        sky_copies.append(copy)
    ty_row = band * ROWS - HALO + iota((tall, 128), 0)
    y = center(ty_row, ROWS * SKY)
    known = (ty_row >= 0) & (ty_row < ROWS * SKY)
    for u in range(3):

        def out(r, part, u=u):
            ty_ref[u, r : r + 128, :] = part

        row_pass(jnp.where(known, cheb(u, y), 0.0), out)
    each(smooth, 2, 4)
    for copy in sky_copies:
        copy.wait_recv()
    total = sky_mom[0]
    for k in range(1, SKY):
        total = total + sky_mom[k]
    def exchange(n, total, at, device):
        mom[1 + n] = total
        axis_mom[n, at] = total
        copies = []
        for k in range(1, 4):
            copy = pltpu.make_async_remote_copy(
                src_ref=mom.at[1 + n], dst_ref=axis_mom.at[n, at], send_sem=axis_s.at[n, k], recv_sem=axis_r.at[n, k],
                device_id=(device(k), band), device_id_type=MESH,
            )
            copy.start()
            copies.append(copy)
        return copies

    def gathered(n, copies):
        for copy in copies:
            copy.wait_recv()
        return (axis_mom[n, 0] + axis_mom[n, 1]) + (axis_mom[n, 2] + axis_mom[n, 3])

    x_copies = exchange(0, total, x, lambda k: 4 * lax.rem(x + k, 4) + z)
    den[0].start3()
    den[1].start3(0, 2)
    each(smooth, 4, 5)
    z_copies = exchange(1, gathered(0, x_copies), z, lambda k: 4 * x + lax.rem(z + k, 4))
    den[1].start3(2, 4)
    each(smooth, 5, 8)
    total = gathered(1, z_copies)
    fits = jnp.concatenate(solve_lanes(total) + [jnp.zeros((7, 128), F32)], 0)
    fits = jnp.where(used > 0.0, fits, 0.0)
    nt = (((1,), (1,)), ((), ()))
    right = lax.dot_general(sign, fits, nt, precision=HIGH, preferred_element_type=F32)
    answer = jnp.dot(inverse, right, precision=HIGH, preferred_element_type=F32)
    offsets_ref[...] = answer[:, :9]
    offs[:, 0:NEXP] = answer
    coef = offs[pl.ds(me, 1), :]
    for k in range(9):
        coefs[k : k + 1, :] = jnp.broadcast_to(coef[:, k : k + 1], (1, 256))

    def numerator(half, dist):
        g = lax.rem((x, z)[half] + dist, 4)

        def chunk(b, carry):
            cx, cz = (g, b) if half == 0 else (b, g)
            tx = tx_ref[4 * cx + cz]
            lines = []
            for u in range(3):
                line = coefs[3 * u : 3 * u + 1, :] * tx[0:1]
                for v in range(1, 3):
                    line = line + coefs[3 * u + v : 3 * u + v + 1, :] * tx[v : v + 1]
                lines.append(line)
            step = NUM_ROWS[half] // 4
            for i in range(4):
                rows = slice(NUM_ROWS[0] * half + step * i, NUM_ROWS[0] * half + step * i + step)
                back = None
                for u in range(3):
                    ty = ty_ref[u, rows, :]
                    term = jnp.concatenate([ty, ty], 1) * lines[u]
                    back = term if back is None else back + term
                sv[cx, cz, rows, :] = wv[cx, cz, rows, :] * (sv[cx, cz, rows, :] - back)
            return carry

        lax.fori_loop(0, 4, chunk, 0)

    for half in range(2):
        numerator(half, 2)
        num[half].start1()
    for part in num[2:]:
        part.start1()
    each(smooth, 8, 16)
    for half in range(2):
        numerator(half, 1)
        numerator(half, 3)
        num[half].start2()
    for part in num[2:]:
        part.start2()
    for part in den:
        part.finish1()
    for part in num[:2]:
        part.start3()
    for half in range(2):
        numerator(half, 0)
    for part in den:
        part.start6()
    for part in num[2:]:
        part.start3()
    for part in num[:2]:
        part.finish1()
    for part in num[2:]:
        part.finish1()
    for part in num[:2]:
        part.start6()
    for part in num[2:]:
        part.start6()
    for h in range(2):
        total_den[DEN_ROWS[0] * h : DEN_ROWS[0] * h + DEN_ROWS[h], :] = PRIOR + den[h].finish2()
    for part in num:
        rows = slice(part.row0, part.row0 + 2 * part.half)
        coadd_ref[rows, :] = part.finish2() / total_den[rows, :]
    for copy in halos + bin_copies + sky_copies + x_copies + z_copies:
        copy.wait_send()
    for part in den + num:
        part.drain()


def per_device(image, variance, mask, foot_start, pair_owner):
    k, n = np.arange(512)[:, None], np.arange(256)[None, :]
    ch, cl = taps_matrix(k - n - 128)
    k, n = np.arange(160)[None, :], np.arange(128)[:, None]
    rh, rl = taps_matrix(k - n - HALO)
    big = lambda *shape: pltpu.VMEM(shape, F32)
    half = lambda *shape: pltpu.VMEM(shape, BF16)
    piece = lambda r: [big(4, r // 2, 256), big(4, r // 2, 256), big(4, r, 256), big(4, r, 256),
                       big(r // 2, 256), big(r // 2, 256), big(r, 256), big(r, 256)]
    pieces = lambda a, b: piece(a) + piece(b) + [big(4, b // 2, 256), big(4, b // 2, 256)]
    dma = lambda n: pltpu.SemaphoreType.DMA((n,))
    vmem = pl.BlockSpec(memory_space=pltpu.VMEM)
    tall = ROWS + 2 * HALO
    held = [
        big(16, ROWS, 256), big(4, 4, ROWS, 256), big(4, 4, ROWS, 256),
        pltpu.VMEM((BROWS, BCOLS), jnp.int32), pltpu.SMEM((NEXP,), jnp.int32), pltpu.VMEM((NEXP, NEXP), jnp.int32),
        half(512, 256), half(512, 256), half(128, 160), half(128, 160), big(HALO, COLS), big(HALO, COLS),
        half(tall + 16, 512), half(tall + 16, 512), big(16, 8, 256), big(3, ROWS, 128), half(BROWS, BCOLS),
        big(16, BROWS, 256), big(64, BCOLS), big(NEXP, 8, 128),
    ]
    fit = [big(NEXP, 8, 128), big(3, 40, 128), big(SKY, 40, 128), big(2, 4, 40, 128), big(NEXP, 128), big(16, 256),
           big(ROWS, 256)]
    sems = [dma(7), dma(16), dma(16), dma(2), dma(2), dma(104), dma(104), dma(NEXP), dma(NEXP), dma(SKY), dma(SKY),
            pltpu.SemaphoreType.DMA((2, 4)), pltpu.SemaphoreType.DMA((2, 4))]
    return tuple(pl.pallas_call(
        coadd_kernel,
        in_specs=[pl.BlockSpec(memory_space=pltpu.HBM)] * 9,
        out_specs=[vmem, vmem],
        out_shape=[jax.ShapeDtypeStruct((ROWS, 256), F32), jax.ShapeDtypeStruct((NEXP, 9), F32)],
        scratch_shapes=held + fit + pieces(*DEN_ROWS) + pieces(*NUM_PIECES[0]) + pieces(*NUM_PIECES[1]) + sems,
        compiler_params=pltpu.CompilerParams(collective_id=0, has_side_effects=True, vmem_limit_bytes=52 << 20),
        name="coadd",
    )(*(pltpu.with_memory_space_constraint(a, pltpu.HBM)
        for a in (image, variance, mask, foot_start, pair_owner, ch, cl, rh, rl))))


def solution(mesh):
    placed = (P("exp", "sky", None), P("exp", "sky", None), P("exp", "sky", None), P(), P())
    return jax.shard_map(
        per_device, mesh=mesh, in_specs=placed, out_specs=(P("sky", "exp"), P()), check_vma=False
    )
```

```python
import functools

import jax
import jax.numpy as jnp
import numpy as np
from jax import lax
from jax.experimental import pallas as pl
from jax.experimental.pallas import tpu as pltpu
from jax.sharding import PartitionSpec as P

F32 = jnp.float32
BF16 = jnp.bfloat16
HIGH = lax.Precision.HIGHEST
MESH = pl.DeviceIdType.MESH
BIN = 16
RADIUS = 10
NEXP = 16
ROWS = 512
COLS = 4096
SKY = 8
BROWS = 32
BCOLS = 256
FOOT_BINS = 192
HALO = 16
LAMBDA_REG = 0.25
DEN_ROWS = (224, 288)
NUM_ROWS = (224, 288)
NUM_PIECES = ((176, 224), (48, 64))
PRIOR = 1.0


def iota(shape, dim):
    return lax.broadcasted_iota(jnp.int32, shape, dim)


def center(index, total):
    return (2.0 * index.astype(F32) + 1.0) / total - 1.0


def cheb(order, t):
    if order == 0:
        return jnp.ones_like(t)
    if order == 1:
        return t
    return 2.0 * t * t - 1.0


def split(value):
    high = value.astype(BF16)
    return high, (value - high.astype(F32)).astype(BF16)


def taps_matrix(offset):
    total = np.sum(np.exp(-(np.arange(-RADIUS, RADIUS + 1) ** 2) / 50.0))
    exact = np.where(np.abs(offset) <= RADIUS, np.exp(-(offset**2) / 50.0) / total, 0.0)
    high = exact.astype(BF16)
    return jnp.asarray(high), jnp.asarray((exact - high.astype(np.float64)).astype(BF16))


class Scatter:
    def __init__(self, part, lead, row0, rows, place, foot, bufs, sems, packed):
        self.part, self.lead, self.row0, self.half = part, lead, row0, rows // 2
        self.me, self.sky, self.foot = place[0], place[1], foot
        (self.f1p, self.f1m, self.rp, self.rm, self.f2p, self.f2m, self.r2p, self.r2m), rest = bufs[:8], bufs[8:]
        self.packs, self.lands = rest or (None, None)
        self.send_sems, self.recv_sems, self.counter = sems
        self.packed = packed
        self.copies = {}
        self.first = {"p": [], "m": []}
        self.second = []
        self.third = []

    def device(self, axis, shift):
        x, z = self.me
        if axis == 0:
            x = lax.rem(x + shift + 4, 4)
        else:
            z = lax.rem(z + shift + 4, 4)
        return (4 * x + z, self.sky)

    def to(self, dist):
        return lax.rem(self.me[self.lead] + dist, 4)

    def group(self, dist, r, chunks=(0, 4)):
        rows = pl.ds(self.row0 + r, self.half)
        some = pl.ds(*chunks)
        g = self.to(dist)
        return self.part.at[g, some, rows, :] if self.lead == 0 else self.part.at[some, g, rows, :]

    def own(self, b, dist, r):
        rows = pl.ds(self.row0 + r, self.half)
        g = self.to(dist)
        return self.part[g, b, rows, :] if self.lead == 0 else self.part[b, g, rows, :]

    def remote(self, src, dst, axis, shift):
        n = self.counter[0]
        self.counter[0] += 1
        return pltpu.make_async_remote_copy(
            src_ref=src, dst_ref=dst, send_sem=self.send_sems.at[n], recv_sem=self.recv_sems.at[n],
            device_id=self.device(axis, shift), device_id_type=MESH,
        )

    def keep(self, key, copies, copy):
        self.copies[key] = copy
        copies.append(copy)

    def send(self, key, src, dst, axis, shift):
        copy = self.remote(src, dst, axis, shift)
        copy.start()
        self.copies[key] = copy
        return copy

    def send_group(self, key, packed, slot, dist, r, land, to):
        if not packed:
            return [self.send(key, self.group(dist, r), land, self.lead, to)]
        raw = self.send(key, self.group(dist, r, (1, 2)), land.at[pl.ds(1, 2)], self.lead, to)
        self.packs[slot] = self.own(0, dist, r) + self.own(3, dist, r)
        return [raw, self.send(key + "s", self.packs.at[slot], self.lands.at[slot], self.lead, to)]

    def apart(self, slot, b):
        sender = self.foot[self.device(1, -1 if slot in (0, 2) else 1)[0]]
        g = self.to({0: 1, 1: 3, 2: 0, 3: 0}[slot])
        low = 256 * g + iota((1, 256), 1) >= BIN * sender
        return jnp.where(low if b == 0 else jnp.logical_not(low), self.lands[slot], 0.0)

    def start1(self):
        h = self.half
        self.first["p"] += self.send_group("1p", self.packed[0], 0, 2, 0, self.f1p, 1)
        self.first["m"] += self.send_group("1m", self.packed[0], 1, 2, h, self.f1m, -1)

    def start1_chunk(self, dist):
        b = lax.rem(self.me[1 - self.lead] + dist, 4)
        for key, r, buf, to in (("p", 0, self.f1p, 1), ("m", self.half, self.f1m, -1)):
            if not self.packed[0]:
                copy = self.remote(self.group(2, r).at[b], buf.at[b], self.lead, to)
                copy.start()
                self.keep("1" + key + str(dist), self.first[key], copy)
                continue
            for c in (1, 2):
                name = "1" + key + str(c)
                if name not in self.copies:
                    self.keep(name, self.first[key], self.remote(self.group(2, r).at[c], buf.at[c], self.lead, to))

                @pl.when(b == c)
                def _(name=name):
                    self.copies[name].start()

    def start1_sum(self):
        for key, slot, r, to in (("p", 0, 0, 1), ("m", 1, self.half, -1)):
            self.packs[slot] = self.own(0, 2, r) + self.own(3, 2, r)
            copy = self.remote(self.packs.at[slot], self.lands.at[slot], self.lead, to)
            copy.start()
            self.keep("1s" + key, self.first[key], copy)

    def start2(self):
        h = self.half
        self.second += self.send_group("2p", self.packed[1], 2, 1, h, self.rp.at[:, pl.ds(h, h), :], 1)
        self.second += self.send_group("2m", self.packed[1], 3, 3, 0, self.rm.at[:, pl.ds(0, h), :], -1)

    def start3(self, lo=0, hi=4):
        h = self.half
        for key, buf, dist, shift, land, slot, to in (
            ("p", self.f1p, 1, 0, self.rp, 0, 1), ("m", self.f1m, 3, h, self.rm, 1, -1)
        ):
            if lo == 0:
                for copy in self.first[key]:
                    copy.wait_recv()

            def body(b, carry, buf=buf, dist=dist, shift=shift):
                buf[b] = buf[b] + self.own(b, dist, shift)
                return carry

            if self.packed[0]:
                for b in (0, 3):
                    if lo <= b < hi:
                        buf[b] = self.apart(slot, b) + self.own(b, dist, shift)
                lax.fori_loop(max(lo, 1), min(hi, 3), body, 0)
            else:
                lax.fori_loop(lo, hi, body, 0)
            some = pl.ds(lo, hi - lo)
            self.third.append(
                self.send("3" + key + str(lo), buf.at[some], land.at[some, pl.ds(shift, h), :], self.lead, to)
            )

    def finish1(self):
        h = self.half
        top, low = pl.ds(0, h), pl.ds(h, h)
        for copy in self.second + self.third:
            copy.wait_recv()

        def body(b, carry):
            for shift in (0, h):
                rows = pl.ds(shift, h)
                self.rp[b, rows, :] = self.rp[b, rows, :] + self.rm[b, rows, :] + self.own(b, 0, shift)
            return carry

        if self.packed[1]:
            for b in (0, 3):
                self.rp[b, top, :] = self.rp[b, top, :] + self.apart(3, b) + self.own(b, 0, 0)
                self.rp[b, low, :] = self.apart(2, b) + self.rm[b, low, :] + self.own(b, 0, h)
            lax.fori_loop(1, 3, body, 0)
        else:
            lax.fori_loop(0, 4, body, 0)
        axis = 1 - self.lead
        at = lambda dist: lax.rem(self.me[axis] + dist, 4)
        self.send("4p", self.rp.at[at(2), top, :], self.f2p, axis, 1)
        self.send("4m", self.rp.at[at(2), low, :], self.f2m, axis, -1)
        self.send("5p", self.rp.at[at(1), low, :], self.r2p.at[low, :], axis, 1)
        self.send("5m", self.rp.at[at(3), top, :], self.r2m.at[top, :], axis, -1)

    def start6(self):
        axis = 1 - self.lead
        for key, buf, dist, shift, land, to in (
            ("p", self.f2p, 1, 0, self.r2p, 1), ("m", self.f2m, 3, self.half, self.r2m, -1)
        ):
            self.copies["4" + key].wait_recv()
            g = lax.rem(self.me[axis] + dist, 4)
            rows = pl.ds(shift, self.half)
            buf[...] = buf[...] + self.rp[g, rows, :]
            self.send("6" + key, buf, land.at[rows, :], axis, to)

    def finish2(self):
        for key in ("5p", "5m", "6p", "6m"):
            self.copies[key].wait_recv()
        g = self.me[1 - self.lead]
        return self.rp[g] + self.r2p[...] + self.r2m[...]

    def drain(self):
        for copy in self.copies.values():
            copy.wait_send()


def invert(system):
    lane, row = iota((NEXP, 128), 1), iota((NEXP, 128), 0)
    work = jnp.concatenate([system, jnp.zeros((NEXP, 112), F32)], 1)
    work = work + jnp.where(lane == row + NEXP, 1.0, 0.0)
    for j in range(NEXP):
        pivot_row = work[j : j + 1, :] / work[j : j + 1, j : j + 1]
        factor = work[:, j : j + 1]
        work = jnp.where(row == j, pivot_row, work - factor * pivot_row)
    return work[:, NEXP : 2 * NEXP]


def moments(bins, me, band):
    image = jnp.concatenate([bins[:, 0, :], bins[:, 4, :], bins[:, 1, :], bins[:, 5, :]], 1)
    weight = jnp.concatenate([bins[:, 2, :], bins[:, 6, :], bins[:, 3, :], bins[:, 7, :]], 1)
    ws, ds = [], []
    for d in range(1, 9):
        other = pltpu.roll(weight, NEXP - d, 0)
        w = weight * other / (weight + other + 1.0)
        ws.append(w)
        ds.append(w * (image - pltpu.roll(image, NEXP - d, 0)))
    w, wd = jnp.concatenate(ws, 0), jnp.concatenate(ds, 0)

    def basis(rows, base):
        k, lane = iota((rows, 512), 0), iota((rows, 512), 1)
        y = center(BROWS * band + 2 * me + lane // 256, BCOLS)
        x = center(lane % 256, BCOLS)

        def pick(order, t):
            t2 = 2.0 * t * t - 1.0
            out = jnp.where(order == 0, 1.0, jnp.where(order == 1, t, t2))
            if base == 5:
                out = jnp.where(order == 3, 2.0 * t * t2 - t, out)
                out = jnp.where(order == 4, 2.0 * t2 * t2 - 1.0, out)
            return out

        return jnp.where(k < base * base, pick(k // base, y) * pick(k % base, x), 0.0)

    nt = (((1,), (1,)), ((), ()))
    gram = lax.dot_general(basis(32, 5), w, nt, precision=HIGH, preferred_element_type=F32)
    rhs = lax.dot_general(basis(16, 3), wd, nt, precision=HIGH, preferred_element_type=F32)
    return jnp.concatenate([gram[:25], rhs[:9], jnp.zeros((6, 128), F32)], 0)


def solve_lanes(mom):
    m = lambda a, b: mom[5 * a + b : 5 * a + b + 1, :]
    cache = {}

    def entry(k, l):
        u, v, s, t = k // 3, k % 3, l // 3, l % 3
        key = tuple(sorted(((u + s, v + t), (abs(u - s), v + t), (u + s, abs(v - t)), (abs(u - s), abs(v - t)))))
        if key not in cache:
            cache[key] = 0.25 * ((m(*key[0]) + m(*key[1])) + (m(*key[2]) + m(*key[3])))
        return cache[key]

    a = [[entry(k, l) for l in range(k + 1)] for k in range(9)]
    b = [mom[25 + k : 26 + k, :] for k in range(9)]
    inv = [None] * 9
    for j in range(9):
        inv[j] = 1.0 / a[j][j]
        for k in range(j + 1, 9):
            f = a[k][j] * inv[j]
            for l in range(j + 1, k + 1):
                a[k][l] = a[k][l] - f * a[l][j]
            b[k] = b[k] - f * b[j]
    out = [None] * 9
    for j in reversed(range(9)):
        total = b[j]
        for k in range(j + 1, 9):
            total = total - a[k][j] * out[k]
        out[j] = total * inv[j]
    return out


def early(n):
    t = (n - 1) // 2
    other = t + t // 2 - 2
    odd = lax.rem(n - 1, 2)
    return 2 + odd * other, 2 + (1 - odd) * other


def late(n):
    return lax.rem((n - 7) // 3 + 3, 4), lax.rem(lax.rem(n - 7, 3) + 3, 4)


NUM_SCRATCH = 20


def coadd_kernel(image_hbm, variance_hbm, mask_hbm, foot_hbm, owner_hbm, ch_hbm, cl_hbm, rh_hbm, rl_hbm,
                 coadd_ref, offsets_ref, *scratch):
    (img, wv, sv, mask_ref, foot_ref, owner_ref, ch_ref, cl_ref, rh_ref, rl_ref, up_ref, down_ref, xh, xl, tx_ref,
     ty_ref, blocks, sums, binned, bins_own), scratch = scratch[:NUM_SCRATCH], scratch[NUM_SCRATCH:]
    (bins, mom, sky_mom, axis_mom, offs, coefs, total_den), scratch = scratch[:7], scratch[7:]
    bufs, scratch = scratch[:54], scratch[54:]
    (small_sems, var_sems, img_sems, halo_s, halo_r, send_sems, recv_sems,
     bin_s, bin_r, sky_s, sky_r, axis_s, axis_r) = scratch
    me, band = lax.axis_index("exp"), lax.axis_index("sky")
    x, z = me // 4, lax.rem(me, 4)
    tall = ROWS + 2 * HALO

    barrier = pltpu.get_barrier_semaphore()
    for k in range(1, NEXP):
        pl.semaphore_signal(barrier, inc=1, device_id=(lax.rem(me + k, NEXP), band), device_id_type=MESH)
    for k in range(1, SKY):
        pl.semaphore_signal(barrier, inc=1, device_id=(me, lax.rem(band + k, SKY)), device_id_type=MESH)

    def place(rel):
        return lax.rem(x + rel[0], 4), lax.rem(z + rel[1], 4)

    def load_var(n, rel):
        cx, cz = place(rel)
        cols = pl.ds(pl.multiple_of(256 * (4 * cx + cz), 256), 256)
        return pltpu.make_async_copy(variance_hbm.at[0, :, cols], wv.at[cx, cz], var_sems.at[n])

    def load_img(n, rel):
        cx, cz = place(rel)
        cols = pl.ds(pl.multiple_of(256 * (4 * cx + cz), 256), 256)
        return pltpu.make_async_copy(image_hbm.at[0, :, cols], img.at[4 * cx + cz], img_sems.at[n])

    def each(fn, lo=0, hi=16):
        if lo == 0:
            fn(0, (2, 2))
        for first, last, rel in ((1, 7, early), (7, 16, late)):
            first, last = max(lo, first), min(hi, last)
            if first < last:

                def body(n, carry, rel=rel):
                    fn(n, rel(n))
                    return carry

                lax.fori_loop(first, last, body, 0)

    small = [
        pltpu.make_async_copy(src, dst, small_sems.at[n])
        for n, (src, dst) in enumerate((
            (mask_hbm.at[0], mask_ref), (foot_hbm, foot_ref), (owner_hbm, owner_ref),
            (ch_hbm, ch_ref), (cl_hbm, cl_ref), (rh_hbm, rh_ref), (rl_hbm, rl_ref),
        ))
    ]
    for copy in small[:2]:
        copy.start()
    each(lambda n, rel: load_var(n, rel).start())
    each(lambda n, rel: load_img(n, rel).start())
    for copy in small[2:]:
        copy.start()

    for copy in small[:2]:
        copy.wait()
    start = foot_ref[me]
    cell = iota((BROWS, BCOLS), 1)
    inside = (cell >= start) & (cell < start + FOOT_BINS)
    blocks[...] = jnp.where(inside, mask_ref[...].astype(F32), 0.0).astype(BF16)

    def onehot(m):
        hit = iota((256, 256), 0) == 16 * m + iota((256, 256), 1) // BIN
        return jnp.where(hit, 1.0, 0.0).astype(BF16)

    def weights(n, rel):
        load_var(n, rel).wait()
        cx, cz = place(rel)
        wide = jnp.dot(blocks[...], onehot(4 * cx + cz), preferred_element_type=F32)
        for r in range(4):
            rows = slice(128 * r, 128 * r + 128)
            keep = jnp.broadcast_to(wide[8 * r : 8 * r + 8][:, None, :], (8, BIN, 256)).reshape(128, 256)
            w = keep * (1.0 / wv[cx, cz, rows, :])
            wv[cx, cz, rows, :] = w
            sums[4 * cx + cz, 8 * r : 8 * r + 8, :] = jnp.sum(w.reshape(8, BIN, 256), axis=1)

    where = ((x, z), band)
    take = lambda n: bufs[18 * (n // 2) : 18 * (n // 2) + 8] if n % 2 == 0 else bufs[18 * (n // 2) + 8 : 18 * (n // 2) + 18]
    sems = (send_sems, recv_sems, [0])
    den = [Scatter(wv, h, DEN_ROWS[0] * h, DEN_ROWS[h], where, foot_ref, take(h), sems, (h == 1, h == 1)) for h in range(2)]
    num = [
        Scatter(sv, h, NUM_ROWS[0] * h + NUM_PIECES[0][h] * q, NUM_PIECES[q][h], where, foot_ref, take(2 + 2 * q + h),
                sems, (h == 1, h == 1))
        for q in range(2) for h in range(2)
    ]

    weights(0, (2, 2))
    pl.semaphore_wait(barrier, NEXP + SKY - 2)
    for part in den:
        part.start1_chunk(2)
    halos = []
    for n, (rows, dst, to) in enumerate(((ROWS - HALO, up_ref, band + 1), (0, down_ref, band + SKY - 1))):
        copy = pltpu.make_async_remote_copy(
            src_ref=image_hbm.at[0, pl.ds(rows, HALO), :], dst_ref=dst, send_sem=halo_s.at[n], recv_sem=halo_r.at[n],
            device_id=(me, lax.rem(to, SKY)), device_id_type=MESH,
        )
        copy.start()
        halos.append(copy)
    for t in range(3):
        dist = (0, 1, 3)[t]
        weights(1 + 2 * t, (2, dist))
        den[0].start1_chunk(dist)
        weights(2 + 2 * t, (dist, 2))
        den[1].start1_chunk(dist)
    den[1].start1_sum()
    each(weights, 7, 16)

    def image_sums(n, rel):
        load_img(n, rel).wait()
        cx, cz = place(rel)
        m = 4 * cx + cz
        parts = []
        for r in range(4):
            parts.append(jnp.sum(img[m, 128 * r : 128 * r + 128, :].reshape(8, BIN, 256), axis=1))
        both = jnp.concatenate([jnp.concatenate(parts, 0) * (1.0 / (BIN * BIN)), sums[m]], 0)
        high = both.astype(BF16)
        rest = both - high.astype(F32)
        mid = rest.astype(BF16)
        low = (rest - mid.astype(F32)).astype(BF16)
        got = lax.dot_general(
            jnp.concatenate([high, mid, low], 0), onehot(m), (((1,), (1,)), ((), ())), preferred_element_type=F32
        )
        binned[...] = binned[...] + (got[:64] + got[64:128] + got[128:])

    binned[...] = jnp.zeros((64, BCOLS), F32)
    each(image_sums)
    for m in range(NEXP):
        tile = jnp.concatenate([binned[2 * m : 2 * m + 2, :], binned[32 + 2 * m : 34 + 2 * m, :]], 0)
        bins_own[m] = jnp.concatenate([tile[:, :128], tile[:, 128:]], 0)
    bin_copies = []
    for k in range(1, NEXP):
        to = lax.rem(me + k, NEXP)
        copy = pltpu.make_async_remote_copy(
            src_ref=bins_own.at[to], dst_ref=bins.at[me], send_sem=bin_s.at[k], recv_sem=bin_r.at[k],
            device_id=(to, band), device_id_type=MESH,
        )
        copy.start()
        bin_copies.append(copy)
    bins[me] = bins_own[me]
    for part in den:
        part.start2()

    for copy in small[2:]:
        copy.wait()
    for copy in halos:
        copy.wait_recv()

    def put(j, first, lane0, value):
        rows, width = value.shape
        col = 256 * j - 128 + lane0 + iota((1, width), 1)
        keep = (col >= BIN * start) & (col < BIN * (start + FOOT_BINS))
        high, low = split(jnp.where(keep, value, 0.0))
        xh[first : first + rows, lane0 : lane0 + width] = high
        xl[first : first + rows, lane0 : lane0 + width] = low

    def row_pass(value, out):
        high, low = split(value)
        for i in range(ROWS // 128):
            zh, zl = high[128 * i : 128 * i + 160], low[128 * i : 128 * i + 160]
            out(
                128 * i,
                jnp.dot(rh_ref[...], zh, preferred_element_type=F32)
                + jnp.dot(rl_ref[...], zh, preferred_element_type=F32)
                + jnp.dot(rh_ref[...], zl, preferred_element_type=F32),
            )

    def smooth(n, rel):
        cx, cz = place(rel)
        j = 4 * cx + cz
        before, after = jnp.maximum(j - 1, 0), jnp.minimum(j + 1, 15)
        lo = pl.multiple_of(jnp.maximum(256 * j - 128, 0), 128)
        mid = pl.multiple_of(256 * j, 128)
        hi = pl.multiple_of(jnp.minimum(256 * j + 256, COLS - 128), 128)
        for first, ref, known in ((0, up_ref, band > 0), (HALO + ROWS, down_ref, band < SKY - 1)):
            put(j, first, 0, jnp.where(known, ref[:, pl.ds(lo, 128)], 0.0))
            put(j, first, 128, jnp.where(known, ref[:, pl.ds(mid, 256)], 0.0))
            put(j, first, 384, jnp.where(known, ref[:, pl.ds(hi, 128)], 0.0))
        put(j, HALO, 0, img[before, :, 128:256])
        put(j, HALO, 128, img[j])
        put(j, HALO, 384, img[after, :, 0:128])
        xcol = center(256 * j - 128 + iota((16, 512), 1), COLS)
        order = iota((16, 512), 0)
        put(j, tall, 0, jnp.where(order == 0, 1.0, jnp.where(order == 1, xcol, 2.0 * xcol * xcol - 1.0)))
        across = (
            jnp.dot(xh[...], ch_ref[...], preferred_element_type=F32)
            + jnp.dot(xl[...], ch_ref[...], preferred_element_type=F32)
            + jnp.dot(xh[...], cl_ref[...], preferred_element_type=F32)
        )
        tx_ref[j] = across[tall : tall + 8]

        def out(r, part):
            sv[cx, cz, r : r + 128, :] = part

        row_pass(across[:tall], out)

    owner = owner_ref[...].astype(F32)
    both = owner + owner.T
    eye = iota((NEXP, NEXP), 0) == iota((NEXP, NEXP), 1)
    degree = jnp.sum(both, axis=1, keepdims=True) + LAMBDA_REG
    inverse = invert(jnp.where(eye, degree, 0.0) - both)
    lane, row = iota((NEXP, 128), 1), iota((NEXP, 128), 0)
    first = lax.rem(lane, NEXP)
    shift = lane // NEXP + 1
    second = lax.rem(first + shift, NEXP)
    at_first, at_second = row == first, row == second
    partner = jnp.dot(both, jnp.where(at_second, 1.0, 0.0), precision=HIGH, preferred_element_type=F32)
    used = jnp.sum(jnp.where(at_first, partner, 0.0), axis=0, keepdims=True)
    used = jnp.where((shift[:1] == 8) & (first[:1] >= 8), 0.0, used)
    sign = jnp.where(at_first, 1.0, 0.0) - jnp.where(at_second, 1.0, 0.0)

    each(smooth, 0, 2)
    for copy in bin_copies:
        copy.wait_recv()
    own = moments(bins, me, band)
    mom[0] = own
    sky_mom[band] = own
    sky_copies = []
    for k in range(1, SKY):
        copy = pltpu.make_async_remote_copy(
            src_ref=mom.at[0], dst_ref=sky_mom.at[band], send_sem=sky_s.at[k], recv_sem=sky_r.at[k],
            device_id=(me, lax.rem(band + k, SKY)), device_id_type=MESH,
        )
        copy.start()
        sky_copies.append(copy)
    ty_row = band * ROWS - HALO + iota((tall, 128), 0)
    y = center(ty_row, ROWS * SKY)
    known = (ty_row >= 0) & (ty_row < ROWS * SKY)
    for u in range(3):

        def out(r, part, u=u):
            ty_ref[u, r : r + 128, :] = part

        row_pass(jnp.where(known, cheb(u, y), 0.0), out)
    each(smooth, 2, 4)
    for copy in sky_copies:
        copy.wait_recv()
    total = sky_mom[0]
    for k in range(1, SKY):
        total = total + sky_mom[k]
    def exchange(n, total, at, device):
        mom[1 + n] = total
        axis_mom[n, at] = total
        copies = []
        for k in range(1, 4):
            copy = pltpu.make_async_remote_copy(
                src_ref=mom.at[1 + n], dst_ref=axis_mom.at[n, at], send_sem=axis_s.at[n, k], recv_sem=axis_r.at[n, k],
                device_id=(device(k), band), device_id_type=MESH,
            )
            copy.start()
            copies.append(copy)
        return copies

    def gathered(n, copies):
        for copy in copies:
            copy.wait_recv()
        return (axis_mom[n, 0] + axis_mom[n, 1]) + (axis_mom[n, 2] + axis_mom[n, 3])

    x_copies = exchange(0, total, x, lambda k: 4 * lax.rem(x + k, 4) + z)
    den[0].start3()
    den[1].start3(0, 2)
    each(smooth, 4, 5)
    z_copies = exchange(1, gathered(0, x_copies), z, lambda k: 4 * x + lax.rem(z + k, 4))
    den[1].start3(2, 4)
    each(smooth, 5, 11)
    total = gathered(1, z_copies)
    fits = jnp.concatenate(solve_lanes(total) + [jnp.zeros((7, 128), F32)], 0)
    fits = jnp.where(used > 0.0, fits, 0.0)
    nt = (((1,), (1,)), ((), ()))
    right = lax.dot_general(sign, fits, nt, precision=HIGH, preferred_element_type=F32)
    answer = jnp.dot(inverse, right, precision=HIGH, preferred_element_type=F32)
    offsets_ref[...] = answer[:, :9]
    offs[:, 0:NEXP] = answer
    coef = offs[pl.ds(me, 1), :]
    for k in range(9):
        coefs[k : k + 1, :] = jnp.broadcast_to(coef[:, k : k + 1], (1, 256))

    def numerator(half, dist):
        g = lax.rem((x, z)[half] + dist, 4)

        def chunk(b, carry):
            cx, cz = (g, b) if half == 0 else (b, g)
            tx = tx_ref[4 * cx + cz]
            lines = []
            for u in range(3):
                line = coefs[3 * u : 3 * u + 1, :] * tx[0:1]
                for v in range(1, 3):
                    line = line + coefs[3 * u + v : 3 * u + v + 1, :] * tx[v : v + 1]
                lines.append(line)
            step = NUM_ROWS[half] // 4
            for i in range(4):
                rows = slice(NUM_ROWS[0] * half + step * i, NUM_ROWS[0] * half + step * i + step)
                back = None
                for u in range(3):
                    ty = ty_ref[u, rows, :]
                    term = jnp.concatenate([ty, ty], 1) * lines[u]
                    back = term if back is None else back + term
                sv[cx, cz, rows, :] = wv[cx, cz, rows, :] * (sv[cx, cz, rows, :] - back)
            return carry

        lax.fori_loop(0, 4, chunk, 0)

    for half in range(2):
        numerator(half, 2)
        num[half].start1()
    for part in num[2:]:
        part.start1()
    each(smooth, 11, 16)
    for half in range(2):
        numerator(half, 1)
        numerator(half, 3)
        num[half].start2()
    for part in num[2:]:
        part.start2()
    for part in den:
        part.finish1()
    for part in num[:2]:
        part.start3()
    for half in range(2):
        numerator(half, 0)
    for part in den:
        part.start6()
    for part in num[2:]:
        part.start3()
    for part in num[:2]:
        part.finish1()
    for part in num[2:]:
        part.finish1()
    for part in num[:2]:
        part.start6()
    for part in num[2:]:
        part.start6()
    for h in range(2):
        total_den[DEN_ROWS[0] * h : DEN_ROWS[0] * h + DEN_ROWS[h], :] = PRIOR + den[h].finish2()
    for part in num:
        rows = slice(part.row0, part.row0 + 2 * part.half)
        coadd_ref[rows, :] = part.finish2() / total_den[rows, :]
    for copy in halos + bin_copies + sky_copies + x_copies + z_copies:
        copy.wait_send()
    for part in den + num:
        part.drain()


def per_device(image, variance, mask, foot_start, pair_owner):
    k, n = np.arange(512)[:, None], np.arange(256)[None, :]
    ch, cl = taps_matrix(k - n - 128)
    k, n = np.arange(160)[None, :], np.arange(128)[:, None]
    rh, rl = taps_matrix(k - n - HALO)
    big = lambda *shape: pltpu.VMEM(shape, F32)
    half = lambda *shape: pltpu.VMEM(shape, BF16)
    piece = lambda r: [big(4, r // 2, 256), big(4, r // 2, 256), big(4, r, 256), big(4, r, 256),
                       big(r // 2, 256), big(r // 2, 256), big(r, 256), big(r, 256)]
    pieces = lambda a, b: piece(a) + piece(b) + [big(4, b // 2, 256), big(4, b // 2, 256)]
    dma = lambda n: pltpu.SemaphoreType.DMA((n,))
    vmem = pl.BlockSpec(memory_space=pltpu.VMEM)
    tall = ROWS + 2 * HALO
    held = [
        big(16, ROWS, 256), big(4, 4, ROWS, 256), big(4, 4, ROWS, 256),
        pltpu.VMEM((BROWS, BCOLS), jnp.int32), pltpu.SMEM((NEXP,), jnp.int32), pltpu.VMEM((NEXP, NEXP), jnp.int32),
        half(512, 256), half(512, 256), half(128, 160), half(128, 160), big(HALO, COLS), big(HALO, COLS),
        half(tall + 16, 512), half(tall + 16, 512), big(16, 8, 256), big(3, ROWS, 128), half(BROWS, BCOLS),
        big(16, BROWS, 256), big(64, BCOLS), big(NEXP, 8, 128),
    ]
    fit = [big(NEXP, 8, 128), big(3, 40, 128), big(SKY, 40, 128), big(2, 4, 40, 128), big(NEXP, 128), big(16, 256),
           big(ROWS, 256)]
    sems = [dma(7), dma(16), dma(16), dma(2), dma(2), dma(104), dma(104), dma(NEXP), dma(NEXP), dma(SKY), dma(SKY),
            pltpu.SemaphoreType.DMA((2, 4)), pltpu.SemaphoreType.DMA((2, 4))]
    return tuple(pl.pallas_call(
        coadd_kernel,
        in_specs=[pl.BlockSpec(memory_space=pltpu.HBM)] * 9,
        out_specs=[vmem, vmem],
        out_shape=[jax.ShapeDtypeStruct((ROWS, 256), F32), jax.ShapeDtypeStruct((NEXP, 9), F32)],
        scratch_shapes=held + fit + pieces(*DEN_ROWS) + pieces(*NUM_PIECES[0]) + pieces(*NUM_PIECES[1]) + sems,
        compiler_params=pltpu.CompilerParams(collective_id=0, has_side_effects=True, vmem_limit_bytes=52 << 20),
        name="coadd",
    )(*(pltpu.with_memory_space_constraint(a, pltpu.HBM)
        for a in (image, variance, mask, foot_start, pair_owner, ch, cl, rh, rl))))


def solution(mesh):
    placed = (P("exp", "sky", None), P("exp", "sky", None), P("exp", "sky", None), P(), P())
    return jax.shard_map(
        per_device, mesh=mesh, in_specs=placed, out_specs=(P("sky", "exp"), P()), check_vma=False
    )
```

```python
import functools

import jax
import jax.numpy as jnp
import numpy as np
from jax import lax
from jax.experimental import pallas as pl
from jax.experimental.pallas import tpu as pltpu
from jax.sharding import PartitionSpec as P

F32 = jnp.float32
BF16 = jnp.bfloat16
HIGH = lax.Precision.HIGHEST
MESH = pl.DeviceIdType.MESH
BIN = 16
RADIUS = 10
NEXP = 16
ROWS = 512
COLS = 4096
SKY = 8
BROWS = 32
BCOLS = 256
FOOT_BINS = 192
HALO = 16
LAMBDA_REG = 0.25
DEN_ROWS = (224, 288)
NUM_ROWS = (224, 288)
NUM_PIECES = ((160, 208), (64, 80))
PRIOR = 1.0


def iota(shape, dim):
    return lax.broadcasted_iota(jnp.int32, shape, dim)


def center(index, total):
    return (2.0 * index.astype(F32) + 1.0) / total - 1.0


def cheb(order, t):
    if order == 0:
        return jnp.ones_like(t)
    if order == 1:
        return t
    return 2.0 * t * t - 1.0


def split(value):
    high = value.astype(BF16)
    return high, (value - high.astype(F32)).astype(BF16)


def taps_matrix(offset):
    total = np.sum(np.exp(-(np.arange(-RADIUS, RADIUS + 1) ** 2) / 50.0))
    exact = np.where(np.abs(offset) <= RADIUS, np.exp(-(offset**2) / 50.0) / total, 0.0)
    high = exact.astype(BF16)
    return jnp.asarray(high), jnp.asarray((exact - high.astype(np.float64)).astype(BF16))


class Scatter:
    def __init__(self, part, lead, row0, rows, place, foot, bufs, sems, packed):
        self.part, self.lead, self.row0, self.half = part, lead, row0, rows // 2
        self.me, self.sky, self.foot = place[0], place[1], foot
        (self.f1p, self.f1m, self.rp, self.rm, self.f2p, self.f2m, self.r2p, self.r2m), rest = bufs[:8], bufs[8:]
        self.packs, self.lands = rest or (None, None)
        self.send_sems, self.recv_sems, self.counter = sems
        self.packed = packed
        self.copies = {}
        self.first = {"p": [], "m": []}
        self.second = []
        self.third = []

    def device(self, axis, shift):
        x, z = self.me
        if axis == 0:
            x = lax.rem(x + shift + 4, 4)
        else:
            z = lax.rem(z + shift + 4, 4)
        return (4 * x + z, self.sky)

    def to(self, dist):
        return lax.rem(self.me[self.lead] + dist, 4)

    def group(self, dist, r, chunks=(0, 4)):
        rows = pl.ds(self.row0 + r, self.half)
        some = pl.ds(*chunks)
        g = self.to(dist)
        return self.part.at[g, some, rows, :] if self.lead == 0 else self.part.at[some, g, rows, :]

    def own(self, b, dist, r):
        rows = pl.ds(self.row0 + r, self.half)
        g = self.to(dist)
        return self.part[g, b, rows, :] if self.lead == 0 else self.part[b, g, rows, :]

    def remote(self, src, dst, axis, shift):
        n = self.counter[0]
        self.counter[0] += 1
        return pltpu.make_async_remote_copy(
            src_ref=src, dst_ref=dst, send_sem=self.send_sems.at[n], recv_sem=self.recv_sems.at[n],
            device_id=self.device(axis, shift), device_id_type=MESH,
        )

    def keep(self, key, copies, copy):
        self.copies[key] = copy
        copies.append(copy)

    def send(self, key, src, dst, axis, shift):
        copy = self.remote(src, dst, axis, shift)
        copy.start()
        self.copies[key] = copy
        return copy

    def send_group(self, key, packed, slot, dist, r, land, to):
        if not packed:
            return [self.send(key, self.group(dist, r), land, self.lead, to)]
        raw = self.send(key, self.group(dist, r, (1, 2)), land.at[pl.ds(1, 2)], self.lead, to)
        self.packs[slot] = self.own(0, dist, r) + self.own(3, dist, r)
        return [raw, self.send(key + "s", self.packs.at[slot], self.lands.at[slot], self.lead, to)]

    def apart(self, slot, b):
        sender = self.foot[self.device(1, -1 if slot in (0, 2) else 1)[0]]
        g = self.to({0: 1, 1: 3, 2: 0, 3: 0}[slot])
        low = 256 * g + iota((1, 256), 1) >= BIN * sender
        return jnp.where(low if b == 0 else jnp.logical_not(low), self.lands[slot], 0.0)

    def start1(self):
        h = self.half
        self.first["p"] += self.send_group("1p", self.packed[0], 0, 2, 0, self.f1p, 1)
        self.first["m"] += self.send_group("1m", self.packed[0], 1, 2, h, self.f1m, -1)

    def start1_chunk(self, dist):
        b = lax.rem(self.me[1 - self.lead] + dist, 4)
        for key, r, buf, to in (("p", 0, self.f1p, 1), ("m", self.half, self.f1m, -1)):
            if not self.packed[0]:
                copy = self.remote(self.group(2, r).at[b], buf.at[b], self.lead, to)
                copy.start()
                self.keep("1" + key + str(dist), self.first[key], copy)
                continue
            for c in (1, 2):
                name = "1" + key + str(c)
                if name not in self.copies:
                    self.keep(name, self.first[key], self.remote(self.group(2, r).at[c], buf.at[c], self.lead, to))

                @pl.when(b == c)
                def _(name=name):
                    self.copies[name].start()

    def start1_sum(self):
        for key, slot, r, to in (("p", 0, 0, 1), ("m", 1, self.half, -1)):
            self.packs[slot] = self.own(0, 2, r) + self.own(3, 2, r)
            copy = self.remote(self.packs.at[slot], self.lands.at[slot], self.lead, to)
            copy.start()
            self.keep("1s" + key, self.first[key], copy)

    def start2(self):
        h = self.half
        self.second += self.send_group("2p", self.packed[1], 2, 1, h, self.rp.at[:, pl.ds(h, h), :], 1)
        self.second += self.send_group("2m", self.packed[1], 3, 3, 0, self.rm.at[:, pl.ds(0, h), :], -1)

    def start3(self, lo=0, hi=4):
        h = self.half
        for key, buf, dist, shift, land, slot, to in (
            ("p", self.f1p, 1, 0, self.rp, 0, 1), ("m", self.f1m, 3, h, self.rm, 1, -1)
        ):
            if lo == 0:
                for copy in self.first[key]:
                    copy.wait_recv()

            def body(b, carry, buf=buf, dist=dist, shift=shift):
                buf[b] = buf[b] + self.own(b, dist, shift)
                return carry

            if self.packed[0]:
                for b in (0, 3):
                    if lo <= b < hi:
                        buf[b] = self.apart(slot, b) + self.own(b, dist, shift)
                lax.fori_loop(max(lo, 1), min(hi, 3), body, 0)
            else:
                lax.fori_loop(lo, hi, body, 0)
            some = pl.ds(lo, hi - lo)
            self.third.append(
                self.send("3" + key + str(lo), buf.at[some], land.at[some, pl.ds(shift, h), :], self.lead, to)
            )

    def finish1(self):
        h = self.half
        top, low = pl.ds(0, h), pl.ds(h, h)
        for copy in self.second + self.third:
            copy.wait_recv()

        def body(b, carry):
            for shift in (0, h):
                rows = pl.ds(shift, h)
                self.rp[b, rows, :] = self.rp[b, rows, :] + self.rm[b, rows, :] + self.own(b, 0, shift)
            return carry

        if self.packed[1]:
            for b in (0, 3):
                self.rp[b, top, :] = self.rp[b, top, :] + self.apart(3, b) + self.own(b, 0, 0)
                self.rp[b, low, :] = self.apart(2, b) + self.rm[b, low, :] + self.own(b, 0, h)
            lax.fori_loop(1, 3, body, 0)
        else:
            lax.fori_loop(0, 4, body, 0)
        axis = 1 - self.lead
        at = lambda dist: lax.rem(self.me[axis] + dist, 4)
        self.send("4p", self.rp.at[at(2), top, :], self.f2p, axis, 1)
        self.send("4m", self.rp.at[at(2), low, :], self.f2m, axis, -1)
        self.send("5p", self.rp.at[at(1), low, :], self.r2p.at[low, :], axis, 1)
        self.send("5m", self.rp.at[at(3), top, :], self.r2m.at[top, :], axis, -1)

    def start6(self):
        axis = 1 - self.lead
        for key, buf, dist, shift, land, to in (
            ("p", self.f2p, 1, 0, self.r2p, 1), ("m", self.f2m, 3, self.half, self.r2m, -1)
        ):
            self.copies["4" + key].wait_recv()
            g = lax.rem(self.me[axis] + dist, 4)
            rows = pl.ds(shift, self.half)
            buf[...] = buf[...] + self.rp[g, rows, :]
            self.send("6" + key, buf, land.at[rows, :], axis, to)

    def finish2(self):
        for key in ("5p", "5m", "6p", "6m"):
            self.copies[key].wait_recv()
        g = self.me[1 - self.lead]
        return self.rp[g] + self.r2p[...] + self.r2m[...]

    def drain(self):
        for copy in self.copies.values():
            copy.wait_send()


def invert(system):
    lane, row = iota((NEXP, 128), 1), iota((NEXP, 128), 0)
    work = jnp.concatenate([system, jnp.zeros((NEXP, 112), F32)], 1)
    work = work + jnp.where(lane == row + NEXP, 1.0, 0.0)
    for j in range(NEXP):
        pivot_row = work[j : j + 1, :] / work[j : j + 1, j : j + 1]
        factor = work[:, j : j + 1]
        work = jnp.where(row == j, pivot_row, work - factor * pivot_row)
    return work[:, NEXP : 2 * NEXP]


def moments(bins, me, band):
    image = jnp.concatenate([bins[:, 0, :], bins[:, 4, :], bins[:, 1, :], bins[:, 5, :]], 1)
    weight = jnp.concatenate([bins[:, 2, :], bins[:, 6, :], bins[:, 3, :], bins[:, 7, :]], 1)
    ws, ds = [], []
    for d in range(1, 9):
        other = pltpu.roll(weight, NEXP - d, 0)
        w = weight * other / (weight + other + 1.0)
        ws.append(w)
        ds.append(w * (image - pltpu.roll(image, NEXP - d, 0)))
    w, wd = jnp.concatenate(ws, 0), jnp.concatenate(ds, 0)

    def basis(rows, base):
        k, lane = iota((rows, 512), 0), iota((rows, 512), 1)
        y = center(BROWS * band + 2 * me + lane // 256, BCOLS)
        x = center(lane % 256, BCOLS)

        def pick(order, t):
            t2 = 2.0 * t * t - 1.0
            out = jnp.where(order == 0, 1.0, jnp.where(order == 1, t, t2))
            if base == 5:
                out = jnp.where(order == 3, 2.0 * t * t2 - t, out)
                out = jnp.where(order == 4, 2.0 * t2 * t2 - 1.0, out)
            return out

        return jnp.where(k < base * base, pick(k // base, y) * pick(k % base, x), 0.0)

    nt = (((1,), (1,)), ((), ()))
    gram = lax.dot_general(basis(32, 5), w, nt, precision=HIGH, preferred_element_type=F32)
    rhs = lax.dot_general(basis(16, 3), wd, nt, precision=HIGH, preferred_element_type=F32)
    return jnp.concatenate([gram[:25], rhs[:9], jnp.zeros((6, 128), F32)], 0)


def solve_lanes(mom):
    m = lambda a, b: mom[5 * a + b : 5 * a + b + 1, :]
    cache = {}

    def entry(k, l):
        u, v, s, t = k // 3, k % 3, l // 3, l % 3
        key = tuple(sorted(((u + s, v + t), (abs(u - s), v + t), (u + s, abs(v - t)), (abs(u - s), abs(v - t)))))
        if key not in cache:
            cache[key] = 0.25 * ((m(*key[0]) + m(*key[1])) + (m(*key[2]) + m(*key[3])))
        return cache[key]

    a = [[entry(k, l) for l in range(k + 1)] for k in range(9)]
    b = [mom[25 + k : 26 + k, :] for k in range(9)]
    inv = [None] * 9
    for j in range(9):
        inv[j] = 1.0 / a[j][j]
        for k in range(j + 1, 9):
            f = a[k][j] * inv[j]
            for l in range(j + 1, k + 1):
                a[k][l] = a[k][l] - f * a[l][j]
            b[k] = b[k] - f * b[j]
    out = [None] * 9
    for j in reversed(range(9)):
        total = b[j]
        for k in range(j + 1, 9):
            total = total - a[k][j] * out[k]
        out[j] = total * inv[j]
    return out


def early(n):
    t = (n - 1) // 2
    other = t + t // 2 - 2
    odd = lax.rem(n - 1, 2)
    return 2 + odd * other, 2 + (1 - odd) * other


def late(n):
    return lax.rem((n - 7) // 3 + 3, 4), lax.rem(lax.rem(n - 7, 3) + 3, 4)


NUM_SCRATCH = 20


def coadd_kernel(image_hbm, variance_hbm, mask_hbm, foot_hbm, owner_hbm, ch_hbm, cl_hbm, rh_hbm, rl_hbm,
                 coadd_ref, offsets_ref, *scratch):
    (img, wv, sv, mask_ref, foot_ref, owner_ref, ch_ref, cl_ref, rh_ref, rl_ref, up_ref, down_ref, xh, xl, tx_ref,
     ty_ref, blocks, sums, binned, bins_own), scratch = scratch[:NUM_SCRATCH], scratch[NUM_SCRATCH:]
    (bins, mom, sky_mom, axis_mom, offs, coefs, total_den), scratch = scratch[:7], scratch[7:]
    bufs, scratch = scratch[:54], scratch[54:]
    (small_sems, var_sems, img_sems, halo_s, halo_r, send_sems, recv_sems,
     bin_s, bin_r, sky_s, sky_r, axis_s, axis_r) = scratch
    me, band = lax.axis_index("exp"), lax.axis_index("sky")
    x, z = me // 4, lax.rem(me, 4)
    tall = ROWS + 2 * HALO

    barrier = pltpu.get_barrier_semaphore()
    for k in range(1, NEXP):
        pl.semaphore_signal(barrier, inc=1, device_id=(lax.rem(me + k, NEXP), band), device_id_type=MESH)
    for k in range(1, SKY):
        pl.semaphore_signal(barrier, inc=1, device_id=(me, lax.rem(band + k, SKY)), device_id_type=MESH)

    def place(rel):
        return lax.rem(x + rel[0], 4), lax.rem(z + rel[1], 4)

    def load_var(n, rel):
        cx, cz = place(rel)
        cols = pl.ds(pl.multiple_of(256 * (4 * cx + cz), 256), 256)
        return pltpu.make_async_copy(variance_hbm.at[0, :, cols], wv.at[cx, cz], var_sems.at[n])

    def load_img(n, rel):
        cx, cz = place(rel)
        cols = pl.ds(pl.multiple_of(256 * (4 * cx + cz), 256), 256)
        return pltpu.make_async_copy(image_hbm.at[0, :, cols], img.at[4 * cx + cz], img_sems.at[n])

    def each(fn, lo=0, hi=16):
        if lo == 0:
            fn(0, (2, 2))
        for first, last, rel in ((1, 7, early), (7, 16, late)):
            first, last = max(lo, first), min(hi, last)
            if first < last:

                def body(n, carry, rel=rel):
                    fn(n, rel(n))
                    return carry

                lax.fori_loop(first, last, body, 0)

    small = [
        pltpu.make_async_copy(src, dst, small_sems.at[n])
        for n, (src, dst) in enumerate((
            (mask_hbm.at[0], mask_ref), (foot_hbm, foot_ref), (owner_hbm, owner_ref),
            (ch_hbm, ch_ref), (cl_hbm, cl_ref), (rh_hbm, rh_ref), (rl_hbm, rl_ref),
        ))
    ]
    for copy in small[:2]:
        copy.start()
    each(lambda n, rel: load_var(n, rel).start(), 0, 7)

    for copy in small[:2]:
        copy.wait()
    start = foot_ref[me]
    cell = iota((BROWS, BCOLS), 1)
    inside = (cell >= start) & (cell < start + FOOT_BINS)
    blocks[...] = jnp.where(inside, mask_ref[...].astype(F32), 0.0).astype(BF16)

    def onehot(m):
        hit = iota((256, 256), 0) == 16 * m + iota((256, 256), 1) // BIN
        return jnp.where(hit, 1.0, 0.0).astype(BF16)

    def weights(n, rel):
        load_var(n, rel).wait()
        cx, cz = place(rel)
        wide = jnp.dot(blocks[...], onehot(4 * cx + cz), preferred_element_type=F32)
        for r in range(4):
            rows = slice(128 * r, 128 * r + 128)
            keep = jnp.broadcast_to(wide[8 * r : 8 * r + 8][:, None, :], (8, BIN, 256)).reshape(128, 256)
            w = keep * (1.0 / wv[cx, cz, rows, :])
            wv[cx, cz, rows, :] = w
            sums[4 * cx + cz, 8 * r : 8 * r + 8, :] = jnp.sum(w.reshape(8, BIN, 256), axis=1)

    where = ((x, z), band)
    take = lambda n: bufs[18 * (n // 2) : 18 * (n // 2) + 8] if n % 2 == 0 else bufs[18 * (n // 2) + 8 : 18 * (n // 2) + 18]
    sems = (send_sems, recv_sems, [0])
    den = [Scatter(wv, h, DEN_ROWS[0] * h, DEN_ROWS[h], where, foot_ref, take(h), sems, (h == 1, h == 1)) for h in range(2)]
    num = [
        Scatter(sv, h, NUM_ROWS[0] * h + NUM_PIECES[0][h] * q, NUM_PIECES[q][h], where, foot_ref, take(2 + 2 * q + h),
                sems, (h == 1, h == 1))
        for q in range(2) for h in range(2)
    ]

    weights(0, (2, 2))
    pl.semaphore_wait(barrier, NEXP + SKY - 2)
    for part in den:
        part.start1_chunk(2)
    each(lambda n, rel: load_var(n, rel).start(), 7, 16)
    each(lambda n, rel: load_img(n, rel).start())
    for copy in small[2:]:
        copy.start()
    halos = []
    for n, (rows, dst, to) in enumerate(((ROWS - HALO, up_ref, band + 1), (0, down_ref, band + SKY - 1))):
        copy = pltpu.make_async_remote_copy(
            src_ref=image_hbm.at[0, pl.ds(rows, HALO), :], dst_ref=dst, send_sem=halo_s.at[n], recv_sem=halo_r.at[n],
            device_id=(me, lax.rem(to, SKY)), device_id_type=MESH,
        )
        copy.start()
        halos.append(copy)
    for t in range(3):
        dist = (0, 1, 3)[t]
        weights(1 + 2 * t, (2, dist))
        den[0].start1_chunk(dist)
        weights(2 + 2 * t, (dist, 2))
        den[1].start1_chunk(dist)
    den[1].start1_sum()
    each(weights, 7, 16)

    def image_sums(n, rel):
        load_img(n, rel).wait()
        cx, cz = place(rel)
        m = 4 * cx + cz
        parts = []
        for r in range(4):
            parts.append(jnp.sum(img[m, 128 * r : 128 * r + 128, :].reshape(8, BIN, 256), axis=1))
        both = jnp.concatenate([jnp.concatenate(parts, 0) * (1.0 / (BIN * BIN)), sums[m]], 0)
        high = both.astype(BF16)
        rest = both - high.astype(F32)
        mid = rest.astype(BF16)
        low = (rest - mid.astype(F32)).astype(BF16)
        got = lax.dot_general(
            jnp.concatenate([high, mid, low], 0), onehot(m), (((1,), (1,)), ((), ())), preferred_element_type=F32
        )
        binned[...] = binned[...] + (got[:64] + got[64:128] + got[128:])

    binned[...] = jnp.zeros((64, BCOLS), F32)
    each(image_sums)
    for m in range(NEXP):
        tile = jnp.concatenate([binned[2 * m : 2 * m + 2, :], binned[32 + 2 * m : 34 + 2 * m, :]], 0)
        bins_own[m] = jnp.concatenate([tile[:, :128], tile[:, 128:]], 0)
    bin_copies = []
    for k in range(1, NEXP):
        to = lax.rem(me + k, NEXP)
        copy = pltpu.make_async_remote_copy(
            src_ref=bins_own.at[to], dst_ref=bins.at[me], send_sem=bin_s.at[k], recv_sem=bin_r.at[k],
            device_id=(to, band), device_id_type=MESH,
        )
        copy.start()
        bin_copies.append(copy)
    bins[me] = bins_own[me]
    for part in den:
        part.start2()

    for copy in small[2:]:
        copy.wait()
    for copy in halos:
        copy.wait_recv()

    def put(j, first, lane0, value):
        rows, width = value.shape
        col = 256 * j - 128 + lane0 + iota((1, width), 1)
        keep = (col >= BIN * start) & (col < BIN * (start + FOOT_BINS))
        high, low = split(jnp.where(keep, value, 0.0))
        xh[first : first + rows, lane0 : lane0 + width] = high
        xl[first : first + rows, lane0 : lane0 + width] = low

    def row_pass(value, out):
        high, low = split(value)
        for i in range(ROWS // 128):
            zh, zl = high[128 * i : 128 * i + 160], low[128 * i : 128 * i + 160]
            out(
                128 * i,
                jnp.dot(rh_ref[...], zh, preferred_element_type=F32)
                + jnp.dot(rl_ref[...], zh, preferred_element_type=F32)
                + jnp.dot(rh_ref[...], zl, preferred_element_type=F32),
            )

    def smooth(n, rel):
        cx, cz = place(rel)
        j = 4 * cx + cz
        before, after = jnp.maximum(j - 1, 0), jnp.minimum(j + 1, 15)
        lo = pl.multiple_of(jnp.maximum(256 * j - 128, 0), 128)
        mid = pl.multiple_of(256 * j, 128)
        hi = pl.multiple_of(jnp.minimum(256 * j + 256, COLS - 128), 128)
        for first, ref, known in ((0, up_ref, band > 0), (HALO + ROWS, down_ref, band < SKY - 1)):
            put(j, first, 0, jnp.where(known, ref[:, pl.ds(lo, 128)], 0.0))
            put(j, first, 128, jnp.where(known, ref[:, pl.ds(mid, 256)], 0.0))
            put(j, first, 384, jnp.where(known, ref[:, pl.ds(hi, 128)], 0.0))
        put(j, HALO, 0, img[before, :, 128:256])
        put(j, HALO, 128, img[j])
        put(j, HALO, 384, img[after, :, 0:128])
        xcol = center(256 * j - 128 + iota((16, 512), 1), COLS)
        order = iota((16, 512), 0)
        put(j, tall, 0, jnp.where(order == 0, 1.0, jnp.where(order == 1, xcol, 2.0 * xcol * xcol - 1.0)))
        across = (
            jnp.dot(xh[...], ch_ref[...], preferred_element_type=F32)
            + jnp.dot(xl[...], ch_ref[...], preferred_element_type=F32)
            + jnp.dot(xh[...], cl_ref[...], preferred_element_type=F32)
        )
        tx_ref[j] = across[tall : tall + 8]

        def out(r, part):
            sv[cx, cz, r : r + 128, :] = part

        row_pass(across[:tall], out)

    owner = owner_ref[...].astype(F32)
    both = owner + owner.T
    eye = iota((NEXP, NEXP), 0) == iota((NEXP, NEXP), 1)
    degree = jnp.sum(both, axis=1, keepdims=True) + LAMBDA_REG
    inverse = invert(jnp.where(eye, degree, 0.0) - both)
    lane, row = iota((NEXP, 128), 1), iota((NEXP, 128), 0)
    first = lax.rem(lane, NEXP)
    shift = lane // NEXP + 1
    second = lax.rem(first + shift, NEXP)
    at_first, at_second = row == first, row == second
    partner = jnp.dot(both, jnp.where(at_second, 1.0, 0.0), precision=HIGH, preferred_element_type=F32)
    used = jnp.sum(jnp.where(at_first, partner, 0.0), axis=0, keepdims=True)
    used = jnp.where((shift[:1] == 8) & (first[:1] >= 8), 0.0, used)
    sign = jnp.where(at_first, 1.0, 0.0) - jnp.where(at_second, 1.0, 0.0)

    each(smooth, 0, 2)
    for copy in bin_copies:
        copy.wait_recv()
    own = moments(bins, me, band)
    mom[0] = own
    sky_mom[band] = own
    sky_copies = []
    for k in range(1, SKY):
        copy = pltpu.make_async_remote_copy(
            src_ref=mom.at[0], dst_ref=sky_mom.at[band], send_sem=sky_s.at[k], recv_sem=sky_r.at[k],
            device_id=(me, lax.rem(band + k, SKY)), device_id_type=MESH,
        )
        copy.start()
        sky_copies.append(copy)
    ty_row = band * ROWS - HALO + iota((tall, 128), 0)
    y = center(ty_row, ROWS * SKY)
    known = (ty_row >= 0) & (ty_row < ROWS * SKY)
    for u in range(3):

        def out(r, part, u=u):
            ty_ref[u, r : r + 128, :] = part

        row_pass(jnp.where(known, cheb(u, y), 0.0), out)
    each(smooth, 2, 4)
    for copy in sky_copies:
        copy.wait_recv()
    total = sky_mom[0]
    for k in range(1, SKY):
        total = total + sky_mom[k]
    def exchange(n, total, at, device):
        mom[1 + n] = total
        axis_mom[n, at] = total
        copies = []
        for k in range(1, 4):
            copy = pltpu.make_async_remote_copy(
                src_ref=mom.at[1 + n], dst_ref=axis_mom.at[n, at], send_sem=axis_s.at[n, k], recv_sem=axis_r.at[n, k],
                device_id=(device(k), band), device_id_type=MESH,
            )
            copy.start()
            copies.append(copy)
        return copies

    def gathered(n, copies):
        for copy in copies:
            copy.wait_recv()
        return (axis_mom[n, 0] + axis_mom[n, 1]) + (axis_mom[n, 2] + axis_mom[n, 3])

    x_copies = exchange(0, total, x, lambda k: 4 * lax.rem(x + k, 4) + z)
    den[0].start3()
    den[1].start3(0, 2)
    each(smooth, 4, 5)
    z_copies = exchange(1, gathered(0, x_copies), z, lambda k: 4 * x + lax.rem(z + k, 4))
    den[1].start3(2, 4)
    each(smooth, 5, 8)
    total = gathered(1, z_copies)
    fits = jnp.concatenate(solve_lanes(total) + [jnp.zeros((7, 128), F32)], 0)
    fits = jnp.where(used > 0.0, fits, 0.0)
    nt = (((1,), (1,)), ((), ()))
    right = lax.dot_general(sign, fits, nt, precision=HIGH, preferred_element_type=F32)
    answer = jnp.dot(inverse, right, precision=HIGH, preferred_element_type=F32)
    offsets_ref[...] = answer[:, :9]
    offs[:, 0:NEXP] = answer
    coef = offs[pl.ds(me, 1), :]
    for k in range(9):
        coefs[k : k + 1, :] = jnp.broadcast_to(coef[:, k : k + 1], (1, 256))

    def numerator(half, dist):
        g = lax.rem((x, z)[half] + dist, 4)

        def chunk(b, carry):
            cx, cz = (g, b) if half == 0 else (b, g)
            tx = tx_ref[4 * cx + cz]
            lines = []
            for u in range(3):
                line = coefs[3 * u : 3 * u + 1, :] * tx[0:1]
                for v in range(1, 3):
                    line = line + coefs[3 * u + v : 3 * u + v + 1, :] * tx[v : v + 1]
                lines.append(line)
            step = NUM_ROWS[half] // 4
            for i in range(4):
                rows = slice(NUM_ROWS[0] * half + step * i, NUM_ROWS[0] * half + step * i + step)
                back = None
                for u in range(3):
                    ty = ty_ref[u, rows, :]
                    term = jnp.concatenate([ty, ty], 1) * lines[u]
                    back = term if back is None else back + term
                sv[cx, cz, rows, :] = wv[cx, cz, rows, :] * (sv[cx, cz, rows, :] - back)
            return carry

        lax.fori_loop(0, 4, chunk, 0)

    for half in range(2):
        numerator(half, 2)
        num[half].start1()
    for part in num[2:]:
        part.start1()
    each(smooth, 8, 16)
    for half in range(2):
        numerator(half, 1)
        numerator(half, 3)
        num[half].start2()
    for part in num[2:]:
        part.start2()
    for part in den:
        part.finish1()
    for part in num[:2]:
        part.start3()
    for half in range(2):
        numerator(half, 0)
    for part in den:
        part.start6()
    for part in num[2:]:
        part.start3()
    for part in num[:2]:
        part.finish1()
    for part in num[2:]:
        part.finish1()
    for part in num[:2]:
        part.start6()
    for part in num[2:]:
        part.start6()
    for h in range(2):
        total_den[DEN_ROWS[0] * h : DEN_ROWS[0] * h + DEN_ROWS[h], :] = PRIOR + den[h].finish2()
    for part in num:
        rows = slice(part.row0, part.row0 + 2 * part.half)
        coadd_ref[rows, :] = part.finish2() / total_den[rows, :]
    for copy in halos + bin_copies + sky_copies + x_copies + z_copies:
        copy.wait_send()
    for part in den + num:
        part.drain()


def per_device(image, variance, mask, foot_start, pair_owner):
    k, n = np.arange(512)[:, None], np.arange(256)[None, :]
    ch, cl = taps_matrix(k - n - 128)
    k, n = np.arange(160)[None, :], np.arange(128)[:, None]
    rh, rl = taps_matrix(k - n - HALO)
    big = lambda *shape: pltpu.VMEM(shape, F32)
    half = lambda *shape: pltpu.VMEM(shape, BF16)
    piece = lambda r: [big(4, r // 2, 256), big(4, r // 2, 256), big(4, r, 256), big(4, r, 256),
                       big(r // 2, 256), big(r // 2, 256), big(r, 256), big(r, 256)]
    pieces = lambda a, b: piece(a) + piece(b) + [big(4, b // 2, 256), big(4, b // 2, 256)]
    dma = lambda n: pltpu.SemaphoreType.DMA((n,))
    vmem = pl.BlockSpec(memory_space=pltpu.VMEM)
    tall = ROWS + 2 * HALO
    held = [
        big(16, ROWS, 256), big(4, 4, ROWS, 256), big(4, 4, ROWS, 256),
        pltpu.VMEM((BROWS, BCOLS), jnp.int32), pltpu.SMEM((NEXP,), jnp.int32), pltpu.VMEM((NEXP, NEXP), jnp.int32),
        half(512, 256), half(512, 256), half(128, 160), half(128, 160), big(HALO, COLS), big(HALO, COLS),
        half(tall + 16, 512), half(tall + 16, 512), big(16, 8, 256), big(3, ROWS, 128), half(BROWS, BCOLS),
        big(16, BROWS, 256), big(64, BCOLS), big(NEXP, 8, 128),
    ]
    fit = [big(NEXP, 8, 128), big(3, 40, 128), big(SKY, 40, 128), big(2, 4, 40, 128), big(NEXP, 128), big(16, 256),
           big(ROWS, 256)]
    sems = [dma(7), dma(16), dma(16), dma(2), dma(2), dma(104), dma(104), dma(NEXP), dma(NEXP), dma(SKY), dma(SKY),
            pltpu.SemaphoreType.DMA((2, 4)), pltpu.SemaphoreType.DMA((2, 4))]
    return tuple(pl.pallas_call(
        coadd_kernel,
        in_specs=[pl.BlockSpec(memory_space=pltpu.HBM)] * 9,
        out_specs=[vmem, vmem],
        out_shape=[jax.ShapeDtypeStruct((ROWS, 256), F32), jax.ShapeDtypeStruct((NEXP, 9), F32)],
        scratch_shapes=held + fit + pieces(*DEN_ROWS) + pieces(*NUM_PIECES[0]) + pieces(*NUM_PIECES[1]) + sems,
        compiler_params=pltpu.CompilerParams(collective_id=0, has_side_effects=True, vmem_limit_bytes=52 << 20),
        name="coadd",
    )(*(pltpu.with_memory_space_constraint(a, pltpu.HBM)
        for a in (image, variance, mask, foot_start, pair_owner, ch, cl, rh, rl))))


def solution(mesh):
    placed = (P("exp", "sky", None), P("exp", "sky", None), P("exp", "sky", None), P(), P())
    return jax.shard_map(
        per_device, mesh=mesh, in_specs=placed, out_specs=(P("sky", "exp"), P()), check_vma=False
    )
```
